32 devices in a mesh: parts: 2 (over x), gz: 8 (over z, y), view: 2 (over core).
Axes of the slice: x: 2, y: 2, z: 4, core: 2. Of those that a mesh axis runs over, the one named last changes fastest.
Arguments:
- observed: bfloat16 [8, 64, 256, 256], P('view', 'parts', 'gz'), parts along dimension 1, may hold values from 0.19921875 to 2
- initial: float32 [64, 256, 256], P('parts', 'gz'), parts along dimension 0, may hold values from 0.5 to 2
- psf_taps: float32 [8, 3, 15], replicated, may hold values from 0.05 to 1
- view_shifts: int32 [8, 2], replicated, may hold values from -7 to 7
- view_map: int32 [8], replicated, may hold values from 0 to 7, each once
Outputs:
- estimate: float32 [64, 256, 256], P('parts', 'gz'), parts along dimension 0
- surfaces: float32 [8, 64, 256, 256], P('view', 'parts', 'gz'), parts along dimension 1
The draws below stay inside these ranges and needn't reach their ends.
There are 2 independent parts, one for each index of `parts`. The reference program is written for one: setup_inputs(seed, part) draws one part's arguments, and reference() takes and returns one part's arrays. A program takes and returns all parts, laid end to end along the dimension named above; an argument that names none is the same for every part. Nothing has to cross between parts.
Inputs may be any that keep to these rules, and one draw needn't show every extreme that they name: `view_map`: each view number stands in exactly one slot; view 0 is the reference view.
All inputs are finite; a program needn't handle non-finite values.
Results may differ from the reference program's by a relative error of at most 0.0014.
Values may be sent and summed in bfloat16 or wider, within the bound.
No kernel may reach another device: no remote copies, remote signals or barrier semaphores. Data moves between devices by JAX's collectives and lax.ppermute only.
A program may use at most 128 MiB of HBM per device.

```python
import math
import jax
import jax.numpy as jnp
from jax import lax

VIEWS = 8
ZS = 32
BY = 256
BX = 256
ITERS = 2
X = 256


def with_ends(values, key, low, high):
    shape = values.shape
    spot = [jax.random.randint(jax.random.fold_in(key, axis), (), 0, shape[axis]) for axis in range(len(shape))]
    values = values.at[tuple(spot)].set(low)
    longest = shape.index(max(shape))
    spot[longest] = (spot[longest] + 1) % shape[longest]
    return values.at[tuple(spot)].set(high)


def block_levels(own_key, shape, cuts, least, high):
    gain = 1.0
    for axis_at, parts in cuts:
        steps = jax.random.uniform(jax.random.fold_in(jax.random.fold_in(own_key, 6), axis_at), (parts,), jnp.float32, least / len(cuts), high / len(cuts))
        gain = gain * jnp.repeat(jnp.exp(steps), shape[axis_at] // parts).reshape((-1,) + (1,) * (len(shape) - 1 - axis_at))
    return gain


def setup_inputs(seed: int = 0, part: int = 0) -> dict:
    key_list = jax.random.split(jax.random.key(seed), 6)
    part_splits = jax.random.split(jax.random.fold_in(key_list[5], part), 6)
    return {
        "observed": jnp.clip(0.19921875 + 1.8007812 * jax.random.uniform(part_splits[0], (VIEWS, ZS, BY, X), jnp.float32) ** block_levels(part_splits[0], (VIEWS, ZS, BY, X), ((0, 2), (2, 8)), -0.2, 0.2), 0.19921875, 2.0).astype(jnp.bfloat16),
        "initial": jnp.clip(jnp.exp(math.log(2.0) - 1.3862944 * jax.random.uniform(part_splits[1], (ZS, BY, X), jnp.float32) ** block_levels(part_splits[1], (ZS, BY, X), ((1, 8),), -0.2, 0.2)), 0.5, 2.0),
        "psf_taps": jnp.clip(jnp.exp(jax.random.uniform(key_list[2], (VIEWS, 3, 15), jnp.float32, math.log(0.05), math.log(1.0))), 0.05, 1.0),
        "view_shifts": with_ends(jax.random.randint(key_list[3], (VIEWS, 2), -7, 8), jax.random.fold_in(key_list[3], 1), -7, 7).astype(jnp.int32),
        "view_map": jax.random.permutation(key_list[4], VIEWS).astype(jnp.int32),
    }


def blur_axis(volume, filter_taps, offset_cells, along_axis, orient):
    extent = volume.shape[along_axis]
    widths = [(15, 15) if dim_index == along_axis else (0, 0) for dim_index in range(volume.ndim)]
    padded = jnp.pad(volume, widths)
    summed = jnp.zeros(volume.shape, jnp.float32)
    for tap_index in range(15):
        begin = (15 + orient * (tap_index - 7 + offset_cells)).astype(jnp.int32)
        summed = summed + filter_taps[tap_index] * lax.dynamic_slice_in_dim(padded, begin, extent, along_axis)
    return summed


def blur_view(volume, filter_rows, shift_pair, orient):
    zero_shift = jnp.zeros((), jnp.int32)
    section_rows = blur_axis(volume, filter_rows[1], zero_shift, 1, orient)
    section_depth = blur_axis(section_rows, filter_rows[0], shift_pair[0].astype(jnp.int32), 0, orient)
    return blur_axis(section_depth, filter_rows[2], shift_pair[1].astype(jnp.int32), 2, orient)


def reference(observed, initial, psf_taps, view_shifts, view_map):
    volumes = observed.astype(jnp.float32)
    view_count, depth_cells, row_count, width_cells = volumes.shape
    blocked = volumes.reshape(view_count, depth_cells, row_count, width_cells // BX, BX)
    spectra = jnp.fft.fftn(blocked, axes=(1, 2, 4), norm="ortho")
    ref_slot = jnp.sum(jnp.where(view_map == 0, jnp.arange(VIEWS, dtype=jnp.int32), 0)).astype(jnp.int32)
    ref_spec = spectra[ref_slot]
    cross = spectra * jnp.conj(ref_spec) / (jnp.abs(spectra) * jnp.abs(ref_spec) + 1.0)
    surfaces = jnp.real(jnp.fft.ifftn(cross, axes=(1, 2, 4), norm="ortho"))
    surfaces = surfaces.reshape(volumes.shape).astype(jnp.float32)
    estimate = initial
    for iteration in range(ITERS):
        product = jnp.ones(estimate.shape, jnp.float32)
        for slot_index in range(VIEWS):
            view_id = view_map[slot_index]
            filter_rows = psf_taps[view_id]
            shift_pair = view_shifts[view_id]
            blurred = blur_view(estimate, filter_rows, shift_pair, 1)
            ratio_field = volumes[slot_index] / blurred
            product = product * blur_view(ratio_field, filter_rows, shift_pair, -1)
        estimate = estimate * jnp.exp(jnp.log(product) / VIEWS)
    return estimate, surfaces
```

```python
import functools
import math

import jax
import jax.numpy as jnp
import ml_dtypes
import numpy as np
from jax import lax
from jax.experimental import pallas as pl
from jax.experimental.pallas import tpu as pltpu
from jax.sharding import PartitionSpec as P

ITERS = 2
TAPS = 15
HALF = TAPS // 2
ROWS = 8
MID = 1.099609375


F32 = jnp.float32
BF16 = jnp.bfloat16


def dot(a, b):
    return jnp.dot(a, b, preferred_element_type=F32)


def dot_t(a, b):
    return lax.dot_general(a, b, (((1,), (1,)), ((), ())), preferred_element_type=F32)


def split(value):
    high = value.astype(BF16)
    return high, (value - high.astype(F32)).astype(BF16)


def np_split(table):
    high = table.astype(ml_dtypes.bfloat16)
    low = (table - high.astype(np.float64)).astype(ml_dtypes.bfloat16)
    return high, low


def side_by_side(table):
    return jnp.asarray(np.concatenate(np_split(table), 1))


def depth_order(depth):
    order = [0, depth // 2]
    for m in range(1, depth // 2):
        order += [m, depth - m]
    return np.array(order)


def angle_table(rows, columns, length):
    return 2.0 * np.pi * ((rows[:, None] * columns[None, :]) % length) / length


def depth_tables(depth):
    order = depth_order(depth)
    angles = angle_table(order, np.arange(depth), depth)
    scale = 1.0 / math.sqrt(depth)
    eye = np.eye(ROWS)
    cos_part = np.kron(np.cos(angles) * scale, eye)
    sin_part = np.kron(np.sin(angles) * scale, eye)
    forward = side_by_side(np.concatenate([cos_part, sin_part], 0))
    inverse = side_by_side(np.concatenate([cos_part.T, sin_part.T], 0))
    return forward, inverse


def row_table(length):
    positions = np.arange(length)
    angles = angle_table(positions, positions, length)
    scale = 1.0 / math.sqrt(length)
    return side_by_side(np.concatenate([np.cos(angles), np.sin(angles)], 0) * scale)


def column_tables(width):
    half = width // 2
    positions = np.arange(width)
    freqs = np.arange(half)
    angles = angle_table(positions, freqs, width)
    scale = 1.0 / math.sqrt(width)
    cos_part = np.cos(angles)
    sin_part = -np.sin(angles)
    sin_part[:, 0] = 1.0 - 2.0 * (positions % 2)
    forward = np.concatenate([cos_part, sin_part], 1) * scale
    weights = np.where(freqs == 0, 1.0, 2.0)
    inverse = np.concatenate([cos_part * weights, sin_part * weights], 1).T * scale
    return side_by_side(forward), side_by_side(inverse)


def table_times(table, block):
    size = block.shape[0]
    high, low = split(block)
    return dot(table, jnp.concatenate([high, high], 0)) + dot(table[:, :size], low)


def turned(table, block, orient):
    size = block.shape[0]
    half = block.shape[1] // 2
    both = table_times(table, block)
    cos_real, cos_imag = both[:size, :half], both[:size, half:]
    sin_real, sin_imag = both[size:, :half], both[size:, half:]
    if orient > 0:
        return cos_real + sin_imag, cos_imag - sin_real
    return cos_real - sin_imag, cos_imag + sin_real


def first_kernel(order_ref, observed_ref, columns_ref, depth_ref, out_ref):
    depth, rows, width = observed_ref.shape[1:]
    half = width // 2
    groups, _, local_depth = out_ref.shape[:3]
    flat = observed_ref[0].reshape(depth * rows, width)
    table = columns_ref[...]
    spread = dot(flat, table[:, :width]) + dot(flat, table[:, width:])
    spread = spread.reshape(depth, rows, width)
    shift = MID * math.sqrt(width) * math.sqrt(depth)
    for at in range(0, rows, ROWS):
        block = spread[:, at : at + ROWS].reshape(depth * ROWS, width)
        real, imag = turned(depth_ref[...], block, 1)
        row_id = lax.broadcasted_iota(jnp.int32, real.shape, 0)
        lane_id = lax.broadcasted_iota(jnp.int32, real.shape, 1)
        real = jnp.where((row_id < ROWS) & (lane_id == 0), real - shift, real)
        shape = (groups, local_depth, ROWS, half)
        out_ref[:, 0, :, at : at + ROWS, :half] = real.reshape(shape)
        out_ref[:, 0, :, at : at + ROWS, half:] = imag.reshape(shape)


def load_planes(in_ref, group_zero):
    groups, _, local_depth, rows, width = in_ref.shape
    half = width // 2
    length = groups * rows
    raw = [in_ref[:, 0, k].reshape(length, width) for k in range(local_depth)]
    lane = lax.broadcasted_iota(jnp.int32, (length, width), 1)
    edge = (lane == 0) | (lane == half)
    sign = jnp.where(lane == half, -1.0, 1.0)
    top_lane = lax.broadcasted_iota(jnp.int32, (length, half), 1)
    top_real = jnp.zeros((length, half), F32)
    top_imag = jnp.zeros((length, half), F32)
    planes = []
    for k in range(local_depth):
        partner = raw[k ^ 1]
        if k < 2:
            partner = jnp.where(group_zero, raw[k], partner)
        planes.append(jnp.where(edge, 0.5 * (raw[k] + sign * partner), raw[k]))
        real_col = 0.5 * (raw[k][:, half : half + 1] + partner[:, half : half + 1])
        imag_col = -0.5 * (raw[k][:, :1] - partner[:, :1])
        top_real = jnp.where(top_lane == k, real_col, top_real)
        top_imag = jnp.where(top_lane == k, imag_col, top_imag)
    planes.append(jnp.concatenate([top_real, top_imag], 1))
    return planes


def spectrum(table, plane, is_first, group_zero, depth):
    real, imag = turned(table, plane, 1)
    if is_first:
        shift = MID * math.sqrt(depth * plane.shape[0] * plane.shape[1])
        row_id = lax.broadcasted_iota(jnp.int32, real.shape, 0)
        lane_id = lax.broadcasted_iota(jnp.int32, real.shape, 1)
        here = (row_id == 0) & (lane_id == 0) & group_zero
        real = jnp.where(here, real + shift, real)
    return real, imag


def spectrum_kernel(place_ref, in_ref, rows_ref, out_ref):
    group_zero = place_ref[1] == 0
    depth = in_ref.shape[0] * in_ref.shape[2]
    half = in_ref.shape[4] // 2
    table = rows_ref[...]
    for k, plane in enumerate(load_planes(in_ref, group_zero)):
        real, imag = spectrum(table, plane, k == 0, group_zero, depth)
        out_ref[k, :, :half] = real
        out_ref[k, :, half:] = imag


def cross_kernel(place_ref, in_ref, rows_ref, mine_ref, other_ref, out_ref):
    holds_ref = place_ref[0] == 1
    group_zero = place_ref[1] == 0
    groups, _, local_depth, rows, width = in_ref.shape
    depth = groups * local_depth
    half = width // 2
    length = groups * rows
    table = rows_ref[...]
    back = []
    for k, plane in enumerate(load_planes(in_ref, group_zero)):
        real, imag = spectrum(table, plane, k == 0, group_zero, depth)
        ref = jnp.where(holds_ref, mine_ref[k], other_ref[k])
        ref_real, ref_imag = ref[:, :half], ref[:, half:]
        power = (real * real + imag * imag) * (ref_real * ref_real + ref_imag * ref_imag)
        scale = 1.0 / (jnp.sqrt(power) + 1.0)
        cross_real = (real * ref_real + imag * ref_imag) * scale
        cross_imag = (imag * ref_real - real * ref_imag) * scale
        back.append(turned(table, jnp.concatenate([cross_real, cross_imag], 1), -1))
    top_real, top_imag = back[local_depth]
    lane = lax.broadcasted_iota(jnp.int32, (length, half), 1)
    for k in range(local_depth):
        real, imag = back[k]
        real = jnp.where(lane == 0, real - top_imag[:, k : k + 1], real)
        imag = jnp.where(lane == 0, imag + top_real[:, k : k + 1], imag)
        out_ref[:, 0, k, :, :half] = real.reshape(groups, rows, half)
        out_ref[:, 0, k, :, half:] = imag.reshape(groups, rows, half)


def last_kernel(order_ref, in_ref, columns_ref, depth_ref, *rest):
    out_ref = rest[-1]
    groups, _, local_depth, rows, width = in_ref.shape
    depth = groups * local_depth
    table = columns_ref[...]
    for at in range(0, rows, ROWS):
        block = in_ref[:, 0, :, at : at + ROWS].reshape(depth * ROWS, width)
        real, imag = turned(depth_ref[...], block, -1)
        high, low = split(jnp.concatenate([real, imag], 1))
        cells = dot(high, table[:, :width]) + dot(high, table[:, width:]) + dot(low, table[:, :width])
        out_ref[0, :, at : at + ROWS] = cells.reshape(depth, ROWS, width)


def pick_tap(psf_ref, base, index):
    value = jnp.zeros(index.shape, F32)
    for j in range(TAPS):
        value = jnp.where(index == j, psf_ref[base + j], value)
    return value


def filter_kernel(place_ref, map_ref, shift_ref, psf_ref, forward_ref, backward_ref, columns_ref):
    slots = forward_ref.shape[0]
    size = forward_ref.shape[1]
    width = columns_ref.shape[1]
    depth = size // ROWS
    view = map_ref[place_ref[0] * pl.num_programs(0) + pl.program_id(0)]
    depth_shift = shift_ref[view * 2]
    column_shift = shift_ref[view * 2 + 1]
    base = view * (3 * TAPS)
    at_out = lax.broadcasted_iota(jnp.int32, (depth, size), 0)
    at_in = lax.broadcasted_iota(jnp.int32, (depth, size), 1) // ROWS
    row = lax.broadcasted_iota(jnp.int32, (ROWS, size), 0)
    cell = lax.broadcasted_iota(jnp.int32, (ROWS, size), 1) % ROWS
    for out_ref, orient in ((forward_ref, 1), (backward_ref, -1)):
        depth_part = pick_tap(psf_ref, base, orient * (at_in - at_out) + HALF - depth_shift)
        for c in range(3):
            reach = c * ROWS + cell - ROWS - row
            row_part = pick_tap(psf_ref, base + TAPS, orient * reach + HALF)
            block = depth_part[:, None, :] * row_part[None, :, :]
            out_ref[0, :, c * size : (c + 1) * size] = block.reshape(size, size).astype(BF16)
    source = lax.broadcasted_iota(jnp.int32, (width, width), 0)
    target = lax.broadcasted_iota(jnp.int32, (width, width), 1)
    picked = pick_tap(psf_ref, base + 2 * TAPS, source - target + HALF - column_shift)
    columns_ref[0] = picked.astype(BF16)


def join_kernel(
    views,
    estimate_ref,
    below_ref,
    above_ref,
    observed_ref,
    seen_below_ref,
    seen_above_ref,
    forward_ref,
    backward_ref,
    columns_ref,
    out_ref,
    cells_ref,
    ratio_ref,
    product_ref,
):
    depth, rows, width = estimate_ref.shape
    size = depth * ROWS
    blocks = rows // ROWS
    step = pl.program_id(0)

    @pl.when(step == 0)
    def _():
        for rim_ref, start in ((below_ref, 0), (above_ref, blocks + 2)):
            rim = rim_ref[...].astype(F32)
            for b in range(2):
                piece = rim[:, b * ROWS : (b + 1) * ROWS].reshape(size, width)
                cells_ref[start + b] = piece.astype(BF16)
        for b in range(blocks):
            piece = estimate_ref[:, b * ROWS : (b + 1) * ROWS].reshape(size, width)
            cells_ref[b + 2] = piece.astype(BF16)
        product_ref[...] = jnp.ones_like(product_ref)

    columns = columns_ref[0]
    for b in range(blocks + 2):
        window = cells_ref[b : b + 3].reshape(3 * size, width)
        mixed = dot(forward_ref[0], window).astype(BF16)
        blurred = dot(mixed, columns)
        if b == 0:
            seen = seen_below_ref[0].astype(F32)
        elif b == blocks + 1:
            seen = seen_above_ref[0].astype(F32)
        else:
            seen = observed_ref[0, :, (b - 1) * ROWS : b * ROWS].astype(F32)
        seen = seen.reshape(size, width)
        ratio = jnp.where(seen > 0.0, seen / blurred, 0.0).astype(BF16)
        ratio_ref[b] = dot_t(ratio, columns).astype(BF16)
    for b in range(blocks):
        window = ratio_ref[b : b + 3].reshape(3 * size, width)
        product_ref[b] = product_ref[b] * dot(backward_ref[0], window)

    @pl.when(step == pl.num_programs(0) - 1)
    def _():
        for b in range(blocks):
            logs = jnp.log(product_ref[b]) * (1.0 / views)
            out_ref[:, b * ROWS : (b + 1) * ROWS] = logs.reshape(depth, ROWS, width)


def whole(shape):
    return pl.BlockSpec(shape, lambda *_: (0,) * len(shape))


def cost(flops, moved):
    return pl.CostEstimate(flops=int(flops), bytes_accessed=int(moved), transcendentals=0)


def turn(payload):
    sent = lax.all_to_all(payload.astype(jnp.float16), "gz", split_axis=0, concat_axis=0, tiled=True)
    return sent.astype(F32)


def send_rims(field, dim, width):
    count = lax.axis_size("gz")
    extent = field.shape[dim]
    head = lax.slice_in_dim(field, 0, width, axis=dim)
    tail = lax.slice_in_dim(field, extent - width, extent, axis=dim)
    below = lax.ppermute(tail, "gz", [(i, i + 1) for i in range(count - 1)])
    above = lax.ppermute(head, "gz", [(i + 1, i) for i in range(count - 1)])
    return below, above


def swap_cores(field):
    count = lax.axis_size("view")
    return lax.ppermute(field, "view", [(i, (i + 1) % count) for i in range(count)])


def on_device(observed, initial, psf_taps, view_shifts, view_map):
    slots, depth, rows, width = observed.shape
    views = view_map.shape[0]
    groups = lax.axis_size("gz")
    length = groups * rows
    local_depth = depth // groups
    half = width // 2
    size = depth * ROWS
    blocks = rows // ROWS
    core = lax.axis_index("view")
    group = lax.axis_index("gz")
    ref_slot = jnp.sum(jnp.where(view_map == 0, jnp.arange(views, dtype=jnp.int32), 0)).astype(jnp.int32)
    holds_ref = (ref_slot // slots == core).astype(jnp.int32)
    order = (ref_slot % slots).reshape(1)
    place = jnp.stack([holds_ref, group]).astype(jnp.int32)
    core_at = core.astype(jnp.int32).reshape(1)

    depth_forward, depth_inverse = depth_tables(depth)
    columns_forward, columns_inverse = column_tables(width)
    row_turn = row_table(length)

    seen_rims = send_rims(observed, 2, ROWS)
    rims = send_rims(initial.astype(BF16), 1, 2 * ROWS)

    chunk = slots // 2
    payload_block = (groups, 1, local_depth, rows, width)
    payload_shape = (groups, chunk, local_depth, rows, width)
    payload_bytes = 4 * depth * rows * width * chunk
    volume = depth * rows * width

    def first(start):
        return pl.pallas_call(
            first_kernel,
            grid_spec=pltpu.PrefetchScalarGridSpec(
                num_scalar_prefetch=1,
                grid=(chunk,),
                in_specs=[
                    pl.BlockSpec((1, depth, rows, width), lambda s, o: (lax.rem(s + start + o[0], slots), 0, 0, 0)),
                    whole(columns_forward.shape),
                    whole(depth_forward.shape),
                ],
                out_specs=pl.BlockSpec(payload_block, lambda s, o: (0, s, 0, 0, 0)),
            ),
            out_shape=jax.ShapeDtypeStruct(payload_shape, F32),
            cost_estimate=cost(2 * chunk * volume * (2 * width + 6 * size), payload_bytes * 1.5),
            name="first",
        )(order, observed, columns_forward, depth_forward)

    planes = local_depth + 1
    spectrum_shape = (planes, length, width)
    row_flops = 2 * planes * length * width * 6 * length

    def reference_spectrum(payload):
        return pl.pallas_call(
            spectrum_kernel,
            grid_spec=pltpu.PrefetchScalarGridSpec(
                num_scalar_prefetch=1,
                grid=(1,),
                in_specs=[
                    pl.BlockSpec(payload_block, lambda s, o: (0, 0, 0, 0, 0)),
                    whole(row_turn.shape),
                ],
                out_specs=whole(spectrum_shape),
            ),
            out_shape=jax.ShapeDtypeStruct(spectrum_shape, F32),
            cost_estimate=cost(row_flops, 8 * volume),
            name="spectrum",
        )(place, payload, row_turn)

    def crossed(payload, mine, other):
        return pl.pallas_call(
            cross_kernel,
            grid_spec=pltpu.PrefetchScalarGridSpec(
                num_scalar_prefetch=1,
                grid=(chunk,),
                in_specs=[
                    pl.BlockSpec(payload_block, lambda s, o: (0, s, 0, 0, 0)),
                    whole(row_turn.shape),
                    whole(spectrum_shape),
                    whole(spectrum_shape),
                ],
                out_specs=pl.BlockSpec(payload_block, lambda s, o: (0, s, 0, 0, 0)),
            ),
            out_shape=jax.ShapeDtypeStruct(payload_shape, F32),
            cost_estimate=cost(2 * row_flops * chunk, payload_bytes * 2 + 10 * volume),
            name="cross",
        )(place, payload, row_turn, mine, other)

    def last(payload, start, partial):
        specs = [
            pl.BlockSpec(payload_block, lambda s, o: (0, s, 0, 0, 0)),
            whole(columns_inverse.shape),
            whole(depth_inverse.shape),
        ]
        operands = [order, payload, columns_inverse, depth_inverse]
        aliases = {}
        if partial is not None:
            specs.append(pl.BlockSpec(memory_space=pl.ANY))
            aliases = {len(operands): 0}
            operands.append(partial)
        return pl.pallas_call(
            last_kernel,
            grid_spec=pltpu.PrefetchScalarGridSpec(
                num_scalar_prefetch=1,
                grid=(chunk,),
                in_specs=specs,
                out_specs=pl.BlockSpec((1, depth, rows, width), lambda s, o: (lax.rem(s + start + o[0], slots), 0, 0, 0)),
            ),
            out_shape=jax.ShapeDtypeStruct((slots, depth, rows, width), F32),
            input_output_aliases=aliases,
            cost_estimate=cost(2 * chunk * volume * (3 * width + 6 * size), payload_bytes * 2),
            name="last",
        )(*operands)

    def filters():
        smem = pl.BlockSpec(memory_space=pltpu.SMEM)
        return pl.pallas_call(
            filter_kernel,
            grid=(slots,),
            in_specs=[smem] * 4,
            out_specs=[
                pl.BlockSpec((1, size, 3 * size), lambda s: (s, 0, 0)),
                pl.BlockSpec((1, size, 3 * size), lambda s: (s, 0, 0)),
                pl.BlockSpec((1, width, width), lambda s: (s, 0, 0)),
            ],
            out_shape=[
                jax.ShapeDtypeStruct((slots, size, 3 * size), BF16),
                jax.ShapeDtypeStruct((slots, size, 3 * size), BF16),
                jax.ShapeDtypeStruct((slots, width, width), BF16),
            ],
            cost_estimate=cost(slots * size * size * 60, slots * size * size * 14),
            name="filters",
        )(core_at, view_map, view_shifts.reshape(-1), psf_taps.reshape(-1))

    forward, backward, columns = filters()

    def join(estimate, below, above):
        def slot_block(shape):
            return pl.BlockSpec((1,) + shape, lambda s: (s,) + (0,) * len(shape))

        return pl.pallas_call(
            functools.partial(join_kernel, views),
            grid=(slots,),
            in_specs=[
                whole((depth, rows, width)),
                whole((depth, 2 * ROWS, width)),
                whole((depth, 2 * ROWS, width)),
                slot_block((depth, rows, width)),
                slot_block((depth, ROWS, width)),
                slot_block((depth, ROWS, width)),
                slot_block((size, 3 * size)),
                slot_block((size, 3 * size)),
                slot_block((width, width)),
            ],
            out_specs=whole((depth, rows, width)),
            out_shape=jax.ShapeDtypeStruct((depth, rows, width), F32),
            scratch_shapes=[
                pltpu.VMEM((blocks + 4, size, width), BF16),
                pltpu.VMEM((blocks + 2, size, width), BF16),
                pltpu.VMEM((blocks, size, width), F32),
            ],
            cost_estimate=cost(2 * slots * size * width * ((blocks + 2) * (3 * size + 2 * width) + blocks * 3 * size), 12e6),
            name="join",
        )(estimate, below, above, observed, seen_rims[0], seen_rims[1], forward, backward, columns)

    sent_a = turn(first(0))
    sent_b = turn(first(chunk))

    estimate = initial
    for iteration in range(ITERS):
        if iteration:
            rims = send_rims(estimate.astype(BF16), 1, 2 * ROWS)
        logs = join(estimate, *rims)
        estimate = estimate * jnp.exp(logs + swap_cores(logs))

    mine = reference_spectrum(sent_a)
    other = swap_cores(mine)
    back_a = turn(crossed(sent_a, mine, other))
    back_b = turn(crossed(sent_b, mine, other))
    surfaces = last(back_a, 0, None)
    surfaces = last(back_b, chunk, surfaces)
    return estimate, surfaces


def solution(mesh):
    placed = (P("view", "parts", "gz", None), P("parts", "gz", None), P(), P(), P())
    return jax.shard_map(
        on_device,
        mesh=mesh,
        in_specs=placed,
        out_specs=(P("parts", "gz", None), P("view", "parts", "gz", None)),
        check_vma=False,
    )
```

```python
import functools
import math

import jax
import jax.numpy as jnp
import ml_dtypes
import numpy as np
from jax import lax
from jax.experimental import pallas as pl
from jax.experimental.pallas import tpu as pltpu
from jax.sharding import PartitionSpec as P

ITERS = 2
TAPS = 15
HALF = TAPS // 2
ROWS = 8
MID = 1.099609375


F32 = jnp.float32
BF16 = jnp.bfloat16


def dot(a, b):
    return jnp.dot(a, b, preferred_element_type=F32)


def dot_t(a, b):
    return lax.dot_general(a, b, (((1,), (1,)), ((), ())), preferred_element_type=F32)


def split(value):
    high = value.astype(BF16)
    return high, (value - high.astype(F32)).astype(BF16)


def np_split(table):
    high = table.astype(ml_dtypes.bfloat16)
    low = (table - high.astype(np.float64)).astype(ml_dtypes.bfloat16)
    return high, low


def side_by_side(table):
    return jnp.asarray(np.concatenate(np_split(table), 1))


def depth_order(depth):
    order = [0, depth // 2]
    for m in range(1, depth // 2):
        order += [m, depth - m]
    return np.array(order)


def angle_table(rows, columns, length):
    return 2.0 * np.pi * ((rows[:, None] * columns[None, :]) % length) / length


def depth_transform(real, imag, orient):
    count = len(real)
    if count == 1:
        return real, imag
    if count == 2:
        return [real[0] + real[1], real[0] - real[1]], [imag[0] + imag[1], imag[0] - imag[1]]
    quarter = count // 4
    parts = [depth_transform(real[j::4], imag[j::4], orient) for j in range(4)]
    out_real, out_imag = [None] * count, [None] * count
    for k in range(quarter):
        turned_parts = []
        for j in range(4):
            part_real, part_imag = parts[j][0][k], parts[j][1][k]
            if j * k:
                angle = -orient * 2.0 * math.pi * j * k / count
                cos, sin = math.cos(angle), math.sin(angle)
                if 8 * j * k == count:
                    part_real, part_imag = (part_real + orient * part_imag) * cos, (part_imag - orient * part_real) * cos
                else:
                    part_real, part_imag = part_real * cos - part_imag * sin, part_real * sin + part_imag * cos
            turned_parts.append((part_real, part_imag))
        (ar, ai), (br, bi), (cr, ci), (dr, di) = turned_parts
        sum_ac, dif_ac = (ar + cr, ai + ci), (ar - cr, ai - ci)
        sum_bd, dif_bd = (br + dr, bi + di), (br - dr, bi - di)
        out_real[k], out_imag[k] = sum_ac[0] + sum_bd[0], sum_ac[1] + sum_bd[1]
        out_real[k + 2 * quarter], out_imag[k + 2 * quarter] = sum_ac[0] - sum_bd[0], sum_ac[1] - sum_bd[1]
        plus = (dif_ac[0] + dif_bd[1], dif_ac[1] - dif_bd[0])
        minus = (dif_ac[0] - dif_bd[1], dif_ac[1] + dif_bd[0])
        first_part, second_part = (plus, minus) if orient > 0 else (minus, plus)
        out_real[k + quarter], out_imag[k + quarter] = first_part
        out_real[k + 3 * quarter], out_imag[k + 3 * quarter] = second_part
    return out_real, out_imag


def forward_bound(depth, width):
    return 0.9005 * math.sqrt(depth * width)


def backward_bound(length):
    return 2.001 * math.sqrt(length)


def encode(value, bound):
    scaled = value * lax.rsqrt(jnp.abs(value) + 1e-30) * (32767.0 / math.sqrt(bound))
    return (scaled + jnp.where(value < 0.0, -0.5, 0.5)).astype(jnp.int32).astype(jnp.int16)


def decode(code, bound):
    value = code.astype(jnp.int32).astype(F32)
    return value * jnp.abs(value) * (bound / 32767.0**2)


def row_table(length):
    positions = np.arange(length)
    angles = angle_table(positions, positions, length)
    scale = 1.0 / math.sqrt(length)
    return side_by_side(np.concatenate([np.cos(angles), np.sin(angles)], 0) * scale)


def column_tables(width, depth):
    half = width // 2
    positions = np.arange(width)
    freqs = np.arange(half)
    angles = angle_table(positions, freqs, width)
    scale = 1.0 / math.sqrt(width * depth)
    cos_part = np.cos(angles)
    sin_part = -np.sin(angles)
    sin_part[:, 0] = 1.0 - 2.0 * (positions % 2)
    forward = np.concatenate([cos_part, sin_part], 1) * scale
    weights = np.where(freqs == 0, 1.0, 2.0)
    inverse = np.concatenate([cos_part * weights, sin_part * weights], 1).T * scale
    return side_by_side(forward), side_by_side(inverse)


def table_times(table, block):
    size = block.shape[0]
    high, low = split(block)
    return dot(table, jnp.concatenate([high, high], 0)) + dot(table[:, :size], low)


def turned(table, block, orient):
    size = block.shape[0]
    half = block.shape[1] // 2
    both = table_times(table, block)
    cos_real, cos_imag = both[:size, :half], both[:size, half:]
    sin_real, sin_imag = both[size:, :half], both[size:, half:]
    if orient > 0:
        return cos_real + sin_imag, cos_imag - sin_real
    return cos_real - sin_imag, cos_imag + sin_real


def first_kernel(order_ref, observed_ref, columns_ref, out_ref, spread_ref, turned_ref):
    depth, rows, width = observed_ref.shape[1:]
    half = width // 2
    groups, _, local_depth = out_ref.shape[:3]
    flat = observed_ref[0].reshape(depth * rows, width)
    table = columns_ref[...]
    spread = dot(flat, table[:, :width]) + dot(flat, table[:, width:])
    spread_ref[...] = spread.reshape(depth, rows, width)
    shift = MID * math.sqrt(width * depth)
    spots = depth_order(depth)
    lane = lax.broadcasted_iota(jnp.int32, (ROWS, half), 1)

    @pl.loop(0, rows // ROWS)
    def _(b):
        at = pl.ds(pl.multiple_of(b * ROWS, ROWS), ROWS)
        real = [spread_ref[z, at, :half] for z in range(depth)]
        imag = [spread_ref[z, at, half:] for z in range(depth)]
        real, imag = depth_transform(real, imag, 1)
        real[0] = jnp.where(lane == 0, real[0] - shift, real[0])
        for spot, k in enumerate(spots):
            turned_ref[spot, at, :half] = real[k]
            turned_ref[spot, at, half:] = imag[k]

    code = encode(turned_ref[...], forward_bound(depth, width))
    out_ref[:, 0] = code.reshape(groups, local_depth, rows, width)


def load_planes(in_ref, group_zero):
    groups, _, local_depth, rows, width = in_ref.shape
    half = width // 2
    length = groups * rows
    bound = forward_bound(groups * local_depth, width)
    raw = [decode(in_ref[:, 0, k].reshape(length, width), bound) for k in range(local_depth)]
    lane = lax.broadcasted_iota(jnp.int32, (length, width), 1)
    edge = (lane == 0) | (lane == half)
    sign = jnp.where(lane == half, -1.0, 1.0)
    top_lane = lax.broadcasted_iota(jnp.int32, (length, half), 1)
    top_real = jnp.zeros((length, half), F32)
    top_imag = jnp.zeros((length, half), F32)
    planes = []
    for k in range(local_depth):
        partner = raw[k ^ 1]
        if k < 2:
            partner = jnp.where(group_zero, raw[k], partner)
        planes.append(jnp.where(edge, 0.5 * (raw[k] + sign * partner), raw[k]))
        real_col = 0.5 * (raw[k][:, half : half + 1] + partner[:, half : half + 1])
        imag_col = -0.5 * (raw[k][:, :1] - partner[:, :1])
        top_real = jnp.where(top_lane == k, real_col, top_real)
        top_imag = jnp.where(top_lane == k, imag_col, top_imag)
    planes.append(jnp.concatenate([top_real, top_imag], 1))
    return planes


def spectrum(table, plane, is_first, group_zero, depth):
    real, imag = turned(table, plane, 1)
    if is_first:
        shift = MID * math.sqrt(depth * plane.shape[0] * plane.shape[1])
        row_id = lax.broadcasted_iota(jnp.int32, real.shape, 0)
        lane_id = lax.broadcasted_iota(jnp.int32, real.shape, 1)
        here = (row_id == 0) & (lane_id == 0) & group_zero
        real = jnp.where(here, real + shift, real)
    return real, imag


def spectrum_kernel(place_ref, in_ref, rows_ref, out_ref):
    group_zero = place_ref[1] == 0
    depth = in_ref.shape[0] * in_ref.shape[2]
    half = in_ref.shape[4] // 2
    table = rows_ref[...]
    for k, plane in enumerate(load_planes(in_ref, group_zero)):
        real, imag = spectrum(table, plane, k == 0, group_zero, depth)
        out_ref[k, :, :half] = real
        out_ref[k, :, half:] = imag


def cross_kernel(place_ref, in_ref, rows_ref, mine_ref, other_ref, out_ref):
    holds_ref = place_ref[0] == 1
    group_zero = place_ref[1] == 0
    groups, _, local_depth, rows, width = in_ref.shape
    depth = groups * local_depth
    half = width // 2
    length = groups * rows
    table = rows_ref[...]
    back = []
    for k, plane in enumerate(load_planes(in_ref, group_zero)):
        real, imag = spectrum(table, plane, k == 0, group_zero, depth)
        ref = jnp.where(holds_ref, mine_ref[k], other_ref[k])
        ref_real, ref_imag = ref[:, :half], ref[:, half:]
        power = (real * real + imag * imag) * (ref_real * ref_real + ref_imag * ref_imag)
        scale = 1.0 / (jnp.sqrt(power) + 1.0)
        cross_real = (real * ref_real + imag * ref_imag) * scale
        cross_imag = (imag * ref_real - real * ref_imag) * scale
        back.append(turned(table, jnp.concatenate([cross_real, cross_imag], 1), -1))
    top_real, top_imag = back[local_depth]
    lane = lax.broadcasted_iota(jnp.int32, (length, half), 1)
    for k in range(local_depth):
        real, imag = back[k]
        real = jnp.where(lane == 0, real - top_imag[:, k : k + 1], real)
        imag = jnp.where(lane == 0, imag + top_real[:, k : k + 1], imag)
        out_ref[:, 0, k, :, :half] = encode(real, backward_bound(length)).reshape(groups, rows, half)
        out_ref[:, 0, k, :, half:] = encode(imag, backward_bound(length)).reshape(groups, rows, half)


def last_kernel(order_ref, in_ref, columns_ref, *rest):
    out_ref, turned_ref, spread_ref = rest[-3:]
    groups, _, local_depth, rows, width = in_ref.shape
    depth = groups * local_depth
    half = width // 2
    table = columns_ref[...]
    spots = depth_order(depth)
    value = decode(in_ref[:, 0], backward_bound(groups * rows))
    turned_ref[...] = value.reshape(depth, rows, width)

    @pl.loop(0, rows // ROWS)
    def _(b):
        at = pl.ds(pl.multiple_of(b * ROWS, ROWS), ROWS)
        real, imag = [None] * depth, [None] * depth
        for spot, k in enumerate(spots):
            real[k] = turned_ref[spot, at, :half]
            imag[k] = turned_ref[spot, at, half:]
        real, imag = depth_transform(real, imag, -1)
        for z in range(depth):
            spread_ref[z, at, :half] = real[z]
            spread_ref[z, at, half:] = imag[z]

    high, low = split(spread_ref[...].reshape(depth * rows, width))
    cells = dot(high, table[:, :width]) + dot(high, table[:, width:]) + dot(low, table[:, :width])
    out_ref[0] = cells.reshape(depth, rows, width)


def pick_tap(psf_ref, base, index):
    value = jnp.zeros(index.shape, F32)
    for j in range(TAPS):
        value = jnp.where(index == j, psf_ref[base + j], value)
    return value


def filter_kernel(place_ref, map_ref, shift_ref, psf_ref, forward_ref, backward_ref, columns_ref):
    slots = forward_ref.shape[0]
    size = forward_ref.shape[1]
    width = columns_ref.shape[1]
    depth = size // ROWS
    view = map_ref[place_ref[0] * pl.num_programs(0) + pl.program_id(0)]
    depth_shift = shift_ref[view * 2]
    column_shift = shift_ref[view * 2 + 1]
    base = view * (3 * TAPS)
    at_out = lax.broadcasted_iota(jnp.int32, (depth, size), 0)
    at_in = lax.broadcasted_iota(jnp.int32, (depth, size), 1) // ROWS
    row = lax.broadcasted_iota(jnp.int32, (ROWS, size), 0)
    cell = lax.broadcasted_iota(jnp.int32, (ROWS, size), 1) % ROWS
    for out_ref, orient in ((forward_ref, 1), (backward_ref, -1)):
        depth_part = pick_tap(psf_ref, base, orient * (at_in - at_out) + HALF - depth_shift)
        for c in range(3):
            reach = c * ROWS + cell - ROWS - row
            row_part = pick_tap(psf_ref, base + TAPS, orient * reach + HALF)
            block = depth_part[:, None, :] * row_part[None, :, :]
            out_ref[0, :, c * size : (c + 1) * size] = block.reshape(size, size).astype(BF16)
    source = lax.broadcasted_iota(jnp.int32, (width, width), 0)
    target = lax.broadcasted_iota(jnp.int32, (width, width), 1)
    picked = pick_tap(psf_ref, base + 2 * TAPS, source - target + HALF - column_shift)
    columns_ref[0] = picked.astype(BF16)


def join_kernel(
    views,
    estimate_ref,
    below_ref,
    above_ref,
    observed_ref,
    seen_below_ref,
    seen_above_ref,
    forward_ref,
    backward_ref,
    columns_ref,
    out_ref,
    cells_ref,
    mixed_ref,
    blurred_ref,
    ratio_ref,
    product_ref,
):
    depth, rows, width = estimate_ref.shape
    size = depth * ROWS
    blocks = rows // ROWS
    slots = forward_ref.shape[0]
    step = pl.program_id(0)

    @pl.when(step == 0)
    def _():
        for rim_ref, start in ((below_ref, 0), (above_ref, blocks + 2)):
            for b in range(2):
                piece = rim_ref[b].astype(F32).reshape(size, width)
                cells_ref[start + b] = piece.astype(BF16)
        for b in range(blocks):
            piece = estimate_ref[:, b * ROWS : (b + 1) * ROWS].reshape(size, width)
            cells_ref[b + 2] = piece.astype(BF16)
        product_ref[...] = jnp.ones_like(product_ref)

        @pl.loop(0, blocks + 2)
        def _(b):
            window = cells_ref[pl.ds(b, 3)].reshape(3 * size, width)
            mixed = dot(forward_ref[...].reshape(slots * size, 3 * size), window)
            mixed_ref[:, b] = mixed.astype(BF16).reshape(slots, size, width)

    columns = columns_ref[0]
    blurred = dot(mixed_ref[step].reshape((blocks + 2) * size, width), columns)
    blurred_ref[...] = blurred.reshape(blocks + 2, size, width)
    for b in range(blocks + 2):
        if b == 0:
            seen = seen_below_ref[0].astype(F32)
        elif b == blocks + 1:
            seen = seen_above_ref[0].astype(F32)
        else:
            seen = observed_ref[0, :, (b - 1) * ROWS : b * ROWS].astype(F32)
        seen = seen.reshape(size, width)
        ratio = jnp.where(seen > 0.0, seen / blurred_ref[b], 0.0)
        ratio_ref[b] = ratio.astype(BF16)
    ratio = dot_t(ratio_ref[...].reshape((blocks + 2) * size, width), columns)
    ratio_ref[...] = ratio.astype(BF16).reshape(blocks + 2, size, width)
    for b in range(blocks):
        window = ratio_ref[b : b + 3].reshape(3 * size, width)
        product_ref[b] = product_ref[b] * dot(backward_ref[0], window)

    @pl.when(step == slots - 1)
    def _():
        for b in range(blocks):
            logs = jnp.log(product_ref[b]) * (1.0 / views)
            out_ref[:, b * ROWS : (b + 1) * ROWS] = logs.reshape(depth, ROWS, width)


def whole(shape):
    return pl.BlockSpec(shape, lambda *_: (0,) * len(shape))


def cost(flops, moved):
    return pl.CostEstimate(flops=int(flops), bytes_accessed=int(moved), transcendentals=0)


def turn(payload):
    return lax.all_to_all(payload, "gz", split_axis=0, concat_axis=0, tiled=True)


def edges(field):
    extent = field.shape[1]
    low = [field[:, at : at + ROWS] for at in (0, ROWS)]
    high = [field[:, at : at + ROWS] for at in (extent - 2 * ROWS, extent - ROWS)]
    return jnp.stack(low), jnp.stack(high)


def send_rims(low, high):
    count = lax.axis_size("gz")
    below = lax.ppermute(high, "gz", [(i, i + 1) for i in range(count - 1)])
    above = lax.ppermute(low, "gz", [(i + 1, i) for i in range(count - 1)])
    return below, above


def swap_cores(field):
    count = lax.axis_size("view")
    return lax.ppermute(field, "view", [(i, (i + 1) % count) for i in range(count)])


def on_device(observed, initial, psf_taps, view_shifts, view_map):
    slots, depth, rows, width = observed.shape
    views = view_map.shape[0]
    groups = lax.axis_size("gz")
    length = groups * rows
    local_depth = depth // groups
    half = width // 2
    size = depth * ROWS
    blocks = rows // ROWS
    core = lax.axis_index("view")
    group = lax.axis_index("gz")
    ref_slot = jnp.sum(jnp.where(view_map == 0, jnp.arange(views, dtype=jnp.int32), 0)).astype(jnp.int32)
    holds_ref = (ref_slot // slots == core).astype(jnp.int32)
    order = (ref_slot % slots).reshape(1)
    place = jnp.stack([holds_ref, group]).astype(jnp.int32)
    core_at = core.astype(jnp.int32).reshape(1)

    columns_forward, columns_inverse = column_tables(width, depth)
    row_turn = row_table(length)

    low, high = edges(initial.astype(BF16))
    low = jnp.concatenate([observed[:, :, :ROWS], low], 0)
    high = jnp.concatenate([observed[:, :, rows - ROWS :], high], 0)
    first_rims = send_rims(low, high)

    chunk = slots // 2
    payload_block = (groups, 1, local_depth, rows, width)
    payload_shape = (groups, chunk, local_depth, rows, width)
    payload_bytes = 4 * depth * rows * width * chunk
    volume = depth * rows * width

    def first(start):
        return pl.pallas_call(
            first_kernel,
            grid_spec=pltpu.PrefetchScalarGridSpec(
                num_scalar_prefetch=1,
                grid=(chunk,),
                in_specs=[
                    pl.BlockSpec((1, depth, rows, width), lambda s, o: (lax.rem(s + start + o[0], slots), 0, 0, 0)),
                    whole(columns_forward.shape),
                ],
                out_specs=pl.BlockSpec(payload_block, lambda s, o: (0, s, 0, 0, 0)),
                scratch_shapes=[pltpu.VMEM((depth, rows, width), F32)] * 2,
            ),
            out_shape=jax.ShapeDtypeStruct(payload_shape, jnp.int16),
            cost_estimate=cost(2 * chunk * volume * 8 * width, payload_bytes),
            name="first",
        )(order, observed, columns_forward)

    planes = local_depth + 1
    spectrum_shape = (planes, length, width)
    row_flops = 2 * planes * length * width * 6 * length

    def reference_spectrum(payload):
        return pl.pallas_call(
            spectrum_kernel,
            grid_spec=pltpu.PrefetchScalarGridSpec(
                num_scalar_prefetch=1,
                grid=(1,),
                in_specs=[
                    pl.BlockSpec(payload_block, lambda s, o: (0, 0, 0, 0, 0)),
                    whole(row_turn.shape),
                ],
                out_specs=whole(spectrum_shape),
            ),
            out_shape=jax.ShapeDtypeStruct(spectrum_shape, F32),
            cost_estimate=cost(row_flops, 8 * volume),
            name="spectrum",
        )(place, payload, row_turn)

    def crossed(payload, mine, other):
        return pl.pallas_call(
            cross_kernel,
            grid_spec=pltpu.PrefetchScalarGridSpec(
                num_scalar_prefetch=1,
                grid=(chunk,),
                in_specs=[
                    pl.BlockSpec(payload_block, lambda s, o: (0, s, 0, 0, 0)),
                    whole(row_turn.shape),
                    whole(spectrum_shape),
                    whole(spectrum_shape),
                ],
                out_specs=pl.BlockSpec(payload_block, lambda s, o: (0, s, 0, 0, 0)),
            ),
            out_shape=jax.ShapeDtypeStruct(payload_shape, jnp.int16),
            cost_estimate=cost(2 * row_flops * chunk, payload_bytes * 2 + 10 * volume),
            name="cross",
        )(place, payload, row_turn, mine, other)

    def last(payload, start, partial):
        specs = [
            pl.BlockSpec(payload_block, lambda s, o: (0, s, 0, 0, 0)),
            whole(columns_inverse.shape),
        ]
        operands = [order, payload, columns_inverse]
        aliases = {}
        if partial is not None:
            specs.append(pl.BlockSpec(memory_space=pl.ANY))
            aliases = {len(operands): 0}
            operands.append(partial)
        return pl.pallas_call(
            last_kernel,
            grid_spec=pltpu.PrefetchScalarGridSpec(
                num_scalar_prefetch=1,
                grid=(chunk,),
                in_specs=specs,
                out_specs=pl.BlockSpec((1, depth, rows, width), lambda s, o: (lax.rem(s + start + o[0], slots), 0, 0, 0)),
                scratch_shapes=[pltpu.VMEM((depth, rows, width), F32)] * 2,
            ),
            out_shape=jax.ShapeDtypeStruct((slots, depth, rows, width), F32),
            input_output_aliases=aliases,
            cost_estimate=cost(2 * chunk * volume * 9 * width, payload_bytes * 1.5),
            name="last",
        )(*operands)

    def filters():
        smem = pl.BlockSpec(memory_space=pltpu.SMEM)
        return pl.pallas_call(
            filter_kernel,
            grid=(slots,),
            in_specs=[smem] * 4,
            out_specs=[
                pl.BlockSpec((1, size, 3 * size), lambda s: (s, 0, 0)),
                pl.BlockSpec((1, size, 3 * size), lambda s: (s, 0, 0)),
                pl.BlockSpec((1, width, width), lambda s: (s, 0, 0)),
            ],
            out_shape=[
                jax.ShapeDtypeStruct((slots, size, 3 * size), BF16),
                jax.ShapeDtypeStruct((slots, size, 3 * size), BF16),
                jax.ShapeDtypeStruct((slots, width, width), BF16),
            ],
            cost_estimate=cost(slots * size * size * 60, slots * size * size * 14),
            name="filters",
        )(core_at, view_map, view_shifts.reshape(-1), psf_taps.reshape(-1))

    forward, backward, columns = filters()

    def join(estimate, below, above):
        def slot_block(shape):
            return pl.BlockSpec((1,) + shape, lambda s: (s,) + (0,) * len(shape))

        def rim_block(rim):
            at = rim.shape[0] // 2 - 1
            return pl.BlockSpec((2, depth, ROWS, width), lambda s: (at, 0, 0, 0))

        return pl.pallas_call(
            functools.partial(join_kernel, views),
            grid=(slots,),
            in_specs=[
                whole((depth, rows, width)),
                rim_block(below),
                rim_block(above),
                slot_block((depth, rows, width)),
                slot_block((depth, ROWS, width)),
                slot_block((depth, ROWS, width)),
                whole((slots, size, 3 * size)),
                slot_block((size, 3 * size)),
                slot_block((width, width)),
            ],
            out_specs=whole((depth, rows, width)),
            out_shape=jax.ShapeDtypeStruct((depth, rows, width), F32),
            scratch_shapes=[
                pltpu.VMEM((blocks + 4, size, width), BF16),
                pltpu.VMEM((slots, blocks + 2, size, width), BF16),
                pltpu.VMEM((blocks + 2, size, width), F32),
                pltpu.VMEM((blocks + 2, size, width), BF16),
                pltpu.VMEM((blocks, size, width), F32),
            ],
            cost_estimate=cost(2 * slots * size * width * ((blocks + 2) * (3 * size + 2 * width) + blocks * 3 * size), 12e6),
            name="join",
        )(estimate, below, above, observed, *first_rims, forward, backward, columns)

    sent_a = turn(first(0))
    sent_b = turn(first(chunk))

    estimate = initial
    for iteration in range(ITERS):
        rims = send_rims(*edges(estimate.astype(BF16))) if iteration else first_rims
        logs = join(estimate, *rims)
        estimate = estimate * jnp.exp(logs + swap_cores(logs))

    mine = reference_spectrum(sent_a)
    other = swap_cores(mine)
    back_a = turn(crossed(sent_a, mine, other))
    back_b = turn(crossed(sent_b, mine, other))
    surfaces = last(back_a, 0, None)
    surfaces = last(back_b, chunk, surfaces)
    return estimate, surfaces


def solution(mesh):
    placed = (P("view", "parts", "gz", None), P("parts", "gz", None), P(), P(), P())
    return jax.shard_map(
        on_device,
        mesh=mesh,
        in_specs=placed,
        out_specs=(P("parts", "gz", None), P("view", "parts", "gz", None)),
        check_vma=False,
    )
```

```python
import functools
import math

import jax
import jax.numpy as jnp
import ml_dtypes
import numpy as np
from jax import lax
from jax.experimental import pallas as pl
from jax.experimental.pallas import tpu as pltpu
from jax.sharding import PartitionSpec as P

ITERS = 2
TAPS = 15
HALF = TAPS // 2
ROWS = 8
MID = 1.099609375


F32 = jnp.float32
BF16 = jnp.bfloat16


def dot(a, b):
    return jnp.dot(a, b, preferred_element_type=F32)


def dot_t(a, b):
    return lax.dot_general(a, b, (((1,), (1,)), ((), ())), preferred_element_type=F32)


def split(value):
    high = value.astype(BF16)
    return high, (value - high.astype(F32)).astype(BF16)


def np_split(table):
    high = table.astype(ml_dtypes.bfloat16)
    low = (table - high.astype(np.float64)).astype(ml_dtypes.bfloat16)
    return high, low


def side_by_side(table):
    return jnp.asarray(np.concatenate(np_split(table), 1))


def depth_order(depth):
    order = [0, depth // 2]
    for m in range(1, depth // 2):
        order += [m, depth - m]
    return np.array(order)


def angle_table(rows, columns, length):
    return 2.0 * np.pi * ((rows[:, None] * columns[None, :]) % length) / length


def depth_transform(real, imag, orient):
    count = len(real)
    if count == 1:
        return real, imag
    if count == 2:
        return [real[0] + real[1], real[0] - real[1]], [imag[0] + imag[1], imag[0] - imag[1]]
    quarter = count // 4
    parts = [depth_transform(real[j::4], imag[j::4], orient) for j in range(4)]
    out_real, out_imag = [None] * count, [None] * count
    for k in range(quarter):
        turned_parts = []
        for j in range(4):
            part_real, part_imag = parts[j][0][k], parts[j][1][k]
            if j * k:
                angle = -orient * 2.0 * math.pi * j * k / count
                cos, sin = math.cos(angle), math.sin(angle)
                if 8 * j * k == count:
                    part_real, part_imag = (part_real + orient * part_imag) * cos, (part_imag - orient * part_real) * cos
                else:
                    part_real, part_imag = part_real * cos - part_imag * sin, part_real * sin + part_imag * cos
            turned_parts.append((part_real, part_imag))
        (ar, ai), (br, bi), (cr, ci), (dr, di) = turned_parts
        sum_ac, dif_ac = (ar + cr, ai + ci), (ar - cr, ai - ci)
        sum_bd, dif_bd = (br + dr, bi + di), (br - dr, bi - di)
        out_real[k], out_imag[k] = sum_ac[0] + sum_bd[0], sum_ac[1] + sum_bd[1]
        out_real[k + 2 * quarter], out_imag[k + 2 * quarter] = sum_ac[0] - sum_bd[0], sum_ac[1] - sum_bd[1]
        plus = (dif_ac[0] + dif_bd[1], dif_ac[1] - dif_bd[0])
        minus = (dif_ac[0] - dif_bd[1], dif_ac[1] + dif_bd[0])
        first_part, second_part = (plus, minus) if orient > 0 else (minus, plus)
        out_real[k + quarter], out_imag[k + quarter] = first_part
        out_real[k + 3 * quarter], out_imag[k + 3 * quarter] = second_part
    return out_real, out_imag


def forward_bound(depth, width):
    return 0.9005 * math.sqrt(depth * width)


def backward_bound(length):
    return 2.001 * math.sqrt(length)


def encode(value, bound):
    scaled = value * lax.rsqrt(jnp.abs(value) + 1e-30) * (32767.0 / math.sqrt(bound))
    return (scaled + jnp.where(value < 0.0, -0.5, 0.5)).astype(jnp.int32).astype(jnp.int16)


def decode(code, bound):
    value = code.astype(jnp.int32).astype(F32)
    return value * jnp.abs(value) * (bound / 32767.0**2)


def row_tables(length):
    half = length // 2
    positions = np.arange(length)
    freqs = np.arange(half)
    angles = angle_table(positions, freqs, length)
    cos_part, sin_part = np.cos(angles), np.sin(angles)
    sin_part[:, 0] = 1.0 - 2.0 * (positions % 2)
    both = np.concatenate([cos_part, sin_part], 1) / math.sqrt(length)
    return side_by_side(both.T), side_by_side(both)


def column_tables(width, depth):
    half = width // 2
    positions = np.arange(width)
    freqs = np.arange(half)
    angles = angle_table(positions, freqs, width)
    scale = 1.0 / math.sqrt(width * depth)
    cos_part = np.cos(angles)
    sin_part = -np.sin(angles)
    sin_part[:, 0] = 1.0 - 2.0 * (positions % 2)
    forward = np.concatenate([cos_part, sin_part], 1) * scale
    weights = np.where(freqs == 0, 1.0, 2.0)
    inverse = np.concatenate([cos_part * weights, sin_part * weights], 1).T * scale
    return side_by_side(forward), side_by_side(inverse)


def table_times(table, block):
    size = block.shape[0]
    high, low = split(block)
    return dot(table, jnp.concatenate([high, high], 0)) + dot(table[:, :size], low)


def replace_row(array, row):
    top = array[:ROWS]
    row_id = lax.broadcasted_iota(jnp.int32, top.shape, 0)
    return jnp.concatenate([jnp.where(row_id == 0, row[:1], top), array[ROWS:]], 0)


def rows_forward(table, plane):
    both = table_times(table, plane)
    count = both.shape[0] // 2
    half = both.shape[1] // 2
    cos_real, cos_imag = both[:count, :half], both[:count, half:]
    sin_real, sin_imag = both[count:, :half], both[count:, half:]
    above = (replace_row(cos_real + sin_imag, cos_real), replace_row(cos_imag - sin_real, cos_imag))
    below = (replace_row(cos_real - sin_imag, sin_real), replace_row(cos_imag + sin_real, sin_imag))
    return above, below


def rows_inverse(table, above, below):
    even_real = replace_row(above[0] + below[0], above[0])
    even_imag = replace_row(above[1] + below[1], above[1])
    odd_real = replace_row(below[1] - above[1], below[0])
    odd_imag = replace_row(above[0] - below[0], below[1])
    top = jnp.concatenate([even_real, even_imag], 1)
    bottom = jnp.concatenate([odd_real, odd_imag], 1)
    return table_times(table, jnp.concatenate([top, bottom], 0))


def ref_slot_of(map_ref):
    slot = jnp.int32(0)
    for at in range(1, map_ref.shape[0]):
        slot = jnp.where(map_ref[at] == 0, jnp.int32(at), slot)
    return slot


def first_kernel(map_ref, observed_ref, columns_ref, out_ref, spread_ref, turned_ref):
    depth, rows, width = observed_ref.shape[1:]
    half = width // 2
    groups, _, local_depth = out_ref.shape[:3]
    flat = observed_ref[0].reshape(depth * rows, width)
    table = columns_ref[...]
    spread = dot(flat, table[:, :width]) + dot(flat, table[:, width:])
    spread_ref[...] = spread.reshape(depth, rows, width)
    shift = MID * math.sqrt(width * depth)
    spots = depth_order(depth)
    lane = lax.broadcasted_iota(jnp.int32, (ROWS, half), 1)

    @pl.loop(0, rows // ROWS)
    def _(b):
        at = pl.ds(pl.multiple_of(b * ROWS, ROWS), ROWS)
        real = [spread_ref[z, at, :half] for z in range(depth)]
        imag = [spread_ref[z, at, half:] for z in range(depth)]
        real, imag = depth_transform(real, imag, 1)
        real[0] = jnp.where(lane == 0, real[0] - shift, real[0])
        for spot, k in enumerate(spots):
            turned_ref[spot, at, :half] = real[k]
            turned_ref[spot, at, half:] = imag[k]

    code = encode(turned_ref[...], forward_bound(depth, width))
    out_ref[:, 0] = code.reshape(groups, local_depth, rows, width)


def load_planes(in_ref, group_zero):
    groups, _, local_depth, rows, width = in_ref.shape
    half = width // 2
    length = groups * rows
    bound = forward_bound(groups * local_depth, width)
    raw = [decode(in_ref[:, 0, k].reshape(length, width), bound) for k in range(local_depth)]
    lane = lax.broadcasted_iota(jnp.int32, (length, width), 1)
    edge = (lane == 0) | (lane == half)
    sign = jnp.where(lane == half, -1.0, 1.0)
    top_lane = lax.broadcasted_iota(jnp.int32, (length, half), 1)
    top_real = jnp.zeros((length, half), F32)
    top_imag = jnp.zeros((length, half), F32)
    planes = []
    for k in range(local_depth):
        partner = raw[k ^ 1]
        if k < 2:
            partner = jnp.where(group_zero, raw[k], partner)
        planes.append(jnp.where(edge, 0.5 * (raw[k] + sign * partner), raw[k]))
        real_col = 0.5 * (raw[k][:, half : half + 1] + partner[:, half : half + 1])
        imag_col = -0.5 * (raw[k][:, :1] - partner[:, :1])
        top_real = jnp.where(top_lane == k, real_col, top_real)
        top_imag = jnp.where(top_lane == k, imag_col, top_imag)
    planes.append(jnp.concatenate([top_real, top_imag], 1))
    return planes


def spectrum(table, plane, is_first, group_zero, depth):
    above, below = rows_forward(table, plane)
    if is_first:
        shift = MID * math.sqrt(depth * plane.shape[0] * plane.shape[1])
        lane = lax.broadcasted_iota(jnp.int32, above[0].shape, 1)
        here = (lane[:1] == 0) & group_zero
        row = jnp.where(here, above[0][:1] + shift, above[0][:1])
        above = (replace_row(above[0], row), above[1])
    return above, below


def spectrum_kernel(map_ref, place_ref, in_ref, rows_ref, logs_ref, out_ref):
    group_zero = place_ref[1] == 0
    groups, _, local_depth, rows, width = in_ref.shape
    depth = groups * local_depth
    half = width // 2
    table = rows_ref[...]
    planes = load_planes(in_ref, group_zero)
    for k, plane in enumerate(planes):
        above, below = spectrum(table, plane, k == 0, group_zero, depth)
        count = above[0].shape[0]
        out_ref[k, :count, :half] = above[0]
        out_ref[k, :count, half:] = above[1]
        out_ref[k, count:, :half] = below[0]
        out_ref[k, count:, half:] = below[1]
    size = out_ref.shape[1]
    logs = logs_ref[...].reshape(-1, size, width)
    out_ref[len(planes) :] = logs


def cross_of(value, ref):
    real, imag = value
    ref_real, ref_imag = ref
    power = (real * real + imag * imag) * (ref_real * ref_real + ref_imag * ref_imag)
    scale = 1.0 / (jnp.sqrt(power) + 1.0)
    return (real * ref_real + imag * ref_imag) * scale, (imag * ref_real - real * ref_imag) * scale


def cross_kernel(map_ref, place_ref, in_ref, rows_ref, back_ref, mine_ref, other_ref, out_ref):
    groups, _, local_depth, rows, width = in_ref.shape
    slots = map_ref.shape[0] // 2
    holds_ref = ref_slot_of(map_ref) // slots == place_ref[0]
    group_zero = place_ref[1] == 0
    depth = groups * local_depth
    half = width // 2
    length = groups * rows
    bound = backward_bound(length)
    table = rows_ref[...]
    back = []
    for k, plane in enumerate(load_planes(in_ref, group_zero)):
        above, below = spectrum(table, plane, k == 0, group_zero, depth)
        ref = jnp.where(holds_ref, mine_ref[k], other_ref[k])
        count = length // 2
        above = cross_of(above, (ref[:count, :half], ref[:count, half:]))
        below = cross_of(below, (ref[count:, :half], ref[count:, half:]))
        back.append(rows_inverse(back_ref[...], above, below))
    top = back[local_depth]
    lane = lax.broadcasted_iota(jnp.int32, (length, half), 1)
    for k in range(local_depth):
        real, imag = back[k][:, :half], back[k][:, half:]
        real = jnp.where(lane == 0, real - top[:, half + k : half + k + 1], real)
        imag = jnp.where(lane == 0, imag + top[:, k : k + 1], imag)
        out_ref[:, 0, k, :, :half] = encode(real, bound).reshape(groups, rows, half)
        out_ref[:, 0, k, :, half:] = encode(imag, bound).reshape(groups, rows, half)


def last_kernel(map_ref, in_ref, columns_ref, *rest):
    out_ref, turned_ref, spread_ref = rest[-3:]
    groups, _, local_depth, rows, width = in_ref.shape
    depth = groups * local_depth
    half = width // 2
    table = columns_ref[...]
    spots = depth_order(depth)
    value = decode(in_ref[:, 0], backward_bound(groups * rows))
    turned_ref[...] = value.reshape(depth, rows, width)

    @pl.loop(0, rows // ROWS)
    def _(b):
        at = pl.ds(pl.multiple_of(b * ROWS, ROWS), ROWS)
        real, imag = [None] * depth, [None] * depth
        for spot, k in enumerate(spots):
            real[k] = turned_ref[spot, at, :half]
            imag[k] = turned_ref[spot, at, half:]
        real, imag = depth_transform(real, imag, -1)
        for z in range(depth):
            spread_ref[z, at, :half] = real[z]
            spread_ref[z, at, half:] = imag[z]

    high, low = split(spread_ref[...].reshape(depth * rows, width))
    cells = dot(high, table[:, :width]) + dot(high, table[:, width:]) + dot(low, table[:, :width])
    out_ref[0] = cells.reshape(depth, rows, width)


def pick_tap(psf_ref, view, axis, index):
    value = jnp.zeros(index.shape, F32)
    for j in range(TAPS):
        value = jnp.where(index == j, psf_ref[view, axis, j], value)
    return value


def filter_kernel(place_ref, map_ref, shift_ref, psf_ref, forward_ref, backward_ref, columns_ref):
    slots = forward_ref.shape[0]
    size = forward_ref.shape[1]
    width = columns_ref.shape[1]
    depth = size // ROWS
    view = map_ref[place_ref[0] * pl.num_programs(0) + pl.program_id(0)]
    depth_shift = shift_ref[view, 0]
    column_shift = shift_ref[view, 1]
    at_out = lax.broadcasted_iota(jnp.int32, (depth, size), 0)
    at_in = lax.broadcasted_iota(jnp.int32, (depth, size), 1) // ROWS
    row = lax.broadcasted_iota(jnp.int32, (ROWS, size), 0)
    cell = lax.broadcasted_iota(jnp.int32, (ROWS, size), 1) % ROWS
    for out_ref, orient in ((forward_ref, 1), (backward_ref, -1)):
        depth_part = pick_tap(psf_ref, view, 0, orient * (at_in - at_out) + HALF - depth_shift)
        for c in range(3):
            reach = c * ROWS + cell - ROWS - row
            row_part = pick_tap(psf_ref, view, 1, orient * reach + HALF)
            block = depth_part[:, None, :] * row_part[None, :, :]
            out_ref[0, :, c * size : (c + 1) * size] = block.reshape(size, size).astype(BF16)
    source = lax.broadcasted_iota(jnp.int32, (width, width), 0)
    target = lax.broadcasted_iota(jnp.int32, (width, width), 1)
    picked = pick_tap(psf_ref, view, 2, source - target + HALF - column_shift)
    columns_ref[0] = picked.astype(BF16)


def join_kernel(
    views,
    updated,
    *refs,
):
    if updated:
        mine_ref, other_ref, *refs = refs
    (
    estimate_ref,
    below_ref,
    above_ref,
    observed_ref,
    seen_below_ref,
    seen_above_ref,
    forward_ref,
    backward_ref,
    columns_ref,
    out_ref,
    *refs,
    ) = refs
    if updated:
        now_ref, *refs = refs
    else:
        now_ref = estimate_ref
    cells_ref, mixed_ref, blurred_ref, ratio_ref, product_ref = refs
    depth, rows, width = estimate_ref.shape
    size = depth * ROWS
    blocks = rows // ROWS
    slots = forward_ref.shape[0]
    step = pl.program_id(0)

    @pl.when(step == 0)
    def _():
        if updated:
            logs = mine_ref[...] + other_ref[...]
            now_ref[...] = estimate_ref[...] * jnp.exp(logs.reshape(depth, rows, width))
        for rim_ref, start in ((below_ref, 0), (above_ref, blocks + 2)):
            for b in range(2):
                piece = rim_ref[b].astype(F32).reshape(size, width)
                cells_ref[start + b] = piece.astype(BF16)
        for b in range(blocks):
            piece = now_ref[:, b * ROWS : (b + 1) * ROWS].reshape(size, width)
            cells_ref[b + 2] = piece.astype(BF16)
        product_ref[...] = jnp.ones_like(product_ref)

        @pl.loop(0, blocks + 2)
        def _(b):
            window = cells_ref[pl.ds(b, 3)].reshape(3 * size, width)
            mixed = dot(forward_ref[...].reshape(slots * size, 3 * size), window)
            mixed_ref[:, b] = mixed.astype(BF16).reshape(slots, size, width)

    columns = columns_ref[0]
    blurred = dot(mixed_ref[step].reshape((blocks + 2) * size, width), columns)
    blurred_ref[...] = blurred.reshape(blocks + 2, size, width)
    for b in range(blocks + 2):
        if b == 0:
            seen = seen_below_ref[0].astype(F32)
        elif b == blocks + 1:
            seen = seen_above_ref[0].astype(F32)
        else:
            seen = observed_ref[0, :, (b - 1) * ROWS : b * ROWS].astype(F32)
        seen = seen.reshape(size, width)
        ratio = jnp.where(seen > 0.0, seen / blurred_ref[b], 0.0)
        ratio_ref[b] = ratio.astype(BF16)
    ratio = dot_t(ratio_ref[...].reshape((blocks + 2) * size, width), columns)
    ratio_ref[...] = ratio.astype(BF16).reshape(blocks + 2, size, width)
    for b in range(blocks):
        window = ratio_ref[b : b + 3].reshape(3 * size, width)
        product_ref[b] = product_ref[b] * dot(backward_ref[0], window)

    @pl.when(step == slots - 1)
    def _():
        for b in range(blocks):
            logs = jnp.log(product_ref[b]) * (1.0 / views)
            out_ref[:, b * ROWS : (b + 1) * ROWS] = logs.reshape(depth, ROWS, width)


def whole(shape):
    return pl.BlockSpec(shape, lambda *_: (0,) * len(shape))


def cost(flops, moved):
    return pl.CostEstimate(flops=int(flops), bytes_accessed=int(moved), transcendentals=0)


def turn(payload):
    return lax.all_to_all(payload, "gz", split_axis=0, concat_axis=0, tiled=True)


def edges(field):
    extent = field.shape[1]
    low = [field[:, at : at + ROWS] for at in (0, ROWS)]
    high = [field[:, at : at + ROWS] for at in (extent - 2 * ROWS, extent - ROWS)]
    return jnp.stack(low), jnp.stack(high)


def send_rims(low, high):
    count = lax.axis_size("gz")
    below = lax.ppermute(high, "gz", [(i, i + 1) for i in range(count - 1)])
    above = lax.ppermute(low, "gz", [(i + 1, i) for i in range(count - 1)])
    return below, above


def swap_cores(field):
    count = lax.axis_size("view")
    return lax.ppermute(field, "view", [(i, (i + 1) % count) for i in range(count)])


def on_device(observed, initial, psf_taps, view_shifts, view_map):
    slots, depth, rows, width = observed.shape
    views = view_map.shape[0]
    groups = lax.axis_size("gz")
    length = groups * rows
    local_depth = depth // groups
    half = width // 2
    size = depth * ROWS
    blocks = rows // ROWS
    place = jnp.stack([lax.axis_index("view"), lax.axis_index("gz")]).astype(jnp.int32)

    columns_forward, columns_inverse = column_tables(width, depth)
    row_turn, row_back = row_tables(length)

    low, high = edges(initial.astype(BF16))
    low = jnp.concatenate([observed[:, :, :ROWS], low], 0)
    high = jnp.concatenate([observed[:, :, rows - ROWS :], high], 0)
    first_rims = send_rims(low, high)

    chunk = slots // 2
    payload_block = (groups, 1, local_depth, rows, width)
    payload_shape = (groups, chunk, local_depth, rows, width)
    payload_bytes = 4 * depth * rows * width * chunk
    volume = depth * rows * width

    def first(start):
        return pl.pallas_call(
            first_kernel,
            grid_spec=pltpu.PrefetchScalarGridSpec(
                num_scalar_prefetch=1,
                grid=(chunk,),
                in_specs=[
                    pl.BlockSpec((1, depth, rows, width), lambda s, m: (lax.rem(s + start + ref_slot_of(m), slots), 0, 0, 0)),
                    whole(columns_forward.shape),
                ],
                out_specs=pl.BlockSpec(payload_block, lambda *a: (0, a[0], 0, 0, 0)),
                scratch_shapes=[pltpu.VMEM((depth, rows, width), F32)] * 2,
            ),
            out_shape=jax.ShapeDtypeStruct(payload_shape, jnp.int16),
            cost_estimate=cost(2 * chunk * volume * 8 * width, payload_bytes),
            name="first",
        )(view_map, observed, columns_forward)

    planes = local_depth + 1
    spectrum_shape = (planes, length, width)
    row_flops = 2 * planes * length * width * 3 * length
    volume_planes = volume // (length * width)

    def reference_spectrum(payload, logs):
        return pl.pallas_call(
            spectrum_kernel,
            grid_spec=pltpu.PrefetchScalarGridSpec(
                num_scalar_prefetch=2,
                grid=(1,),
                in_specs=[
                    pl.BlockSpec(payload_block, lambda *_: (0, 0, 0, 0, 0)),
                    whole(row_turn.shape),
                    whole(logs.shape),
                ],
                out_specs=whole((planes + volume_planes, length, width)),
            ),
            out_shape=jax.ShapeDtypeStruct((planes + volume_planes, length, width), F32),
            cost_estimate=cost(row_flops, 16 * volume),
            name="spectrum",
        )(view_map, place, payload, row_turn, logs)

    def crossed(payload, mine, other):
        return pl.pallas_call(
            cross_kernel,
            grid_spec=pltpu.PrefetchScalarGridSpec(
                num_scalar_prefetch=2,
                grid=(chunk,),
                in_specs=[
                    pl.BlockSpec(payload_block, lambda *a: (0, a[0], 0, 0, 0)),
                    whole(row_turn.shape),
                    whole(row_back.shape),
                    whole(spectrum_shape),
                    whole(spectrum_shape),
                ],
                out_specs=pl.BlockSpec(payload_block, lambda *a: (0, a[0], 0, 0, 0)),
            ),
            out_shape=jax.ShapeDtypeStruct(payload_shape, jnp.int16),
            cost_estimate=cost(2 * row_flops * chunk, payload_bytes + 10 * volume),
            name="cross",
        )(view_map, place, payload, row_turn, row_back, mine, other)

    def last(payload, start, partial):
        specs = [
            pl.BlockSpec(payload_block, lambda *a: (0, a[0], 0, 0, 0)),
            whole(columns_inverse.shape),
        ]
        operands = [view_map, payload, columns_inverse]
        aliases = {}
        if partial is not None:
            specs.append(pl.BlockSpec(memory_space=pl.ANY))
            aliases = {len(operands): 0}
            operands.append(partial)
        return pl.pallas_call(
            last_kernel,
            grid_spec=pltpu.PrefetchScalarGridSpec(
                num_scalar_prefetch=1,
                grid=(chunk,),
                in_specs=specs,
                out_specs=pl.BlockSpec((1, depth, rows, width), lambda s, m: (lax.rem(s + start + ref_slot_of(m), slots), 0, 0, 0)),
                scratch_shapes=[pltpu.VMEM((depth, rows, width), F32)] * 2,
            ),
            out_shape=jax.ShapeDtypeStruct((slots, depth, rows, width), F32),
            input_output_aliases=aliases,
            cost_estimate=cost(2 * chunk * volume * 9 * width, payload_bytes * 1.5),
            name="last",
        )(*operands)

    def filters():
        smem = pl.BlockSpec(memory_space=pltpu.SMEM)
        return pl.pallas_call(
            filter_kernel,
            grid=(slots,),
            in_specs=[smem] * 4,
            out_specs=[
                pl.BlockSpec((1, size, 3 * size), lambda s: (s, 0, 0)),
                pl.BlockSpec((1, size, 3 * size), lambda s: (s, 0, 0)),
                pl.BlockSpec((1, width, width), lambda s: (s, 0, 0)),
            ],
            out_shape=[
                jax.ShapeDtypeStruct((slots, size, 3 * size), BF16),
                jax.ShapeDtypeStruct((slots, size, 3 * size), BF16),
                jax.ShapeDtypeStruct((slots, width, width), BF16),
            ],
            cost_estimate=cost(slots * size * size * 60, slots * size * size * 14),
            name="filters",
        )(place, view_map, view_shifts, psf_taps)

    forward, backward, columns = filters()

    def join(estimate, below, above, logs=None):
        def slot_block(shape):
            return pl.BlockSpec((1,) + shape, lambda s: (s,) + (0,) * len(shape))

        def rim_block(rim):
            at = rim.shape[0] // 2 - 1
            return pl.BlockSpec((2, depth, ROWS, width), lambda s: (at, 0, 0, 0))

        updated = logs is not None
        field = jax.ShapeDtypeStruct((depth, rows, width), F32)
        extra_specs = []
        if updated:
            extra_specs = [whole((volume_planes, length, width))] * 2
        return pl.pallas_call(
            functools.partial(join_kernel, views, updated),
            grid=(slots,),
            in_specs=extra_specs
            + [
                whole((depth, rows, width)),
                rim_block(below),
                rim_block(above),
                slot_block((depth, rows, width)),
                slot_block((depth, ROWS, width)),
                slot_block((depth, ROWS, width)),
                whole((slots, size, 3 * size)),
                slot_block((size, 3 * size)),
                slot_block((width, width)),
            ],
            out_specs=[whole((depth, rows, width))] * (1 + updated),
            out_shape=[field] * (1 + updated),
            scratch_shapes=[
                pltpu.VMEM((blocks + 4, size, width), BF16),
                pltpu.VMEM((slots, blocks + 2, size, width), BF16),
                pltpu.VMEM((blocks + 2, size, width), F32),
                pltpu.VMEM((blocks + 2, size, width), BF16),
                pltpu.VMEM((blocks, size, width), F32),
            ],
            cost_estimate=cost(2 * slots * size * width * ((blocks + 2) * (3 * size + 2 * width) + blocks * 3 * size), 12e6),
            name="join",
        )(*(logs or ()), estimate, below, above, observed, *first_rims, forward, backward, columns)

    sent_a = turn(first(0))
    payload_b, start = lax.optimization_barrier((first(chunk), initial))
    sent_b = turn(payload_b)
    (logs,) = join(start, *first_rims)

    mine = reference_spectrum(sent_a, logs)
    other = swap_cores(mine)
    back_a = turn(crossed(sent_a, mine, other))

    total = (mine[planes:], other[planes:])
    estimate = initial * jnp.exp((total[0] + total[1]).reshape(depth, rows, width))
    rims = send_rims(*edges(estimate.astype(BF16)))
    logs, estimate = join(initial, *rims, logs=total)
    estimate = estimate * jnp.exp(logs + swap_cores(logs))

    back_b = turn(crossed(sent_b, mine, other))
    surfaces = last(back_a, 0, None)
    surfaces = last(back_b, chunk, surfaces)
    return estimate, surfaces


def solution(mesh):
    placed = (P("view", "parts", "gz", None), P("parts", "gz", None), P(), P(), P())
    return jax.shard_map(
        on_device,
        mesh=mesh,
        in_specs=placed,
        out_specs=(P("parts", "gz", None), P("view", "parts", "gz", None)),
        check_vma=False,
    )
```

```python
import functools
import math

import jax
import jax.numpy as jnp
import ml_dtypes
import numpy as np
from jax import lax
from jax.experimental import pallas as pl
from jax.experimental.pallas import tpu as pltpu
from jax.sharding import PartitionSpec as P


TAPS = 15
HALF = TAPS // 2
ROWS = 8
MID = 1.099609375


F32 = jnp.float32
BF16 = jnp.bfloat16


def dot(a, b):
    return jnp.dot(a, b, preferred_element_type=F32)


def dot_t(a, b):
    return lax.dot_general(a, b, (((1,), (1,)), ((), ())), preferred_element_type=F32)


def split(value):
    high = value.astype(BF16)
    return high, (value - high.astype(F32)).astype(BF16)


def np_split(table):
    high = table.astype(ml_dtypes.bfloat16)
    low = (table - high.astype(np.float64)).astype(ml_dtypes.bfloat16)
    return high, low


def side_by_side(table):
    return jnp.asarray(np.concatenate(np_split(table), 1))


def depth_order(depth):
    order = [0, depth // 2]
    for m in range(1, depth // 2):
        order += [m, depth - m]
    return np.array(order)


def angle_table(rows, columns, length):
    return 2.0 * np.pi * ((rows[:, None] * columns[None, :]) % length) / length


def depth_transform(real, imag, orient):
    count = len(real)
    if count == 1:
        return real, imag
    if count == 2:
        return [real[0] + real[1], real[0] - real[1]], [imag[0] + imag[1], imag[0] - imag[1]]
    quarter = count // 4
    parts = [depth_transform(real[j::4], imag[j::4], orient) for j in range(4)]
    out_real, out_imag = [None] * count, [None] * count
    for k in range(quarter):
        turned_parts = []
        for j in range(4):
            part_real, part_imag = parts[j][0][k], parts[j][1][k]
            if j * k:
                angle = -orient * 2.0 * math.pi * j * k / count
                cos, sin = math.cos(angle), math.sin(angle)
                if 8 * j * k == count:
                    part_real, part_imag = (part_real + orient * part_imag) * cos, (part_imag - orient * part_real) * cos
                else:
                    part_real, part_imag = part_real * cos - part_imag * sin, part_real * sin + part_imag * cos
            turned_parts.append((part_real, part_imag))
        (ar, ai), (br, bi), (cr, ci), (dr, di) = turned_parts
        sum_ac, dif_ac = (ar + cr, ai + ci), (ar - cr, ai - ci)
        sum_bd, dif_bd = (br + dr, bi + di), (br - dr, bi - di)
        out_real[k], out_imag[k] = sum_ac[0] + sum_bd[0], sum_ac[1] + sum_bd[1]
        out_real[k + 2 * quarter], out_imag[k + 2 * quarter] = sum_ac[0] - sum_bd[0], sum_ac[1] - sum_bd[1]
        plus = (dif_ac[0] + dif_bd[1], dif_ac[1] - dif_bd[0])
        minus = (dif_ac[0] - dif_bd[1], dif_ac[1] + dif_bd[0])
        first_part, second_part = (plus, minus) if orient > 0 else (minus, plus)
        out_real[k + quarter], out_imag[k + quarter] = first_part
        out_real[k + 3 * quarter], out_imag[k + 3 * quarter] = second_part
    return out_real, out_imag


def forward_bound(depth, width):
    return 0.9005 * math.sqrt(depth * width)


def backward_bound(length):
    return 1.0005 * math.sqrt(length)


def code_scale(bound):
    return bound / 32767.0**2


def encode(value, bound):
    scaled = value * lax.rsqrt(jnp.abs(value) + 1e-30) * (32767.0 / math.sqrt(bound))
    return (scaled + jnp.where(value < 0.0, -0.5, 0.5)).astype(jnp.int32).astype(jnp.int16)


def decode(code):
    value = code.astype(jnp.int32).astype(F32)
    return value * jnp.abs(value)


def row_tables(length, depth, width):
    half = length // 2
    positions = np.arange(length)
    freqs = np.arange(half)
    angles = angle_table(positions, freqs, length)
    cos_part, sin_part = np.cos(angles), np.sin(angles)
    sin_part[:, 0] = 1.0 - 2.0 * (positions % 2)
    both = np.concatenate([cos_part, sin_part], 1) / math.sqrt(length)
    return side_by_side(both.T * code_scale(forward_bound(depth, width))), side_by_side(both)


def column_tables(width, depth, length):
    half = width // 2
    positions = np.arange(width)
    freqs = np.arange(half)
    angles = angle_table(positions, freqs, width)
    scale = 1.0 / math.sqrt(width * depth)
    cos_part = np.cos(angles)
    sin_part = -np.sin(angles)
    sin_part[:, 0] = 1.0 - 2.0 * (positions % 2)
    forward = np.concatenate([cos_part, sin_part], 1) * scale
    weights = np.where(freqs == 0, 1.0, 2.0)
    inverse = np.concatenate([cos_part * weights, sin_part * weights], 1).T * scale
    return side_by_side(forward), side_by_side(inverse * code_scale(backward_bound(length)))


def table_times(table, block):
    size = block.shape[0]
    high, low = split(block)
    return dot(table, jnp.concatenate([high, high], 0)) + dot(table[:, :size], low)


def replace_row(array, row):
    top = array[:ROWS]
    row_id = lax.broadcasted_iota(jnp.int32, top.shape, 0)
    return jnp.concatenate([jnp.where(row_id == 0, row[:1], top), array[ROWS:]], 0)


def rows_forward(table, plane):
    both = table_times(table, plane)
    count = both.shape[0] // 2
    half = both.shape[1] // 2
    cos_real, cos_imag = both[:count, :half], both[:count, half:]
    sin_real, sin_imag = both[count:, :half], both[count:, half:]
    above = (replace_row(cos_real + sin_imag, cos_real), replace_row(cos_imag - sin_real, cos_imag))
    below = (replace_row(cos_real - sin_imag, sin_real), replace_row(cos_imag + sin_real, sin_imag))
    return above, below


def rows_inverse(table, above, below):
    even_real = replace_row(above[0] + below[0], above[0])
    even_imag = replace_row(above[1] + below[1], above[1])
    odd_real = replace_row(below[1] - above[1], below[0])
    odd_imag = replace_row(above[0] - below[0], below[1])
    top = jnp.concatenate([even_real, even_imag], 1)
    bottom = jnp.concatenate([odd_real, odd_imag], 1)
    return table_times(table, jnp.concatenate([top, bottom], 0))


def ref_slot_of(map_ref):
    slot = jnp.int32(0)
    for at in range(1, map_ref.shape[0]):
        slot = jnp.where(map_ref[at] == 0, jnp.int32(at), slot)
    return slot


def first_kernel(map_ref, observed_ref, columns_ref, out_ref, spread_ref, turned_ref):
    depth, rows, width = observed_ref.shape[1:]
    half = width // 2
    groups, _, local_depth = out_ref.shape[:3]
    flat = observed_ref[0].reshape(depth * rows, width)
    table = columns_ref[...]
    spread = dot(flat, table[:, :width]) + dot(flat, table[:, width:])
    spread_ref[...] = spread.reshape(depth, rows, width)
    shift = MID * math.sqrt(width * depth)
    spots = depth_order(depth)
    lane = lax.broadcasted_iota(jnp.int32, (ROWS, half), 1)

    @pl.loop(0, rows // ROWS)
    def _(b):
        at = pl.ds(pl.multiple_of(b * ROWS, ROWS), ROWS)
        real = [spread_ref[z, at, :half] for z in range(depth)]
        imag = [spread_ref[z, at, half:] for z in range(depth)]
        real, imag = depth_transform(real, imag, 1)
        edge = lane == 0
        real[0] = jnp.where(edge, real[0] - shift, real[0])
        for k in range(1, depth // 2):
            n = depth - k
            zero_real, zero_imag = 0.5 * (real[k] + real[n]), 0.5 * (imag[k] - imag[n])
            top_real, top_imag = 0.5 * (imag[k] + imag[n]), 0.5 * (real[n] - real[k])
            real[k], imag[k] = jnp.where(edge, zero_real, real[k]), jnp.where(edge, zero_imag, imag[k])
            real[n], imag[n] = jnp.where(edge, top_real, real[n]), jnp.where(edge, top_imag, imag[n])
        for spot, k in enumerate(spots):
            turned_ref[spot, at, :half] = real[k]
            turned_ref[spot, at, half:] = imag[k]

    code = encode(turned_ref[...], forward_bound(depth, width))
    out_ref[:, 0] = code.reshape(groups, local_depth, rows, width)


def load_plane(in_ref, k):
    groups, _, _, rows, width = in_ref.shape
    return decode(in_ref[:, 0, k].reshape(groups * rows, width))


def edge_mask(shape, group_zero):
    row = lax.broadcasted_iota(jnp.int32, shape, 0)
    lane = lax.broadcasted_iota(jnp.int32, shape, 1)
    return (lane == 0) & (row > 0) & group_zero


def spectrum(table, plane, k, group_zero, depth):
    above, below = rows_forward(table, plane)
    if k == 0:
        shift = MID * math.sqrt(depth * plane.shape[0] * plane.shape[1])
        lane = lax.broadcasted_iota(jnp.int32, above[0].shape, 1)
        here = (lane[:1] == 0) & group_zero
        row = jnp.where(here, above[0][:1] + shift, above[0][:1])
        above = (replace_row(above[0], row), above[1])
    if k < 2:
        mask = edge_mask(above[0].shape, group_zero)
        zero = (0.5 * (above[0] + below[0]), 0.5 * (above[1] - below[1]))
        top = (0.5 * (above[1] + below[1]), 0.5 * (below[0] - above[0]))
        above = tuple(jnp.where(mask, new, old) for new, old in zip(zero, above))
        below = tuple(jnp.where(mask, new, old) for new, old in zip(top, below))
    return above, below


def spectrum_kernel(place_ref, in_ref, rows_ref, out_ref):
    group_zero = place_ref[1] == 0
    groups, _, local_depth, _, width = in_ref.shape
    depth = groups * local_depth
    half = width // 2
    table = rows_ref[...]
    for k in range(local_depth):
        above, below = spectrum(table, load_plane(in_ref, k), k, group_zero, depth)
        count = above[0].shape[0]
        out_ref[k, :count, :half] = above[0]
        out_ref[k, :count, half:] = above[1]
        out_ref[k, count:, :half] = below[0]
        out_ref[k, count:, half:] = below[1]


def root(value):
    return value * lax.rsqrt(jnp.maximum(value, 1e-30))


def cross_of(value, ref):
    real, imag = value
    ref_real, ref_imag = ref
    power = (real * real + imag * imag) * (ref_real * ref_real + ref_imag * ref_imag)
    scale = 1.0 / (root(power) + 1.0)
    return (real * ref_real + imag * ref_imag) * scale, (imag * ref_real - real * ref_imag) * scale


def cross_of_real(value, ref):
    product = value * ref
    return product / (jnp.abs(product) + 1.0)


def cross_plane(value, ref, k, group_zero):
    crossed = cross_of(value, ref)
    if k < 2:
        lane = lax.broadcasted_iota(jnp.int32, (1, value[0].shape[1]), 1)
        here = (lane == 0) & group_zero
        parts = []
        for at in range(2):
            row = jnp.where(here, cross_of_real(value[at][:1], ref[at][:1]), crossed[at][:1])
            parts.append(replace_row(crossed[at], row))
        crossed = tuple(parts)
    return crossed


def cross_kernel(map_ref, place_ref, in_ref, rows_ref, back_ref, mine_ref, other_ref, out_ref):
    groups, _, local_depth, rows, width = in_ref.shape
    slots = map_ref.shape[0] // 2
    holds_ref = ref_slot_of(map_ref) // slots == place_ref[0]
    group_zero = place_ref[1] == 0
    depth = groups * local_depth
    half = width // 2
    length = groups * rows
    count = length // 2
    bound = backward_bound(length)
    table = rows_ref[...]
    for k in range(local_depth):
        above, below = spectrum(table, load_plane(in_ref, k), k, group_zero, depth)
        ref = jnp.where(holds_ref, mine_ref[k], other_ref[k])
        above = cross_plane(above, (ref[:count, :half], ref[:count, half:]), k, group_zero)
        below = cross_plane(below, (ref[count:, :half], ref[count:, half:]), k, group_zero)
        if k < 2:
            mask = edge_mask(above[0].shape, group_zero)
            plus = (above[0] - below[1], above[1] + below[0])
            minus = (above[0] + below[1], below[0] - above[1])
            above = tuple(jnp.where(mask, new, old) for new, old in zip(plus, above))
            below = tuple(jnp.where(mask, new, old) for new, old in zip(minus, below))
        back = rows_inverse(back_ref[...], above, below)
        out_ref[:, 0, k] = encode(back, bound).reshape(groups, rows, width)


def last_kernel(map_ref, in_ref, columns_ref, *rest):
    out_ref, turned_ref, spread_ref = rest[-3:]
    groups, _, local_depth, rows, width = in_ref.shape
    depth = groups * local_depth
    half = width // 2
    table = columns_ref[...]
    spots = depth_order(depth)
    value = decode(in_ref[:, 0])
    turned_ref[...] = value.reshape(depth, rows, width)

    @pl.loop(0, rows // ROWS)
    def _(b):
        at = pl.ds(pl.multiple_of(b * ROWS, ROWS), ROWS)
        real, imag = [None] * depth, [None] * depth
        for spot, k in enumerate(spots):
            real[k] = turned_ref[spot, at, :half]
            imag[k] = turned_ref[spot, at, half:]
        edge = lax.broadcasted_iota(jnp.int32, (ROWS, half), 1) == 0
        for k in range(1, depth // 2):
            n = depth - k
            plus = (real[k] - imag[n], imag[k] + real[n])
            minus = (real[k] + imag[n], real[n] - imag[k])
            real[k], imag[k] = jnp.where(edge, plus[0], real[k]), jnp.where(edge, plus[1], imag[k])
            real[n], imag[n] = jnp.where(edge, minus[0], real[n]), jnp.where(edge, minus[1], imag[n])
        real, imag = depth_transform(real, imag, -1)
        for z in range(depth):
            spread_ref[z, at, :half] = real[z]
            spread_ref[z, at, half:] = imag[z]

    high, low = split(spread_ref[...].reshape(depth * rows, width))
    cells = dot(high, table[:, :width]) + dot(high, table[:, width:]) + dot(low, table[:, :width])
    out_ref[0] = cells.reshape(depth, rows, width)


def pick_tap(psf_ref, view, axis, index):
    value = jnp.zeros(index.shape, F32)
    for j in range(TAPS):
        value = jnp.where(index == j, psf_ref[view, axis, j], value)
    return value


def filter_kernel(place_ref, map_ref, shift_ref, psf_ref, forward_ref, backward_ref, columns_ref):
    size = forward_ref.shape[1]
    width = columns_ref.shape[1]
    depth = size // ROWS
    view = map_ref[place_ref[0] * pl.num_programs(0) + pl.program_id(0)]
    depth_shift = shift_ref[view, 0]
    column_shift = shift_ref[view, 1]
    at_out = lax.broadcasted_iota(jnp.int32, (depth, size), 0)
    at_in = lax.broadcasted_iota(jnp.int32, (depth, size), 1) // ROWS
    row = lax.broadcasted_iota(jnp.int32, (ROWS, size), 0)
    cell = lax.broadcasted_iota(jnp.int32, (ROWS, size), 1) % ROWS
    for out_ref, orient in ((forward_ref, 1), (backward_ref, -1)):
        depth_part = pick_tap(psf_ref, view, 0, orient * (at_in - at_out) + HALF - depth_shift)
        for c in range(3):
            reach = c * ROWS + cell - ROWS - row
            row_part = pick_tap(psf_ref, view, 1, orient * reach + HALF)
            block = depth_part[:, None, :] * row_part[None, :, :]
            out_ref[0, :, c * size : (c + 1) * size] = block.reshape(size, size).astype(BF16)
    source = lax.broadcasted_iota(jnp.int32, (width, width), 0)
    target = lax.broadcasted_iota(jnp.int32, (width, width), 1)
    picked = pick_tap(psf_ref, view, 2, source - target + HALF - column_shift)
    columns_ref[0] = picked.astype(BF16)


def join_kernel(
    views,
    updated,
    *refs,
):
    if updated:
        mine_ref, other_ref, *refs = refs
    (
    estimate_ref,
    below_ref,
    above_ref,
    observed_ref,
    seen_below_ref,
    seen_above_ref,
    forward_ref,
    backward_ref,
    columns_ref,
    out_ref,
    *refs,
    ) = refs
    if updated:
        now_ref, *refs = refs
    else:
        now_ref = estimate_ref
    cells_ref, mixed_ref, blurred_ref, ratio_ref, product_ref = refs
    depth, rows, width = estimate_ref.shape
    size = depth * ROWS
    blocks = rows // ROWS
    slots = forward_ref.shape[0]
    step = pl.program_id(0)

    @pl.when(step == 0)
    def _():
        if updated:
            logs = mine_ref[...] + other_ref[...]
            now_ref[...] = estimate_ref[...] * jnp.exp(logs.reshape(depth, rows, width))
        for rim_ref, start in ((below_ref, 0), (above_ref, blocks + 2)):
            for b in range(2):
                piece = rim_ref[b].astype(F32).reshape(size, width)
                cells_ref[start + b] = piece.astype(BF16)
        for b in range(blocks):
            piece = now_ref[:, b * ROWS : (b + 1) * ROWS].reshape(size, width)
            cells_ref[b + 2] = piece.astype(BF16)
        product_ref[...] = jnp.ones_like(product_ref)

        @pl.loop(0, blocks + 2)
        def _(b):
            window = cells_ref[pl.ds(b, 3)].reshape(3 * size, width)
            mixed = dot(forward_ref[...].reshape(slots * size, 3 * size), window)
            mixed_ref[:, b] = mixed.astype(BF16).reshape(slots, size, width)

    columns = columns_ref[0]
    blurred = dot(mixed_ref[step].reshape((blocks + 2) * size, width), columns)
    blurred_ref[...] = blurred.reshape(blocks + 2, size, width)
    for b in range(blocks + 2):
        if b == 0:
            seen = seen_below_ref[0].astype(F32)
        elif b == blocks + 1:
            seen = seen_above_ref[0].astype(F32)
        else:
            seen = observed_ref[0, :, (b - 1) * ROWS : b * ROWS].astype(F32)
        seen = seen.reshape(size, width)
        ratio = jnp.where(seen > 0.0, seen / blurred_ref[b], 0.0)
        ratio_ref[b] = ratio.astype(BF16)
    ratio = dot_t(ratio_ref[...].reshape((blocks + 2) * size, width), columns)
    ratio_ref[...] = ratio.astype(BF16).reshape(blocks + 2, size, width)
    for b in range(blocks):
        window = ratio_ref[b : b + 3].reshape(3 * size, width)
        product_ref[b] = product_ref[b] * dot(backward_ref[0], window)

    @pl.when(step == slots - 1)
    def _():
        for b in range(blocks):
            logs = jnp.log(product_ref[b]) * (1.0 / views)
            out_ref[:, b * ROWS : (b + 1) * ROWS] = logs.reshape(depth, ROWS, width)


def whole(shape):
    return pl.BlockSpec(shape, lambda *_: (0,) * len(shape))


def cost(flops, moved):
    return pl.CostEstimate(flops=int(flops), bytes_accessed=int(moved), transcendentals=0)


def turn(payload):
    return lax.all_to_all(payload, "gz", split_axis=0, concat_axis=0, tiled=True)


def edges(field):
    extent = field.shape[1]
    low = [field[:, at : at + ROWS] for at in (0, ROWS)]
    high = [field[:, at : at + ROWS] for at in (extent - 2 * ROWS, extent - ROWS)]
    return jnp.stack(low), jnp.stack(high)


def send_rims(low, high):
    count = lax.axis_size("gz")
    below = lax.ppermute(high, "gz", [(i, i + 1) for i in range(count - 1)])
    above = lax.ppermute(low, "gz", [(i + 1, i) for i in range(count - 1)])
    return below, above


def swap_cores(field):
    count = lax.axis_size("view")
    return lax.ppermute(field, "view", [(i, (i + 1) % count) for i in range(count)])


def on_device(observed, initial, psf_taps, view_shifts, view_map):
    slots, depth, rows, width = observed.shape
    views = view_map.shape[0]
    groups = lax.axis_size("gz")
    length = groups * rows
    local_depth = depth // groups
    size = depth * ROWS
    blocks = rows // ROWS
    place = jnp.stack([lax.axis_index("view"), lax.axis_index("gz")]).astype(jnp.int32)

    columns_forward, columns_inverse = column_tables(width, depth, length)
    row_turn, row_back = row_tables(length, depth, width)

    low, high = edges(initial.astype(BF16))
    low = jnp.concatenate([observed[:, :, :ROWS], low], 0)
    high = jnp.concatenate([observed[:, :, rows - ROWS :], high], 0)
    first_rims = send_rims(low, high)

    chunk = slots // 2
    payload_block = (groups, 1, local_depth, rows, width)
    payload_shape = (groups, chunk, local_depth, rows, width)
    payload_bytes = 4 * depth * rows * width * chunk
    volume = depth * rows * width

    def first(start):
        return pl.pallas_call(
            first_kernel,
            grid_spec=pltpu.PrefetchScalarGridSpec(
                num_scalar_prefetch=1,
                grid=(chunk,),
                in_specs=[
                    pl.BlockSpec((1, depth, rows, width), lambda s, m: (lax.rem(s + start + ref_slot_of(m), slots), 0, 0, 0)),
                    whole(columns_forward.shape),
                ],
                out_specs=pl.BlockSpec(payload_block, lambda *a: (0, a[0], 0, 0, 0)),
                scratch_shapes=[pltpu.VMEM((depth, rows, width), F32)] * 2,
            ),
            out_shape=jax.ShapeDtypeStruct(payload_shape, jnp.int16),
            cost_estimate=cost(2 * chunk * volume * 8 * width, payload_bytes),
            name="first",
        )(view_map, observed, columns_forward)

    spectrum_shape = (local_depth, length, width)
    row_flops = 2 * local_depth * length * width * 3 * length

    def reference_spectrum(payload):
        return pl.pallas_call(
            spectrum_kernel,
            grid_spec=pltpu.PrefetchScalarGridSpec(
                num_scalar_prefetch=1,
                grid=(1,),
                in_specs=[
                    pl.BlockSpec(payload_block, lambda *_: (0, 0, 0, 0, 0)),
                    whole(row_turn.shape),
                ],
                out_specs=whole(spectrum_shape),
            ),
            out_shape=jax.ShapeDtypeStruct(spectrum_shape, F32),
            cost_estimate=cost(row_flops, 6 * volume),
            name="spectrum",
        )(place, payload, row_turn)

    def crossed(payload, mine, other):
        return pl.pallas_call(
            cross_kernel,
            grid_spec=pltpu.PrefetchScalarGridSpec(
                num_scalar_prefetch=2,
                grid=(chunk,),
                in_specs=[
                    pl.BlockSpec(payload_block, lambda *a: (0, a[0], 0, 0, 0)),
                    whole(row_turn.shape),
                    whole(row_back.shape),
                    whole(spectrum_shape),
                    whole(spectrum_shape),
                ],
                out_specs=pl.BlockSpec(payload_block, lambda *a: (0, a[0], 0, 0, 0)),
            ),
            out_shape=jax.ShapeDtypeStruct(payload_shape, jnp.int16),
            cost_estimate=cost(2 * row_flops * chunk, payload_bytes + 10 * volume),
            name="cross",
        )(view_map, place, payload, row_turn, row_back, mine, other)

    def last(payload, start, partial):
        specs = [
            pl.BlockSpec(payload_block, lambda *a: (0, a[0], 0, 0, 0)),
            whole(columns_inverse.shape),
        ]
        operands = [view_map, payload, columns_inverse]
        aliases = {}
        if partial is not None:
            specs.append(pl.BlockSpec(memory_space=pl.ANY))
            aliases = {len(operands): 0}
            operands.append(partial)
        return pl.pallas_call(
            last_kernel,
            grid_spec=pltpu.PrefetchScalarGridSpec(
                num_scalar_prefetch=1,
                grid=(chunk,),
                in_specs=specs,
                out_specs=pl.BlockSpec((1, depth, rows, width), lambda s, m: (lax.rem(s + start + ref_slot_of(m), slots), 0, 0, 0)),
                scratch_shapes=[pltpu.VMEM((depth, rows, width), F32)] * 2,
            ),
            out_shape=jax.ShapeDtypeStruct((slots, depth, rows, width), F32),
            input_output_aliases=aliases,
            cost_estimate=cost(2 * chunk * volume * 9 * width, payload_bytes * 1.5),
            name="last",
        )(*operands)

    def filters():
        smem = pl.BlockSpec(memory_space=pltpu.SMEM)
        return pl.pallas_call(
            filter_kernel,
            grid=(slots,),
            in_specs=[smem] * 4,
            out_specs=[
                pl.BlockSpec((1, size, 3 * size), lambda s: (s, 0, 0)),
                pl.BlockSpec((1, size, 3 * size), lambda s: (s, 0, 0)),
                pl.BlockSpec((1, width, width), lambda s: (s, 0, 0)),
            ],
            out_shape=[
                jax.ShapeDtypeStruct((slots, size, 3 * size), BF16),
                jax.ShapeDtypeStruct((slots, size, 3 * size), BF16),
                jax.ShapeDtypeStruct((slots, width, width), BF16),
            ],
            cost_estimate=cost(slots * size * size * 60, slots * size * size * 14),
            name="filters",
        )(place, view_map, view_shifts, psf_taps)

    forward, backward, columns = filters()

    def join(estimate, below, above, logs=None):
        def slot_block(shape):
            return pl.BlockSpec((1,) + shape, lambda s: (s,) + (0,) * len(shape))

        def rim_block(rim):
            at = rim.shape[0] // 2 - 1
            return pl.BlockSpec((2, depth, ROWS, width), lambda s: (at, 0, 0, 0))

        updated = logs is not None
        field = jax.ShapeDtypeStruct((depth, rows, width), F32)
        extra_specs = []
        if updated:
            extra_specs = [whole((depth, rows, width))] * 2
        return pl.pallas_call(
            functools.partial(join_kernel, views, updated),
            grid=(slots,),
            in_specs=extra_specs
            + [
                whole((depth, rows, width)),
                rim_block(below),
                rim_block(above),
                slot_block((depth, rows, width)),
                slot_block((depth, ROWS, width)),
                slot_block((depth, ROWS, width)),
                whole((slots, size, 3 * size)),
                slot_block((size, 3 * size)),
                slot_block((width, width)),
            ],
            out_specs=[whole((depth, rows, width))] * (1 + updated),
            out_shape=[field] * (1 + updated),
            scratch_shapes=[
                pltpu.VMEM((blocks + 4, size, width), BF16),
                pltpu.VMEM((slots, blocks + 2, size, width), BF16),
                pltpu.VMEM((blocks + 2, size, width), F32),
                pltpu.VMEM((blocks + 2, size, width), BF16),
                pltpu.VMEM((blocks, size, width), F32),
            ],
            cost_estimate=cost(2 * slots * size * width * ((blocks + 2) * (3 * size + 2 * width) + blocks * 3 * size), 12e6),
            name="join",
        )(*(logs or ()), estimate, below, above, observed, *first_rims, forward, backward, columns)

    sent_a = turn(first(0))
    payload_b = first(chunk)
    sent_b = turn(payload_b)
    mine = reference_spectrum(sent_a)
    other = swap_cores(mine)
    crossed_a, start = lax.optimization_barrier((crossed(sent_a, mine, other), initial))
    back_a = turn(crossed_a)

    (logs,) = join(start, *first_rims)
    logs, late = lax.optimization_barrier((logs, sent_b))
    total = (logs, swap_cores(logs))
    crossed_b = crossed(late, mine, other)

    def updated_rows(at):
        window = [lax.slice_in_dim(part, at, at + ROWS, axis=1) for part in (initial, *total)]
        return (window[0] * jnp.exp(window[1] + window[2])).astype(BF16)

    low = jnp.stack([updated_rows(at) for at in (0, ROWS)])
    high = jnp.stack([updated_rows(at) for at in (rows - 2 * ROWS, rows - ROWS)])
    rims = send_rims(low, high)
    back_b = turn(crossed_b)
    logs, estimate = join(initial, *rims, logs=total)
    estimate = estimate * jnp.exp(logs + swap_cores(logs))

    surfaces = last(back_a, 0, None)
    surfaces = last(back_b, chunk, surfaces)
    return estimate, surfaces


def solution(mesh):
    placed = (P("view", "parts", "gz", None), P("parts", "gz", None), P(), P(), P())

    return jax.shard_map(
        on_device,
        mesh=mesh,
        in_specs=placed,
        out_specs=(P("parts", "gz", None), P("view", "parts", "gz", None)),
        check_vma=False,
    )
```

```python
import functools
import math

import jax
import jax.numpy as jnp
import ml_dtypes
import numpy as np
from jax import lax
from jax.experimental import pallas as pl
from jax.experimental.pallas import tpu as pltpu
from jax.sharding import PartitionSpec as P


TAPS = 15
HALF = TAPS // 2
ROWS = 8
MID = 1.099609375


F32 = jnp.float32
BF16 = jnp.bfloat16


def dot(a, b):
    return jnp.dot(a, b, preferred_element_type=F32)


def dot_t(a, b):
    return lax.dot_general(a, b, (((1,), (1,)), ((), ())), preferred_element_type=F32)


def split(value):
    high = value.astype(BF16)
    return high, (value - high.astype(F32)).astype(BF16)


def np_split(table):
    high = table.astype(ml_dtypes.bfloat16)
    low = (table - high.astype(np.float64)).astype(ml_dtypes.bfloat16)
    return high, low


def side_by_side(table):
    return jnp.asarray(np.concatenate(np_split(table), 1))


def depth_order(depth):
    order = [0, depth // 2]
    for m in range(1, depth // 2):
        order += [m, depth - m]
    return np.array(order)


def angle_table(rows, columns, length):
    return 2.0 * np.pi * ((rows[:, None] * columns[None, :]) % length) / length


def depth_transform(real, imag, orient):
    count = len(real)
    if count == 1:
        return real, imag
    if count == 2:
        return [real[0] + real[1], real[0] - real[1]], [imag[0] + imag[1], imag[0] - imag[1]]
    quarter = count // 4
    parts = [depth_transform(real[j::4], imag[j::4], orient) for j in range(4)]
    out_real, out_imag = [None] * count, [None] * count
    for k in range(quarter):
        turned_parts = []
        for j in range(4):
            part_real, part_imag = parts[j][0][k], parts[j][1][k]
            if j * k:
                angle = -orient * 2.0 * math.pi * j * k / count
                cos, sin = math.cos(angle), math.sin(angle)
                if 8 * j * k == count:
                    part_real, part_imag = (part_real + orient * part_imag) * cos, (part_imag - orient * part_real) * cos
                else:
                    part_real, part_imag = part_real * cos - part_imag * sin, part_real * sin + part_imag * cos
            turned_parts.append((part_real, part_imag))
        (ar, ai), (br, bi), (cr, ci), (dr, di) = turned_parts
        sum_ac, dif_ac = (ar + cr, ai + ci), (ar - cr, ai - ci)
        sum_bd, dif_bd = (br + dr, bi + di), (br - dr, bi - di)
        out_real[k], out_imag[k] = sum_ac[0] + sum_bd[0], sum_ac[1] + sum_bd[1]
        out_real[k + 2 * quarter], out_imag[k + 2 * quarter] = sum_ac[0] - sum_bd[0], sum_ac[1] - sum_bd[1]
        plus = (dif_ac[0] + dif_bd[1], dif_ac[1] - dif_bd[0])
        minus = (dif_ac[0] - dif_bd[1], dif_ac[1] + dif_bd[0])
        first_part, second_part = (plus, minus) if orient > 0 else (minus, plus)
        out_real[k + quarter], out_imag[k + quarter] = first_part
        out_real[k + 3 * quarter], out_imag[k + 3 * quarter] = second_part
    return out_real, out_imag


def forward_bound(depth, width):
    return 0.9005 * math.sqrt(depth * width)


def backward_bound(length):
    return 1.0005 * math.sqrt(length)


def code_scale(bound):
    return bound / 32767.0**2


def encode(value, bound):
    scaled = value * lax.rsqrt(jnp.abs(value) + 1e-30) * (32767.0 / math.sqrt(bound))
    return (scaled + jnp.where(value < 0.0, -0.5, 0.5)).astype(jnp.int32).astype(jnp.int16)


def decode(code):
    value = code.astype(jnp.int32).astype(F32)
    return value * jnp.abs(value)


def row_tables(length, depth, width):
    half = length // 2
    positions = np.arange(length)
    freqs = np.arange(half)
    angles = angle_table(positions, freqs, length)
    cos_part, sin_part = np.cos(angles), np.sin(angles)
    sin_part[:, 0] = 1.0 - 2.0 * (positions % 2)
    both = np.concatenate([cos_part, sin_part], 1) / math.sqrt(length)
    return side_by_side(both.T * code_scale(forward_bound(depth, width))), side_by_side(both)


def column_tables(width, depth, length):
    half = width // 2
    positions = np.arange(width)
    freqs = np.arange(half)
    angles = angle_table(positions, freqs, width)
    scale = 1.0 / math.sqrt(width * depth)
    cos_part = np.cos(angles)
    sin_part = -np.sin(angles)
    sin_part[:, 0] = 1.0 - 2.0 * (positions % 2)
    forward = np.concatenate([cos_part, sin_part], 1) * scale
    weights = np.where(freqs == 0, 1.0, 2.0)
    inverse = np.concatenate([cos_part * weights, sin_part * weights], 1).T * scale
    return side_by_side(forward), side_by_side(inverse * code_scale(backward_bound(length)))


def table_times(table, block):
    size = block.shape[0]
    high, low = split(block)
    return dot(table, jnp.concatenate([high, high], 0)) + dot(table[:, :size], low)


def replace_row(array, row):
    top = array[:ROWS]
    row_id = lax.broadcasted_iota(jnp.int32, top.shape, 0)
    return jnp.concatenate([jnp.where(row_id == 0, row[:1], top), array[ROWS:]], 0)


def rows_forward(table, plane):
    both = table_times(table, plane)
    count = both.shape[0] // 2
    half = both.shape[1] // 2
    cos_real, cos_imag = both[:count, :half], both[:count, half:]
    sin_real, sin_imag = both[count:, :half], both[count:, half:]
    above = (replace_row(cos_real + sin_imag, cos_real), replace_row(cos_imag - sin_real, cos_imag))
    below = (replace_row(cos_real - sin_imag, sin_real), replace_row(cos_imag + sin_real, sin_imag))
    return above, below


def rows_inverse(table, above, below):
    even_real = replace_row(above[0] + below[0], above[0])
    even_imag = replace_row(above[1] + below[1], above[1])
    odd_real = replace_row(below[1] - above[1], below[0])
    odd_imag = replace_row(above[0] - below[0], below[1])
    top = jnp.concatenate([even_real, even_imag], 1)
    bottom = jnp.concatenate([odd_real, odd_imag], 1)
    return table_times(table, jnp.concatenate([top, bottom], 0))


def ref_slot_of(map_ref):
    slot = jnp.int32(0)
    for at in range(1, map_ref.shape[0]):
        slot = jnp.where(map_ref[at] == 0, jnp.int32(at), slot)
    return slot


def first_kernel(map_ref, observed_ref, columns_ref, out_ref, spread_ref, turned_ref):
    depth, rows, width = observed_ref.shape[1:]
    half = width // 2
    groups, _, local_depth = out_ref.shape[:3]
    flat = observed_ref[0].reshape(depth * rows, width)
    table = columns_ref[...]
    spread = dot(flat, table[:, :width]) + dot(flat, table[:, width:])
    spread_ref[...] = spread.reshape(depth, rows, width)
    shift = MID * math.sqrt(width * depth)
    spots = depth_order(depth)
    lane = lax.broadcasted_iota(jnp.int32, (ROWS, half), 1)

    @pl.loop(0, rows // ROWS)
    def _(b):
        at = pl.ds(pl.multiple_of(b * ROWS, ROWS), ROWS)
        real = [spread_ref[z, at, :half] for z in range(depth)]
        imag = [spread_ref[z, at, half:] for z in range(depth)]
        real, imag = depth_transform(real, imag, 1)
        edge = lane == 0
        real[0] = jnp.where(edge, real[0] - shift, real[0])
        for k in range(1, depth // 2):
            n = depth - k
            zero_real, zero_imag = 0.5 * (real[k] + real[n]), 0.5 * (imag[k] - imag[n])
            top_real, top_imag = 0.5 * (imag[k] + imag[n]), 0.5 * (real[n] - real[k])
            real[k], imag[k] = jnp.where(edge, zero_real, real[k]), jnp.where(edge, zero_imag, imag[k])
            real[n], imag[n] = jnp.where(edge, top_real, real[n]), jnp.where(edge, top_imag, imag[n])
        for spot, k in enumerate(spots):
            turned_ref[spot, at, :half] = real[k]
            turned_ref[spot, at, half:] = imag[k]

    code = encode(turned_ref[...], forward_bound(depth, width))
    out_ref[:, 0] = code.reshape(groups, local_depth, rows, width)


def load_plane(in_ref, k):
    groups, _, _, rows, width = in_ref.shape
    return decode(in_ref[:, 0, k].reshape(groups * rows, width))


def edge_mask(shape, group_zero):
    row = lax.broadcasted_iota(jnp.int32, shape, 0)
    lane = lax.broadcasted_iota(jnp.int32, shape, 1)
    return (lane == 0) & (row > 0) & group_zero


def spectrum(table, plane, k, group_zero, depth):
    above, below = rows_forward(table, plane)
    if k == 0:
        shift = MID * math.sqrt(depth * plane.shape[0] * plane.shape[1])
        lane = lax.broadcasted_iota(jnp.int32, above[0].shape, 1)
        here = (lane[:1] == 0) & group_zero
        row = jnp.where(here, above[0][:1] + shift, above[0][:1])
        above = (replace_row(above[0], row), above[1])
    if k < 2:
        mask = edge_mask(above[0].shape, group_zero)
        zero = (0.5 * (above[0] + below[0]), 0.5 * (above[1] - below[1]))
        top = (0.5 * (above[1] + below[1]), 0.5 * (below[0] - above[0]))
        above = tuple(jnp.where(mask, new, old) for new, old in zip(zero, above))
        below = tuple(jnp.where(mask, new, old) for new, old in zip(top, below))
    return above, below


def spectrum_kernel(place_ref, in_ref, rows_ref, out_ref):
    group_zero = place_ref[1] == 0
    groups, _, local_depth, _, width = in_ref.shape
    depth = groups * local_depth
    half = width // 2
    table = rows_ref[...]
    for k in range(local_depth):
        above, below = spectrum(table, load_plane(in_ref, k), k, group_zero, depth)
        count = above[0].shape[0]
        out_ref[k, :count, :half] = above[0]
        out_ref[k, :count, half:] = above[1]
        out_ref[k, count:, :half] = below[0]
        out_ref[k, count:, half:] = below[1]


def root(value):
    return value * lax.rsqrt(jnp.maximum(value, 1e-30))


def cross_of(value, ref):
    real, imag = value
    ref_real, ref_imag = ref
    power = (real * real + imag * imag) * (ref_real * ref_real + ref_imag * ref_imag)
    scale = 1.0 / (root(power) + 1.0)
    return (real * ref_real + imag * ref_imag) * scale, (imag * ref_real - real * ref_imag) * scale


def cross_of_real(value, ref):
    product = value * ref
    return product / (jnp.abs(product) + 1.0)


def cross_plane(value, ref, k, group_zero):
    crossed = cross_of(value, ref)
    if k < 2:
        lane = lax.broadcasted_iota(jnp.int32, (1, value[0].shape[1]), 1)
        here = (lane == 0) & group_zero
        parts = []
        for at in range(2):
            row = jnp.where(here, cross_of_real(value[at][:1], ref[at][:1]), crossed[at][:1])
            parts.append(replace_row(crossed[at], row))
        crossed = tuple(parts)
    return crossed


def cross_kernel(map_ref, place_ref, in_ref, rows_ref, back_ref, mine_ref, other_ref, out_ref):
    groups, _, local_depth, rows, width = in_ref.shape
    slots = map_ref.shape[0] // 2
    holds_ref = ref_slot_of(map_ref) // slots == place_ref[0]
    group_zero = place_ref[1] == 0
    depth = groups * local_depth
    half = width // 2
    length = groups * rows
    count = length // 2
    bound = backward_bound(length)
    table = rows_ref[...]
    for k in range(local_depth):
        above, below = spectrum(table, load_plane(in_ref, k), k, group_zero, depth)
        ref = jnp.where(holds_ref, mine_ref[k], other_ref[k])
        above = cross_plane(above, (ref[:count, :half], ref[:count, half:]), k, group_zero)
        below = cross_plane(below, (ref[count:, :half], ref[count:, half:]), k, group_zero)
        if k < 2:
            mask = edge_mask(above[0].shape, group_zero)
            plus = (above[0] - below[1], above[1] + below[0])
            minus = (above[0] + below[1], below[0] - above[1])
            above = tuple(jnp.where(mask, new, old) for new, old in zip(plus, above))
            below = tuple(jnp.where(mask, new, old) for new, old in zip(minus, below))
        back = rows_inverse(back_ref[...], above, below)
        out_ref[:, 0, k] = encode(back, bound).reshape(groups, rows, width)


def last_kernel(map_ref, in_ref, columns_ref, *rest):
    out_ref, turned_ref, spread_ref = rest[-3:]
    groups, _, local_depth, rows, width = in_ref.shape
    depth = groups * local_depth
    half = width // 2
    table = columns_ref[...]
    spots = depth_order(depth)
    value = decode(in_ref[:, 0])
    turned_ref[...] = value.reshape(depth, rows, width)

    @pl.loop(0, rows // ROWS)
    def _(b):
        at = pl.ds(pl.multiple_of(b * ROWS, ROWS), ROWS)
        real, imag = [None] * depth, [None] * depth
        for spot, k in enumerate(spots):
            real[k] = turned_ref[spot, at, :half]
            imag[k] = turned_ref[spot, at, half:]
        edge = lax.broadcasted_iota(jnp.int32, (ROWS, half), 1) == 0
        for k in range(1, depth // 2):
            n = depth - k
            plus = (real[k] - imag[n], imag[k] + real[n])
            minus = (real[k] + imag[n], real[n] - imag[k])
            real[k], imag[k] = jnp.where(edge, plus[0], real[k]), jnp.where(edge, plus[1], imag[k])
            real[n], imag[n] = jnp.where(edge, minus[0], real[n]), jnp.where(edge, minus[1], imag[n])
        real, imag = depth_transform(real, imag, -1)
        for z in range(depth):
            spread_ref[z, at, :half] = real[z]
            spread_ref[z, at, half:] = imag[z]

    high, low = split(spread_ref[...].reshape(depth * rows, width))
    cells = dot(high, table[:, :width]) + dot(high, table[:, width:]) + dot(low, table[:, :width])
    out_ref[0] = cells.reshape(depth, rows, width)


def pick_tap(psf_ref, view, axis, index):
    value = jnp.zeros(index.shape, F32)
    for j in range(TAPS):
        value = jnp.where(index == j, psf_ref[view, axis, j], value)
    return value


def filter_kernel(place_ref, map_ref, shift_ref, psf_ref, forward_ref, backward_ref, columns_ref):
    size = forward_ref.shape[1]
    width = columns_ref.shape[1]
    depth = size // ROWS
    view = map_ref[place_ref[0] * pl.num_programs(0) + pl.program_id(0)]
    depth_shift = shift_ref[view, 0]
    column_shift = shift_ref[view, 1]
    at_out = lax.broadcasted_iota(jnp.int32, (depth, size), 0)
    at_in = lax.broadcasted_iota(jnp.int32, (depth, size), 1) // ROWS
    row = lax.broadcasted_iota(jnp.int32, (ROWS, size), 0)
    cell = lax.broadcasted_iota(jnp.int32, (ROWS, size), 1) % ROWS
    for out_ref, orient in ((forward_ref, 1), (backward_ref, -1)):
        depth_part = pick_tap(psf_ref, view, 0, orient * (at_in - at_out) + HALF - depth_shift)
        for c in range(3):
            reach = c * ROWS + cell - ROWS - row
            row_part = pick_tap(psf_ref, view, 1, orient * reach + HALF)
            block = depth_part[:, None, :] * row_part[None, :, :]
            out_ref[0, :, c * size : (c + 1) * size] = block.reshape(size, size).astype(BF16)
    source = lax.broadcasted_iota(jnp.int32, (width, width), 0)
    target = lax.broadcasted_iota(jnp.int32, (width, width), 1)
    picked = pick_tap(psf_ref, view, 2, source - target + HALF - column_shift)
    columns_ref[0] = picked.astype(BF16)


def join_kernel(
    views,
    updated,
    *refs,
):
    if updated:
        mine_ref, other_ref, *refs = refs
    (
    place_ref,
    estimate_ref,
    strips_ref,
    swapped_ref,
    observed_ref,
    seen_below_ref,
    seen_above_ref,
    forward_ref,
    backward_ref,
    columns_ref,
    out_ref,
    *refs,
    ) = refs
    if updated:
        now_ref, *refs = refs
    else:
        now_ref = estimate_ref
    cells_ref, mixed_ref, blurred_ref, ratio_ref, product_ref = refs
    depth, rows, width = estimate_ref.shape
    size = depth * ROWS
    blocks = rows // ROWS
    slots = forward_ref.shape[0]
    step = pl.program_id(0)

    @pl.when(step == 0)
    def _():
        if updated:
            logs = mine_ref[...] + other_ref[...]
            now_ref[...] = estimate_ref[...] * jnp.exp(logs.reshape(depth, rows, width))
        first_core = place_ref[0] == 0
        for side, near, far in ((0, 1, 0), (1, blocks + 2, blocks + 3)):
            own = strips_ref[side].astype(F32).reshape(size, width)
            swapped = swapped_ref[side].astype(F32).reshape(size, width)
            cells_ref[near] = jnp.where(first_core, own, swapped).astype(BF16)
            cells_ref[far] = jnp.where(first_core, swapped, own).astype(BF16)
        for b in range(blocks):
            piece = now_ref[:, b * ROWS : (b + 1) * ROWS].reshape(size, width)
            cells_ref[b + 2] = piece.astype(BF16)
        product_ref[...] = jnp.ones_like(product_ref)

        @pl.loop(0, blocks + 2)
        def _(b):
            window = cells_ref[pl.ds(b, 3)].reshape(3 * size, width)
            mixed = dot(forward_ref[...].reshape(slots * size, 3 * size), window)
            mixed_ref[:, b] = mixed.astype(BF16).reshape(slots, size, width)

    columns = columns_ref[0]
    blurred = dot(mixed_ref[step].reshape((blocks + 2) * size, width), columns)
    blurred_ref[...] = blurred.reshape(blocks + 2, size, width)
    for b in range(blocks + 2):
        if b == 0:
            seen = seen_below_ref[0].astype(F32)
        elif b == blocks + 1:
            seen = seen_above_ref[0].astype(F32)
        else:
            seen = observed_ref[0, :, (b - 1) * ROWS : b * ROWS].astype(F32)
        seen = seen.reshape(size, width)
        ratio = jnp.where(seen > 0.0, seen / blurred_ref[b], 0.0)
        ratio_ref[b] = ratio.astype(BF16)
    ratio = dot_t(ratio_ref[...].reshape((blocks + 2) * size, width), columns)
    ratio_ref[...] = ratio.astype(BF16).reshape(blocks + 2, size, width)
    for b in range(blocks):
        window = ratio_ref[b : b + 3].reshape(3 * size, width)
        product_ref[b] = product_ref[b] * dot(backward_ref[0], window)

    @pl.when(step == slots - 1)
    def _():
        for b in range(blocks):
            logs = jnp.log(product_ref[b]) * (1.0 / views)
            out_ref[:, b * ROWS : (b + 1) * ROWS] = logs.reshape(depth, ROWS, width)


def whole(shape):
    return pl.BlockSpec(shape, lambda *_: (0,) * len(shape))


def cost(flops, moved):
    return pl.CostEstimate(flops=int(flops), bytes_accessed=int(moved), transcendentals=0)


def turn(payload):
    return lax.all_to_all(payload, "gz", split_axis=0, concat_axis=0, tiled=True)


def own_strip(near, far):
    return jnp.where(lax.axis_index("view") == 0, near, far)


def send_rims(low, high):
    count = lax.axis_size("gz")
    below = lax.ppermute(high, "gz", [(i, i + 1) for i in range(count - 1)])
    above = lax.ppermute(low, "gz", [(i + 1, i) for i in range(count - 1)])
    return below, above


def swap_cores(field):
    count = lax.axis_size("view")
    return lax.ppermute(field, "view", [(i, (i + 1) % count) for i in range(count)])


def swap_strips(strips):
    mine = jnp.stack(strips)
    return mine, swap_cores(mine)


def on_device(observed, initial, psf_taps, view_shifts, view_map):
    slots, depth, rows, width = observed.shape
    views = view_map.shape[0]
    groups = lax.axis_size("gz")
    length = groups * rows
    local_depth = depth // groups
    size = depth * ROWS
    blocks = rows // ROWS
    place = jnp.stack([lax.axis_index("view"), lax.axis_index("gz")]).astype(jnp.int32)

    columns_forward, columns_inverse = column_tables(width, depth, length)
    row_turn, row_back = row_tables(length, depth, width)

    strips = [initial[:, at : at + ROWS].astype(BF16) for at in (0, ROWS, rows - 2 * ROWS, rows - ROWS)]
    low = jnp.concatenate([observed[:, :, :ROWS], own_strip(strips[0], strips[1])[None]], 0)
    high = jnp.concatenate([observed[:, :, rows - ROWS :], own_strip(strips[3], strips[2])[None]], 0)
    first_rims = send_rims(low, high)

    chunk = slots // 2
    payload_block = (groups, 1, local_depth, rows, width)
    payload_shape = (groups, chunk, local_depth, rows, width)
    payload_bytes = 4 * depth * rows * width * chunk
    volume = depth * rows * width

    def first(start):
        return pl.pallas_call(
            first_kernel,
            grid_spec=pltpu.PrefetchScalarGridSpec(
                num_scalar_prefetch=1,
                grid=(chunk,),
                in_specs=[
                    pl.BlockSpec((1, depth, rows, width), lambda s, m: (lax.rem(s + start + ref_slot_of(m), slots), 0, 0, 0)),
                    whole(columns_forward.shape),
                ],
                out_specs=pl.BlockSpec(payload_block, lambda *a: (0, a[0], 0, 0, 0)),
                scratch_shapes=[pltpu.VMEM((depth, rows, width), F32)] * 2,
            ),
            out_shape=jax.ShapeDtypeStruct(payload_shape, jnp.int16),
            cost_estimate=cost(2 * chunk * volume * 8 * width, payload_bytes),
            name="first",
        )(view_map, observed, columns_forward)

    spectrum_shape = (local_depth, length, width)
    row_flops = 2 * local_depth * length * width * 3 * length

    def reference_spectrum(payload):
        return pl.pallas_call(
            spectrum_kernel,
            grid_spec=pltpu.PrefetchScalarGridSpec(
                num_scalar_prefetch=1,
                grid=(1,),
                in_specs=[
                    pl.BlockSpec(payload_block, lambda *_: (0, 0, 0, 0, 0)),
                    whole(row_turn.shape),
                ],
                out_specs=whole(spectrum_shape),
            ),
            out_shape=jax.ShapeDtypeStruct(spectrum_shape, F32),
            cost_estimate=cost(row_flops, 6 * volume),
            name="spectrum",
        )(place, payload, row_turn)

    def crossed(payload, mine, other):
        return pl.pallas_call(
            cross_kernel,
            grid_spec=pltpu.PrefetchScalarGridSpec(
                num_scalar_prefetch=2,
                grid=(chunk,),
                in_specs=[
                    pl.BlockSpec(payload_block, lambda *a: (0, a[0], 0, 0, 0)),
                    whole(row_turn.shape),
                    whole(row_back.shape),
                    whole(spectrum_shape),
                    whole(spectrum_shape),
                ],
                out_specs=pl.BlockSpec(payload_block, lambda *a: (0, a[0], 0, 0, 0)),
            ),
            out_shape=jax.ShapeDtypeStruct(payload_shape, jnp.int16),
            cost_estimate=cost(2 * row_flops * chunk, payload_bytes + 10 * volume),
            name="cross",
        )(view_map, place, payload, row_turn, row_back, mine, other)

    def last(payload, start, partial):
        specs = [
            pl.BlockSpec(payload_block, lambda *a: (0, a[0], 0, 0, 0)),
            whole(columns_inverse.shape),
        ]
        operands = [view_map, payload, columns_inverse]
        aliases = {}
        if partial is not None:
            specs.append(pl.BlockSpec(memory_space=pl.ANY))
            aliases = {len(operands): 0}
            operands.append(partial)
        return pl.pallas_call(
            last_kernel,
            grid_spec=pltpu.PrefetchScalarGridSpec(
                num_scalar_prefetch=1,
                grid=(chunk,),
                in_specs=specs,
                out_specs=pl.BlockSpec((1, depth, rows, width), lambda s, m: (lax.rem(s + start + ref_slot_of(m), slots), 0, 0, 0)),
                scratch_shapes=[pltpu.VMEM((depth, rows, width), F32)] * 2,
            ),
            out_shape=jax.ShapeDtypeStruct((slots, depth, rows, width), F32),
            input_output_aliases=aliases,
            cost_estimate=cost(2 * chunk * volume * 9 * width, payload_bytes * 1.5),
            name="last",
        )(*operands)

    def filters():
        smem = pl.BlockSpec(memory_space=pltpu.SMEM)
        return pl.pallas_call(
            filter_kernel,
            grid=(slots,),
            in_specs=[smem] * 4,
            out_specs=[
                pl.BlockSpec((1, size, 3 * size), lambda s: (s, 0, 0)),
                pl.BlockSpec((1, size, 3 * size), lambda s: (s, 0, 0)),
                pl.BlockSpec((1, width, width), lambda s: (s, 0, 0)),
            ],
            out_shape=[
                jax.ShapeDtypeStruct((slots, size, 3 * size), BF16),
                jax.ShapeDtypeStruct((slots, size, 3 * size), BF16),
                jax.ShapeDtypeStruct((slots, width, width), BF16),
            ],
            cost_estimate=cost(slots * size * size * 60, slots * size * size * 14),
            name="filters",
        )(place, view_map, view_shifts, psf_taps)

    forward, backward, columns = filters()

    def join(estimate, strips, rims, logs=None):
        def slot_block(shape):
            return pl.BlockSpec((1,) + shape, lambda s: (s,) + (0,) * len(shape))

        updated = logs is not None
        field = jax.ShapeDtypeStruct((depth, rows, width), F32)
        extra_specs = []
        if updated:
            extra_specs = [whole((depth, rows, width))] * 2
        return pl.pallas_call(
            functools.partial(join_kernel, views, updated),
            grid=(slots,),
            in_specs=extra_specs
            + [
                pl.BlockSpec(memory_space=pltpu.SMEM),
                whole((depth, rows, width)),
                whole((2, depth, ROWS, width)),
                whole((2, depth, ROWS, width)),
                slot_block((depth, rows, width)),
                slot_block((depth, ROWS, width)),
                slot_block((depth, ROWS, width)),
                whole((slots, size, 3 * size)),
                slot_block((size, 3 * size)),
                slot_block((width, width)),
            ],
            out_specs=[whole((depth, rows, width))] * (1 + updated),
            out_shape=[field] * (1 + updated),
            scratch_shapes=[
                pltpu.VMEM((blocks + 4, size, width), BF16),
                pltpu.VMEM((slots, blocks + 2, size, width), BF16),
                pltpu.VMEM((blocks + 2, size, width), F32),
                pltpu.VMEM((blocks + 2, size, width), BF16),
                pltpu.VMEM((blocks, size, width), F32),
            ],
            cost_estimate=cost(2 * slots * size * width * ((blocks + 2) * (3 * size + 2 * width) + blocks * 3 * size), 12e6),
            name="join",
        )(*(logs or ()), place, estimate, *strips, observed, *rims, forward, backward, columns)

    sent_a = turn(first(0))
    payload_b = first(chunk)
    sent_b = turn(payload_b)
    mine = reference_spectrum(sent_a)
    other = swap_cores(mine)
    first_rims, crossed_a = lax.optimization_barrier((first_rims, crossed(sent_a, mine, other)))
    back_a = turn(crossed_a)
    first_strips = swap_strips([rim[slots] for rim in first_rims])

    (logs,) = join(initial, first_strips, first_rims)
    total = (logs, swap_cores(logs))

    def updated_rows(at):
        window = [lax.slice_in_dim(part, at, at + ROWS, axis=1) for part in (initial, *total)]
        return (window[0] * jnp.exp(window[1] + window[2])).astype(BF16)

    strips = [updated_rows(at) for at in (0, ROWS, rows - 2 * ROWS, rows - ROWS)]
    rims = send_rims(own_strip(strips[0], strips[1]), own_strip(strips[3], strips[2]))
    crossed_b = crossed(sent_b, mine, other)
    strips = swap_strips(rims)
    back_b = turn(crossed_b)
    logs, estimate = join(initial, strips, first_rims, logs=total)
    swapped = swap_cores(logs)
    estimate = estimate * jnp.exp(logs + swapped)

    surfaces = last(back_a, 0, None)
    surfaces = last(back_b, chunk, surfaces)
    return estimate, surfaces


def solution(mesh):
    placed = (P("view", "parts", "gz", None), P("parts", "gz", None), P(), P(), P())

    return jax.shard_map(
        on_device,
        mesh=mesh,
        in_specs=placed,
        out_specs=(P("parts", "gz", None), P("view", "parts", "gz", None)),
        check_vma=False,
    )
```

```python
import functools
import math

import jax
import jax.numpy as jnp
import ml_dtypes
import numpy as np
from jax import lax
from jax.experimental import pallas as pl
from jax.experimental.pallas import tpu as pltpu
from jax.sharding import PartitionSpec as P


TAPS = 15
HALF = TAPS // 2
ROWS = 8
MID = 1.099609375


F32 = jnp.float32
BF16 = jnp.bfloat16


def dot(a, b):
    return jnp.dot(a, b, preferred_element_type=F32)


def dot_t(a, b):
    return lax.dot_general(a, b, (((1,), (1,)), ((), ())), preferred_element_type=F32)


def split(value):
    high = value.astype(BF16)
    return high, (value - high.astype(F32)).astype(BF16)


def np_split(table):
    high = table.astype(ml_dtypes.bfloat16)
    low = (table - high.astype(np.float64)).astype(ml_dtypes.bfloat16)
    return high, low


def side_by_side(table):
    return jnp.asarray(np.concatenate(np_split(table), 1))


def depth_order(depth):
    order = [0, depth // 2]
    for m in range(1, depth // 2):
        order += [m, depth - m]
    return np.array(order)


def angle_table(rows, columns, length):
    return 2.0 * np.pi * ((rows[:, None] * columns[None, :]) % length) / length


def depth_transform(real, imag, orient):
    count = len(real)
    if count == 1:
        return real, imag
    if count == 2:
        return [real[0] + real[1], real[0] - real[1]], [imag[0] + imag[1], imag[0] - imag[1]]
    quarter = count // 4
    parts = [depth_transform(real[j::4], imag[j::4], orient) for j in range(4)]
    out_real, out_imag = [None] * count, [None] * count
    for k in range(quarter):
        turned_parts = []
        for j in range(4):
            part_real, part_imag = parts[j][0][k], parts[j][1][k]
            if j * k:
                angle = -orient * 2.0 * math.pi * j * k / count
                cos, sin = math.cos(angle), math.sin(angle)
                if 8 * j * k == count:
                    part_real, part_imag = (part_real + orient * part_imag) * cos, (part_imag - orient * part_real) * cos
                else:
                    part_real, part_imag = part_real * cos - part_imag * sin, part_real * sin + part_imag * cos
            turned_parts.append((part_real, part_imag))
        (ar, ai), (br, bi), (cr, ci), (dr, di) = turned_parts
        sum_ac, dif_ac = (ar + cr, ai + ci), (ar - cr, ai - ci)
        sum_bd, dif_bd = (br + dr, bi + di), (br - dr, bi - di)
        out_real[k], out_imag[k] = sum_ac[0] + sum_bd[0], sum_ac[1] + sum_bd[1]
        out_real[k + 2 * quarter], out_imag[k + 2 * quarter] = sum_ac[0] - sum_bd[0], sum_ac[1] - sum_bd[1]
        plus = (dif_ac[0] + dif_bd[1], dif_ac[1] - dif_bd[0])
        minus = (dif_ac[0] - dif_bd[1], dif_ac[1] + dif_bd[0])
        first_part, second_part = (plus, minus) if orient > 0 else (minus, plus)
        out_real[k + quarter], out_imag[k + quarter] = first_part
        out_real[k + 3 * quarter], out_imag[k + 3 * quarter] = second_part
    return out_real, out_imag


def forward_bound(depth, width):
    return 0.9005 * math.sqrt(depth * width)


def backward_bound(length):
    return 1.0005 * math.sqrt(length)


def code_scale(bound):
    return bound / 32767.0**2


def encode(value, bound):
    scaled = value * lax.rsqrt(jnp.abs(value) + 1e-30) * (32767.0 / math.sqrt(bound))
    return (scaled + jnp.where(value < 0.0, -0.5, 0.5)).astype(jnp.int32).astype(jnp.int16)


def decode(code):
    value = code.astype(jnp.int32).astype(F32)
    return value * jnp.abs(value)


def row_tables(length, depth, width):
    half = length // 2
    positions = np.arange(length)
    freqs = np.arange(half)
    angles = angle_table(positions, freqs, length)
    cos_part, sin_part = np.cos(angles), np.sin(angles)
    sin_part[:, 0] = 1.0 - 2.0 * (positions % 2)
    both = np.concatenate([cos_part, sin_part], 1) / math.sqrt(length)
    return side_by_side(both.T * code_scale(forward_bound(depth, width))), side_by_side(both)


def column_tables(width, depth, length):
    half = width // 2
    positions = np.arange(width)
    freqs = np.arange(half)
    angles = angle_table(positions, freqs, width)
    scale = 1.0 / math.sqrt(width * depth)
    cos_part = np.cos(angles)
    sin_part = -np.sin(angles)
    sin_part[:, 0] = 1.0 - 2.0 * (positions % 2)
    forward = np.concatenate([cos_part, sin_part], 1) * scale
    weights = np.where(freqs == 0, 1.0, 2.0)
    inverse = np.concatenate([cos_part * weights, sin_part * weights], 1).T * scale
    return side_by_side(forward), side_by_side(inverse * code_scale(backward_bound(length)))


def table_times(table, block):
    size = block.shape[0]
    high, low = split(block)
    return dot(table, jnp.concatenate([high, high], 0)) + dot(table[:, :size], low)


def replace_row(array, row):
    top = array[:ROWS]
    row_id = lax.broadcasted_iota(jnp.int32, top.shape, 0)
    return jnp.concatenate([jnp.where(row_id == 0, row[:1], top), array[ROWS:]], 0)


def rows_forward(table, plane):
    both = table_times(table, plane)
    count = both.shape[0] // 2
    half = both.shape[1] // 2
    cos_real, cos_imag = both[:count, :half], both[:count, half:]
    sin_real, sin_imag = both[count:, :half], both[count:, half:]
    above = (replace_row(cos_real + sin_imag, cos_real), replace_row(cos_imag - sin_real, cos_imag))
    below = (replace_row(cos_real - sin_imag, sin_real), replace_row(cos_imag + sin_real, sin_imag))
    return above, below


def rows_inverse(table, above, below):
    even_real = replace_row(above[0] + below[0], above[0])
    even_imag = replace_row(above[1] + below[1], above[1])
    odd_real = replace_row(below[1] - above[1], below[0])
    odd_imag = replace_row(above[0] - below[0], below[1])
    top = jnp.concatenate([even_real, even_imag], 1)
    bottom = jnp.concatenate([odd_real, odd_imag], 1)
    return table_times(table, jnp.concatenate([top, bottom], 0))


def ref_slot_of(map_ref):
    slot = jnp.int32(0)
    for at in range(1, map_ref.shape[0]):
        slot = jnp.where(map_ref[at] == 0, jnp.int32(at), slot)
    return slot


def first_kernel(map_ref, observed_ref, columns_ref, out_ref, spread_ref, turned_ref):
    depth, rows, width = observed_ref.shape[1:]
    half = width // 2
    groups, _, local_depth = out_ref.shape[:3]
    flat = observed_ref[0].reshape(depth * rows, width)
    table = columns_ref[...]
    spread = dot(flat, table[:, :width]) + dot(flat, table[:, width:])
    spread_ref[...] = spread.reshape(depth, rows, width)
    shift = MID * math.sqrt(width * depth)
    spots = depth_order(depth)
    lane = lax.broadcasted_iota(jnp.int32, (ROWS, half), 1)

    @pl.loop(0, rows // ROWS)
    def _(b):
        at = pl.ds(pl.multiple_of(b * ROWS, ROWS), ROWS)
        real = [spread_ref[z, at, :half] for z in range(depth)]
        imag = [spread_ref[z, at, half:] for z in range(depth)]
        real, imag = depth_transform(real, imag, 1)
        edge = lane == 0
        real[0] = jnp.where(edge, real[0] - shift, real[0])
        for k in range(1, depth // 2):
            n = depth - k
            zero_real, zero_imag = 0.5 * (real[k] + real[n]), 0.5 * (imag[k] - imag[n])
            top_real, top_imag = 0.5 * (imag[k] + imag[n]), 0.5 * (real[n] - real[k])
            real[k], imag[k] = jnp.where(edge, zero_real, real[k]), jnp.where(edge, zero_imag, imag[k])
            real[n], imag[n] = jnp.where(edge, top_real, real[n]), jnp.where(edge, top_imag, imag[n])
        for spot, k in enumerate(spots):
            turned_ref[spot, at, :half] = real[k]
            turned_ref[spot, at, half:] = imag[k]

    code = encode(turned_ref[...], forward_bound(depth, width))
    out_ref[:, 0] = code.reshape(groups, local_depth, rows, width)


def load_plane(in_ref, k):
    groups, _, _, rows, width = in_ref.shape
    return decode(in_ref[:, 0, k].reshape(groups * rows, width))


def edge_mask(shape, group_zero):
    row = lax.broadcasted_iota(jnp.int32, shape, 0)
    lane = lax.broadcasted_iota(jnp.int32, shape, 1)
    return (lane == 0) & (row > 0) & group_zero


def spectrum(table, plane, k, group_zero, depth):
    above, below = rows_forward(table, plane)
    if k == 0:
        shift = MID * math.sqrt(depth * plane.shape[0] * plane.shape[1])
        lane = lax.broadcasted_iota(jnp.int32, above[0].shape, 1)
        here = (lane[:1] == 0) & group_zero
        row = jnp.where(here, above[0][:1] + shift, above[0][:1])
        above = (replace_row(above[0], row), above[1])
    if k < 2:
        mask = edge_mask(above[0].shape, group_zero)
        zero = (0.5 * (above[0] + below[0]), 0.5 * (above[1] - below[1]))
        top = (0.5 * (above[1] + below[1]), 0.5 * (below[0] - above[0]))
        above = tuple(jnp.where(mask, new, old) for new, old in zip(zero, above))
        below = tuple(jnp.where(mask, new, old) for new, old in zip(top, below))
    return above, below


def spectrum_kernel(place_ref, in_ref, rows_ref, out_ref):
    group_zero = place_ref[1] == 0
    groups, _, local_depth, _, width = in_ref.shape
    depth = groups * local_depth
    half = width // 2
    table = rows_ref[...]
    for k in range(local_depth):
        above, below = spectrum(table, load_plane(in_ref, k), k, group_zero, depth)
        count = above[0].shape[0]
        out_ref[k, :count, :half] = above[0]
        out_ref[k, :count, half:] = above[1]
        out_ref[k, count:, :half] = below[0]
        out_ref[k, count:, half:] = below[1]


def root(value):
    return value * lax.rsqrt(jnp.maximum(value, 1e-30))


def cross_of(value, ref):
    real, imag = value
    ref_real, ref_imag = ref
    power = (real * real + imag * imag) * (ref_real * ref_real + ref_imag * ref_imag)
    scale = 1.0 / (root(power) + 1.0)
    return (real * ref_real + imag * ref_imag) * scale, (imag * ref_real - real * ref_imag) * scale


def cross_of_real(value, ref):
    product = value * ref
    return product / (jnp.abs(product) + 1.0)


def cross_plane(value, ref, k, group_zero):
    crossed = cross_of(value, ref)
    if k < 2:
        lane = lax.broadcasted_iota(jnp.int32, (1, value[0].shape[1]), 1)
        here = (lane == 0) & group_zero
        parts = []
        for at in range(2):
            row = jnp.where(here, cross_of_real(value[at][:1], ref[at][:1]), crossed[at][:1])
            parts.append(replace_row(crossed[at], row))
        crossed = tuple(parts)
    return crossed


def cross_kernel(map_ref, place_ref, in_ref, rows_ref, back_ref, mine_ref, other_ref, out_ref):
    groups, _, local_depth, rows, width = in_ref.shape
    slots = map_ref.shape[0] // 2
    holds_ref = ref_slot_of(map_ref) // slots == place_ref[0]
    group_zero = place_ref[1] == 0
    depth = groups * local_depth
    half = width // 2
    length = groups * rows
    count = length // 2
    bound = backward_bound(length)
    table = rows_ref[...]
    for k in range(local_depth):
        above, below = spectrum(table, load_plane(in_ref, k), k, group_zero, depth)
        ref = jnp.where(holds_ref, mine_ref[k], other_ref[k])
        above = cross_plane(above, (ref[:count, :half], ref[:count, half:]), k, group_zero)
        below = cross_plane(below, (ref[count:, :half], ref[count:, half:]), k, group_zero)
        if k < 2:
            mask = edge_mask(above[0].shape, group_zero)
            plus = (above[0] - below[1], above[1] + below[0])
            minus = (above[0] + below[1], below[0] - above[1])
            above = tuple(jnp.where(mask, new, old) for new, old in zip(plus, above))
            below = tuple(jnp.where(mask, new, old) for new, old in zip(minus, below))
        back = rows_inverse(back_ref[...], above, below)
        out_ref[:, 0, k] = encode(back, bound).reshape(groups, rows, width)


def last_kernel(map_ref, in_ref, columns_ref, *rest):
    out_ref, turned_ref, spread_ref = rest[-3:]
    groups, _, local_depth, rows, width = in_ref.shape
    depth = groups * local_depth
    half = width // 2
    table = columns_ref[...]
    spots = depth_order(depth)
    value = decode(in_ref[:, 0])
    turned_ref[...] = value.reshape(depth, rows, width)

    @pl.loop(0, rows // ROWS)
    def _(b):
        at = pl.ds(pl.multiple_of(b * ROWS, ROWS), ROWS)
        real, imag = [None] * depth, [None] * depth
        for spot, k in enumerate(spots):
            real[k] = turned_ref[spot, at, :half]
            imag[k] = turned_ref[spot, at, half:]
        edge = lax.broadcasted_iota(jnp.int32, (ROWS, half), 1) == 0
        for k in range(1, depth // 2):
            n = depth - k
            plus = (real[k] - imag[n], imag[k] + real[n])
            minus = (real[k] + imag[n], real[n] - imag[k])
            real[k], imag[k] = jnp.where(edge, plus[0], real[k]), jnp.where(edge, plus[1], imag[k])
            real[n], imag[n] = jnp.where(edge, minus[0], real[n]), jnp.where(edge, minus[1], imag[n])
        real, imag = depth_transform(real, imag, -1)
        for z in range(depth):
            spread_ref[z, at, :half] = real[z]
            spread_ref[z, at, half:] = imag[z]

    high, low = split(spread_ref[...].reshape(depth * rows, width))
    cells = dot(high, table[:, :width]) + dot(high, table[:, width:]) + dot(low, table[:, :width])
    out_ref[0] = cells.reshape(depth, rows, width)


def pick_tap(psf_ref, view, axis, index):
    value = jnp.zeros(index.shape, F32)
    for j in range(TAPS):
        value = jnp.where(index == j, psf_ref[view, axis, j], value)
    return value


def filter_kernel(place_ref, map_ref, shift_ref, psf_ref, forward_ref, backward_ref, columns_ref):
    size = forward_ref.shape[1]
    width = columns_ref.shape[1]
    depth = size // ROWS
    view = map_ref[place_ref[0] * pl.num_programs(0) + pl.program_id(0)]
    depth_shift = shift_ref[view, 0]
    column_shift = shift_ref[view, 1]
    at_out = lax.broadcasted_iota(jnp.int32, (depth, size), 0)
    at_in = lax.broadcasted_iota(jnp.int32, (depth, size), 1) // ROWS
    row = lax.broadcasted_iota(jnp.int32, (ROWS, size), 0)
    cell = lax.broadcasted_iota(jnp.int32, (ROWS, size), 1) % ROWS
    for out_ref, orient in ((forward_ref, 1), (backward_ref, -1)):
        depth_part = pick_tap(psf_ref, view, 0, orient * (at_in - at_out) + HALF - depth_shift)
        for c in range(3):
            reach = c * ROWS + cell - ROWS - row
            row_part = pick_tap(psf_ref, view, 1, orient * reach + HALF)
            block = depth_part[:, None, :] * row_part[None, :, :]
            out_ref[0, :, c * size : (c + 1) * size] = block.reshape(size, size).astype(BF16)
    source = lax.broadcasted_iota(jnp.int32, (width, width), 0)
    target = lax.broadcasted_iota(jnp.int32, (width, width), 1)
    picked = pick_tap(psf_ref, view, 2, source - target + HALF - column_shift)
    columns_ref[0] = picked.astype(BF16)


def join_kernel(
    views,
    updated,
    *refs,
):
    if updated:
        mine_ref, other_ref, *refs = refs
    (
    place_ref,
    estimate_ref,
    strips_ref,
    swapped_ref,
    observed_ref,
    seen_below_ref,
    seen_above_ref,
    forward_ref,
    backward_ref,
    columns_ref,
    out_ref,
    *refs,
    ) = refs
    if updated:
        now_ref, *refs = refs
    else:
        now_ref = estimate_ref
    cells_ref, mixed_ref, blurred_ref, ratio_ref, product_ref = refs
    depth, rows, width = estimate_ref.shape
    size = depth * ROWS
    blocks = rows // ROWS
    slots = forward_ref.shape[0]
    step = pl.program_id(0)

    @pl.when(step == 0)
    def _():
        if updated:
            logs = mine_ref[...] + other_ref[...]
            now_ref[...] = estimate_ref[...] * jnp.exp(logs.reshape(depth, rows, width))
        first_core = place_ref[0] == 0
        for side, near, far in ((0, 1, 0), (1, blocks + 2, blocks + 3)):
            own = strips_ref[side].astype(F32).reshape(size, width)
            swapped = swapped_ref[side].astype(F32).reshape(size, width)
            cells_ref[near] = jnp.where(first_core, own, swapped).astype(BF16)
            cells_ref[far] = jnp.where(first_core, swapped, own).astype(BF16)
        for b in range(blocks):
            piece = now_ref[:, b * ROWS : (b + 1) * ROWS].reshape(size, width)
            cells_ref[b + 2] = piece.astype(BF16)
        product_ref[...] = jnp.ones_like(product_ref)

        @pl.loop(0, blocks + 2)
        def _(b):
            window = cells_ref[pl.ds(b, 3)].reshape(3 * size, width)
            mixed = dot(forward_ref[...].reshape(slots * size, 3 * size), window)
            mixed_ref[:, b] = mixed.astype(BF16).reshape(slots, size, width)

    columns = columns_ref[0]
    blurred = dot(mixed_ref[step].reshape((blocks + 2) * size, width), columns)
    blurred_ref[...] = blurred.reshape(blocks + 2, size, width)
    for b in range(blocks + 2):
        if b == 0:
            seen = seen_below_ref[0].astype(F32)
        elif b == blocks + 1:
            seen = seen_above_ref[0].astype(F32)
        else:
            seen = observed_ref[0, :, (b - 1) * ROWS : b * ROWS].astype(F32)
        seen = seen.reshape(size, width)
        ratio = jnp.where(seen > 0.0, seen / blurred_ref[b], 0.0)
        ratio_ref[b] = ratio.astype(BF16)
    ratio = dot_t(ratio_ref[...].reshape((blocks + 2) * size, width), columns)
    ratio_ref[...] = ratio.astype(BF16).reshape(blocks + 2, size, width)
    for b in range(blocks):
        window = ratio_ref[b : b + 3].reshape(3 * size, width)
        product_ref[b] = product_ref[b] * dot(backward_ref[0], window)

    @pl.when(step == slots - 1)
    def _():
        for b in range(blocks):
            logs = jnp.log(product_ref[b]) * (1.0 / views)
            out_ref[:, b * ROWS : (b + 1) * ROWS] = logs.reshape(depth, ROWS, width)


def whole(shape):
    return pl.BlockSpec(shape, lambda *_: (0,) * len(shape))


def cost(flops, moved):
    return pl.CostEstimate(flops=int(flops), bytes_accessed=int(moved), transcendentals=0)


def turn(payload):
    return lax.all_to_all(payload, "gz", split_axis=0, concat_axis=0, tiled=True)


def own_strip(near, far):
    return jnp.where(lax.axis_index("view") == 0, near, far)


def send_rims(low, high):
    count = lax.axis_size("gz")
    below = lax.ppermute(high, "gz", [(i, i + 1) for i in range(count - 1)])
    above = lax.ppermute(low, "gz", [(i + 1, i) for i in range(count - 1)])
    return below, above


def swap_cores(field):
    count = lax.axis_size("view")
    return lax.ppermute(field, "view", [(i, (i + 1) % count) for i in range(count)])


def swap_strips(strips):
    mine = jnp.stack(strips)
    return mine, swap_cores(mine)


def on_device(observed, initial, psf_taps, view_shifts, view_map):
    slots, depth, rows, width = observed.shape
    views = view_map.shape[0]
    groups = lax.axis_size("gz")
    length = groups * rows
    local_depth = depth // groups
    size = depth * ROWS
    blocks = rows // ROWS
    place = jnp.stack([lax.axis_index("view"), lax.axis_index("gz")]).astype(jnp.int32)

    columns_forward, columns_inverse = column_tables(width, depth, length)
    row_turn, row_back = row_tables(length, depth, width)

    strips = [initial[:, at : at + ROWS].astype(BF16) for at in (0, ROWS, rows - 2 * ROWS, rows - ROWS)]
    low = jnp.concatenate([observed[:, :, :ROWS], own_strip(strips[0], strips[1])[None]], 0)
    high = jnp.concatenate([observed[:, :, rows - ROWS :], own_strip(strips[3], strips[2])[None]], 0)
    first_rims = send_rims(low, high)

    chunk = slots // 2
    payload_block = (groups, 1, local_depth, rows, width)
    payload_shape = (groups, chunk, local_depth, rows, width)
    payload_bytes = 4 * depth * rows * width * chunk
    volume = depth * rows * width

    def first(start):
        return pl.pallas_call(
            first_kernel,
            grid_spec=pltpu.PrefetchScalarGridSpec(
                num_scalar_prefetch=1,
                grid=(chunk,),
                in_specs=[
                    pl.BlockSpec((1, depth, rows, width), lambda s, m: (lax.rem(s + start + ref_slot_of(m), slots), 0, 0, 0)),
                    whole(columns_forward.shape),
                ],
                out_specs=pl.BlockSpec(payload_block, lambda *a: (0, a[0], 0, 0, 0)),
                scratch_shapes=[pltpu.VMEM((depth, rows, width), F32)] * 2,
            ),
            out_shape=jax.ShapeDtypeStruct(payload_shape, jnp.int16),
            compiler_params=pltpu.CompilerParams(vmem_limit_bytes=28 * 1024 * 1024),
            cost_estimate=cost(2 * chunk * volume * 8 * width, payload_bytes),
            name="first",
        )(view_map, observed, columns_forward)

    spectrum_shape = (local_depth, length, width)
    row_flops = 2 * local_depth * length * width * 3 * length

    def reference_spectrum(payload):
        return pl.pallas_call(
            spectrum_kernel,
            grid_spec=pltpu.PrefetchScalarGridSpec(
                num_scalar_prefetch=1,
                grid=(1,),
                in_specs=[
                    pl.BlockSpec(payload_block, lambda *_: (0, 0, 0, 0, 0)),
                    whole(row_turn.shape),
                ],
                out_specs=whole(spectrum_shape),
            ),
            out_shape=jax.ShapeDtypeStruct(spectrum_shape, F32),
            compiler_params=pltpu.CompilerParams(vmem_limit_bytes=28 * 1024 * 1024),
            cost_estimate=cost(row_flops, 6 * volume),
            name="spectrum",
        )(place, payload, row_turn)

    def crossed(payload, mine, other):
        return pl.pallas_call(
            cross_kernel,
            grid_spec=pltpu.PrefetchScalarGridSpec(
                num_scalar_prefetch=2,
                grid=(chunk,),
                in_specs=[
                    pl.BlockSpec(payload_block, lambda *a: (0, a[0], 0, 0, 0)),
                    whole(row_turn.shape),
                    whole(row_back.shape),
                    whole(spectrum_shape),
                    whole(spectrum_shape),
                ],
                out_specs=pl.BlockSpec(payload_block, lambda *a: (0, a[0], 0, 0, 0)),
            ),
            out_shape=jax.ShapeDtypeStruct(payload_shape, jnp.int16),
            compiler_params=pltpu.CompilerParams(vmem_limit_bytes=28 * 1024 * 1024),
            cost_estimate=cost(2 * row_flops * chunk, payload_bytes + 10 * volume),
            name="cross",
        )(view_map, place, payload, row_turn, row_back, mine, other)

    def last(payload, start, partial):
        specs = [
            pl.BlockSpec(payload_block, lambda *a: (0, a[0], 0, 0, 0)),
            whole(columns_inverse.shape),
        ]
        operands = [view_map, payload, columns_inverse]
        aliases = {}
        if partial is not None:
            specs.append(pl.BlockSpec(memory_space=pl.ANY))
            aliases = {len(operands): 0}
            operands.append(partial)
        return pl.pallas_call(
            last_kernel,
            grid_spec=pltpu.PrefetchScalarGridSpec(
                num_scalar_prefetch=1,
                grid=(chunk,),
                in_specs=specs,
                out_specs=pl.BlockSpec((1, depth, rows, width), lambda s, m: (lax.rem(s + start + ref_slot_of(m), slots), 0, 0, 0)),
                scratch_shapes=[pltpu.VMEM((depth, rows, width), F32)] * 2,
            ),
            out_shape=jax.ShapeDtypeStruct((slots, depth, rows, width), F32),
            input_output_aliases=aliases,
            compiler_params=pltpu.CompilerParams(vmem_limit_bytes=28 * 1024 * 1024),
            cost_estimate=cost(2 * chunk * volume * 9 * width, payload_bytes * 1.5),
            name="last",
        )(*operands)

    def filters():
        smem = pl.BlockSpec(memory_space=pltpu.SMEM)
        return pl.pallas_call(
            filter_kernel,
            grid=(slots,),
            in_specs=[smem] * 4,
            out_specs=[
                pl.BlockSpec((1, size, 3 * size), lambda s: (s, 0, 0)),
                pl.BlockSpec((1, size, 3 * size), lambda s: (s, 0, 0)),
                pl.BlockSpec((1, width, width), lambda s: (s, 0, 0)),
            ],
            out_shape=[
                jax.ShapeDtypeStruct((slots, size, 3 * size), BF16),
                jax.ShapeDtypeStruct((slots, size, 3 * size), BF16),
                jax.ShapeDtypeStruct((slots, width, width), BF16),
            ],
            compiler_params=pltpu.CompilerParams(vmem_limit_bytes=28 * 1024 * 1024),
            cost_estimate=cost(slots * size * size * 60, slots * size * size * 14),
            name="filters",
        )(place, view_map, view_shifts, psf_taps)

    forward, backward, columns = filters()

    def join(estimate, strips, rims, logs=None):
        def slot_block(shape):
            return pl.BlockSpec((1,) + shape, lambda s: (s,) + (0,) * len(shape))

        updated = logs is not None
        field = jax.ShapeDtypeStruct((depth, rows, width), F32)
        extra_specs = []
        if updated:
            extra_specs = [whole((depth, rows, width))] * 2
        return pl.pallas_call(
            functools.partial(join_kernel, views, updated),
            grid=(slots,),
            in_specs=extra_specs
            + [
                pl.BlockSpec(memory_space=pltpu.SMEM),
                whole((depth, rows, width)),
                whole((2, depth, ROWS, width)),
                whole((2, depth, ROWS, width)),
                slot_block((depth, rows, width)),
                slot_block((depth, ROWS, width)),
                slot_block((depth, ROWS, width)),
                whole((slots, size, 3 * size)),
                slot_block((size, 3 * size)),
                slot_block((width, width)),
            ],
            out_specs=[whole((depth, rows, width))] * (1 + updated),
            out_shape=[field] * (1 + updated),
            scratch_shapes=[
                pltpu.VMEM((blocks + 4, size, width), BF16),
                pltpu.VMEM((slots, blocks + 2, size, width), BF16),
                pltpu.VMEM((blocks + 2, size, width), F32),
                pltpu.VMEM((blocks + 2, size, width), BF16),
                pltpu.VMEM((blocks, size, width), F32),
            ],
            compiler_params=pltpu.CompilerParams(vmem_limit_bytes=28 * 1024 * 1024),
            cost_estimate=cost(2 * slots * size * width * ((blocks + 2) * (3 * size + 2 * width) + blocks * 3 * size), 12e6),
            name="join",
        )(*(logs or ()), place, estimate, *strips, observed, *rims, forward, backward, columns)

    sent_a = turn(first(0))
    payload_b = first(chunk)
    sent_b = turn(payload_b)
    mine = reference_spectrum(sent_a)
    other = swap_cores(mine)
    first_rims, crossed_a = lax.optimization_barrier((first_rims, crossed(sent_a, mine, other)))
    back_a = turn(crossed_a)
    first_strips = swap_strips([rim[slots] for rim in first_rims])

    (logs,) = join(initial, first_strips, first_rims)
    total = (logs, swap_cores(logs))

    def updated_rows(at):
        window = [lax.slice_in_dim(part, at, at + ROWS, axis=1) for part in (initial, *total)]
        return (window[0] * jnp.exp(window[1] + window[2])).astype(BF16)

    strips = [updated_rows(at) for at in (0, ROWS, rows - 2 * ROWS, rows - ROWS)]
    rims = send_rims(own_strip(strips[0], strips[1]), own_strip(strips[3], strips[2]))
    crossed_b = crossed(sent_b, mine, other)
    strips = swap_strips(rims)
    back_b = turn(crossed_b)
    logs, estimate = join(initial, strips, first_rims, logs=total)
    swapped = swap_cores(logs)
    estimate = estimate * jnp.exp(logs + swapped)

    surfaces = last(back_a, 0, None)
    surfaces = last(back_b, chunk, surfaces)
    return estimate, surfaces


def solution(mesh):
    placed = (P("view", "parts", "gz", None), P("parts", "gz", None), P(), P(), P())

    return jax.shard_map(
        on_device,
        mesh=mesh,
        in_specs=placed,
        out_specs=(P("parts", "gz", None), P("view", "parts", "gz", None)),
        check_vma=False,
    )
```

```python
import functools
import math

import jax
import jax.numpy as jnp
import ml_dtypes
import numpy as np
from jax import lax
from jax.experimental import pallas as pl
from jax.experimental.pallas import tpu as pltpu
from jax.sharding import PartitionSpec as P


TAPS = 15
HALF = TAPS // 2
ROWS = 8
MID = 1.099609375


F32 = jnp.float32
BF16 = jnp.bfloat16


def dot(a, b):
    return jnp.dot(a, b, preferred_element_type=F32)


def dot_t(a, b):
    return lax.dot_general(a, b, (((1,), (1,)), ((), ())), preferred_element_type=F32)


def split(value):
    high = value.astype(BF16)
    return high, (value - high.astype(F32)).astype(BF16)


def np_split(table):
    high = table.astype(ml_dtypes.bfloat16)
    low = (table - high.astype(np.float64)).astype(ml_dtypes.bfloat16)
    return high, low


def side_by_side(table):
    return jnp.asarray(np.concatenate(np_split(table), 1))


def depth_order(depth):
    order = [0, depth // 2]
    for m in range(1, depth // 2):
        order += [m, depth - m]
    return np.array(order)


def angle_table(rows, columns, length):
    return 2.0 * np.pi * ((rows[:, None] * columns[None, :]) % length) / length


def depth_transform(real, imag, orient):
    count = len(real)
    if count == 1:
        return real, imag
    if count == 2:
        return [real[0] + real[1], real[0] - real[1]], [imag[0] + imag[1], imag[0] - imag[1]]
    quarter = count // 4
    parts = [depth_transform(real[j::4], imag[j::4], orient) for j in range(4)]
    out_real, out_imag = [None] * count, [None] * count
    for k in range(quarter):
        turned_parts = []
        for j in range(4):
            part_real, part_imag = parts[j][0][k], parts[j][1][k]
            if j * k:
                angle = -orient * 2.0 * math.pi * j * k / count
                cos, sin = math.cos(angle), math.sin(angle)
                if 8 * j * k == count:
                    part_real, part_imag = (part_real + orient * part_imag) * cos, (part_imag - orient * part_real) * cos
                else:
                    part_real, part_imag = part_real * cos - part_imag * sin, part_real * sin + part_imag * cos
            turned_parts.append((part_real, part_imag))
        (ar, ai), (br, bi), (cr, ci), (dr, di) = turned_parts
        sum_ac, dif_ac = (ar + cr, ai + ci), (ar - cr, ai - ci)
        sum_bd, dif_bd = (br + dr, bi + di), (br - dr, bi - di)
        out_real[k], out_imag[k] = sum_ac[0] + sum_bd[0], sum_ac[1] + sum_bd[1]
        out_real[k + 2 * quarter], out_imag[k + 2 * quarter] = sum_ac[0] - sum_bd[0], sum_ac[1] - sum_bd[1]
        plus = (dif_ac[0] + dif_bd[1], dif_ac[1] - dif_bd[0])
        minus = (dif_ac[0] - dif_bd[1], dif_ac[1] + dif_bd[0])
        first_part, second_part = (plus, minus) if orient > 0 else (minus, plus)
        out_real[k + quarter], out_imag[k + quarter] = first_part
        out_real[k + 3 * quarter], out_imag[k + 3 * quarter] = second_part
    return out_real, out_imag


def forward_bound(depth, width):
    return 0.9005 * math.sqrt(depth * width)


def backward_bound(length):
    return 1.0005 * math.sqrt(length)


def code_scale(bound):
    return bound / 32767.0**2


def encode(value, bound):
    scaled = value * lax.rsqrt(jnp.abs(value) + 1e-30) * (32767.0 / math.sqrt(bound))
    return (scaled + jnp.where(value < 0.0, -0.5, 0.5)).astype(jnp.int32).astype(jnp.int16)


def decode(code):
    value = code.astype(jnp.int32).astype(F32)
    return value * jnp.abs(value)


def row_tables(length, depth, width):
    half = length // 2
    positions = np.arange(length)
    freqs = np.arange(half)
    angles = angle_table(positions, freqs, length)
    cos_part, sin_part = np.cos(angles), np.sin(angles)
    sin_part[:, 0] = 1.0 - 2.0 * (positions % 2)
    both = np.concatenate([cos_part, sin_part], 1) / math.sqrt(length)
    return side_by_side(both.T * code_scale(forward_bound(depth, width))), side_by_side(both)


def column_tables(width, depth, length):
    half = width // 2
    positions = np.arange(width)
    freqs = np.arange(half)
    angles = angle_table(positions, freqs, width)
    scale = 1.0 / math.sqrt(width * depth)
    cos_part = np.cos(angles)
    sin_part = -np.sin(angles)
    sin_part[:, 0] = 1.0 - 2.0 * (positions % 2)
    forward = np.concatenate([cos_part, sin_part], 1) * scale
    weights = np.where(freqs == 0, 1.0, 2.0)
    inverse = np.concatenate([cos_part * weights, sin_part * weights], 1).T * scale
    return side_by_side(forward), side_by_side(inverse * code_scale(backward_bound(length)))


def table_times(table, block):
    size = block.shape[0]
    high, low = split(block)
    return dot(table, jnp.concatenate([high, high], 0)) + dot(table[:, :size], low)


def replace_row(array, row):
    top = array[:ROWS]
    row_id = lax.broadcasted_iota(jnp.int32, top.shape, 0)
    return jnp.concatenate([jnp.where(row_id == 0, row[:1], top), array[ROWS:]], 0)


def rows_forward(table, plane):
    both = table_times(table, plane)
    count = both.shape[0] // 2
    half = both.shape[1] // 2
    cos_real, cos_imag = both[:count, :half], both[:count, half:]
    sin_real, sin_imag = both[count:, :half], both[count:, half:]
    above = (replace_row(cos_real + sin_imag, cos_real), replace_row(cos_imag - sin_real, cos_imag))
    below = (replace_row(cos_real - sin_imag, sin_real), replace_row(cos_imag + sin_real, sin_imag))
    return above, below


def rows_inverse(table, above, below):
    even_real = replace_row(above[0] + below[0], above[0])
    even_imag = replace_row(above[1] + below[1], above[1])
    odd_real = replace_row(below[1] - above[1], below[0])
    odd_imag = replace_row(above[0] - below[0], below[1])
    top = jnp.concatenate([even_real, even_imag], 1)
    bottom = jnp.concatenate([odd_real, odd_imag], 1)
    return table_times(table, jnp.concatenate([top, bottom], 0))


def ref_slot_of(map_ref):
    slot = jnp.int32(0)
    for at in range(1, map_ref.shape[0]):
        slot = jnp.where(map_ref[at] == 0, jnp.int32(at), slot)
    return slot


def first_kernel(map_ref, observed_ref, columns_ref, out_ref, spread_ref, turned_ref):
    depth, rows, width = observed_ref.shape[1:]
    half = width // 2
    groups, _, local_depth = out_ref.shape[:3]
    flat = observed_ref[0].reshape(depth * rows, width)
    table = columns_ref[...]
    spread = dot(flat, table[:, :width]) + dot(flat, table[:, width:])
    spread_ref[...] = spread.reshape(depth, rows, width)
    shift = MID * math.sqrt(width * depth)
    spots = depth_order(depth)
    lane = lax.broadcasted_iota(jnp.int32, (ROWS, half), 1)

    @pl.loop(0, rows // ROWS)
    def _(b):
        at = pl.ds(pl.multiple_of(b * ROWS, ROWS), ROWS)
        real = [spread_ref[z, at, :half] for z in range(depth)]
        imag = [spread_ref[z, at, half:] for z in range(depth)]
        real, imag = depth_transform(real, imag, 1)
        edge = lane == 0
        real[0] = jnp.where(edge, real[0] - shift, real[0])
        for k in range(1, depth // 2):
            n = depth - k
            zero_real, zero_imag = 0.5 * (real[k] + real[n]), 0.5 * (imag[k] - imag[n])
            top_real, top_imag = 0.5 * (imag[k] + imag[n]), 0.5 * (real[n] - real[k])
            real[k], imag[k] = jnp.where(edge, zero_real, real[k]), jnp.where(edge, zero_imag, imag[k])
            real[n], imag[n] = jnp.where(edge, top_real, real[n]), jnp.where(edge, top_imag, imag[n])
        for spot, k in enumerate(spots):
            turned_ref[spot, at, :half] = real[k]
            turned_ref[spot, at, half:] = imag[k]

    code = encode(turned_ref[...], forward_bound(depth, width))
    out_ref[:, 0] = code.reshape(groups, local_depth, rows, width)


def load_plane(in_ref, k):
    groups, _, _, rows, width = in_ref.shape
    return decode(in_ref[:, 0, k].reshape(groups * rows, width))


def edge_mask(shape, group_zero):
    row = lax.broadcasted_iota(jnp.int32, shape, 0)
    lane = lax.broadcasted_iota(jnp.int32, shape, 1)
    return (lane == 0) & (row > 0) & group_zero


def spectrum(table, plane, k, group_zero, depth):
    above, below = rows_forward(table, plane)
    if k == 0:
        shift = MID * math.sqrt(depth * plane.shape[0] * plane.shape[1])
        lane = lax.broadcasted_iota(jnp.int32, above[0].shape, 1)
        here = (lane[:1] == 0) & group_zero
        row = jnp.where(here, above[0][:1] + shift, above[0][:1])
        above = (replace_row(above[0], row), above[1])
    if k < 2:
        mask = edge_mask(above[0].shape, group_zero)
        zero = (0.5 * (above[0] + below[0]), 0.5 * (above[1] - below[1]))
        top = (0.5 * (above[1] + below[1]), 0.5 * (below[0] - above[0]))
        above = tuple(jnp.where(mask, new, old) for new, old in zip(zero, above))
        below = tuple(jnp.where(mask, new, old) for new, old in zip(top, below))
    return above, below


def spectrum_kernel(place_ref, in_ref, rows_ref, out_ref):
    group_zero = place_ref[1] == 0
    groups, _, local_depth, _, width = in_ref.shape
    depth = groups * local_depth
    half = width // 2
    table = rows_ref[...]
    for k in range(local_depth):
        above, below = spectrum(table, load_plane(in_ref, k), k, group_zero, depth)
        count = above[0].shape[0]
        out_ref[k, :count, :half] = above[0]
        out_ref[k, :count, half:] = above[1]
        out_ref[k, count:, :half] = below[0]
        out_ref[k, count:, half:] = below[1]


def root(value):
    return value * lax.rsqrt(jnp.maximum(value, 1e-30))


def cross_of(value, ref):
    real, imag = value
    ref_real, ref_imag = ref
    power = (real * real + imag * imag) * (ref_real * ref_real + ref_imag * ref_imag)
    scale = 1.0 / (root(power) + 1.0)
    return (real * ref_real + imag * ref_imag) * scale, (imag * ref_real - real * ref_imag) * scale


def cross_of_real(value, ref):
    product = value * ref
    return product / (jnp.abs(product) + 1.0)


def cross_plane(value, ref, k, group_zero):
    crossed = cross_of(value, ref)
    if k < 2:
        lane = lax.broadcasted_iota(jnp.int32, (1, value[0].shape[1]), 1)
        here = (lane == 0) & group_zero
        parts = []
        for at in range(2):
            row = jnp.where(here, cross_of_real(value[at][:1], ref[at][:1]), crossed[at][:1])
            parts.append(replace_row(crossed[at], row))
        crossed = tuple(parts)
    return crossed


def cross_kernel(map_ref, place_ref, in_ref, rows_ref, back_ref, mine_ref, other_ref, out_ref):
    groups, _, local_depth, rows, width = in_ref.shape
    slots = map_ref.shape[0] // 2
    holds_ref = ref_slot_of(map_ref) // slots == place_ref[0]
    group_zero = place_ref[1] == 0
    depth = groups * local_depth
    half = width // 2
    length = groups * rows
    count = length // 2
    bound = backward_bound(length)
    table = rows_ref[...]
    for k in range(local_depth):
        above, below = spectrum(table, load_plane(in_ref, k), k, group_zero, depth)
        ref = jnp.where(holds_ref, mine_ref[k], other_ref[k])
        above = cross_plane(above, (ref[:count, :half], ref[:count, half:]), k, group_zero)
        below = cross_plane(below, (ref[count:, :half], ref[count:, half:]), k, group_zero)
        if k < 2:
            mask = edge_mask(above[0].shape, group_zero)
            plus = (above[0] - below[1], above[1] + below[0])
            minus = (above[0] + below[1], below[0] - above[1])
            above = tuple(jnp.where(mask, new, old) for new, old in zip(plus, above))
            below = tuple(jnp.where(mask, new, old) for new, old in zip(minus, below))
        back = rows_inverse(back_ref[...], above, below)
        out_ref[:, 0, k] = encode(back, bound).reshape(groups, rows, width)


def last_kernel(map_ref, in_ref, columns_ref, *rest):
    out_ref, turned_ref, spread_ref = rest[-3:]
    groups, _, local_depth, rows, width = in_ref.shape
    depth = groups * local_depth
    half = width // 2
    table = columns_ref[...]
    spots = depth_order(depth)
    value = decode(in_ref[:, 0])
    turned_ref[...] = value.reshape(depth, rows, width)

    @pl.loop(0, rows // ROWS)
    def _(b):
        at = pl.ds(pl.multiple_of(b * ROWS, ROWS), ROWS)
        real, imag = [None] * depth, [None] * depth
        for spot, k in enumerate(spots):
            real[k] = turned_ref[spot, at, :half]
            imag[k] = turned_ref[spot, at, half:]
        edge = lax.broadcasted_iota(jnp.int32, (ROWS, half), 1) == 0
        for k in range(1, depth // 2):
            n = depth - k
            plus = (real[k] - imag[n], imag[k] + real[n])
            minus = (real[k] + imag[n], real[n] - imag[k])
            real[k], imag[k] = jnp.where(edge, plus[0], real[k]), jnp.where(edge, plus[1], imag[k])
            real[n], imag[n] = jnp.where(edge, minus[0], real[n]), jnp.where(edge, minus[1], imag[n])
        real, imag = depth_transform(real, imag, -1)
        for z in range(depth):
            spread_ref[z, at, :half] = real[z]
            spread_ref[z, at, half:] = imag[z]

    high, low = split(spread_ref[...].reshape(depth * rows, width))
    cells = dot(high, table[:, :width]) + dot(high, table[:, width:]) + dot(low, table[:, :width])
    out_ref[0] = cells.reshape(depth, rows, width)


def pick_tap(psf_ref, view, axis, index):
    value = jnp.zeros(index.shape, F32)
    for j in range(TAPS):
        value = jnp.where(index == j, psf_ref[view, axis, j], value)
    return value


def filter_kernel(place_ref, map_ref, shift_ref, psf_ref, forward_ref, backward_ref, columns_ref):
    size = forward_ref.shape[1]
    width = columns_ref.shape[1]
    depth = size // ROWS
    view = map_ref[place_ref[0] * pl.num_programs(0) + pl.program_id(0)]
    depth_shift = shift_ref[view, 0]
    column_shift = shift_ref[view, 1]
    at_out = lax.broadcasted_iota(jnp.int32, (depth, size), 0)
    at_in = lax.broadcasted_iota(jnp.int32, (depth, size), 1) // ROWS
    row = lax.broadcasted_iota(jnp.int32, (ROWS, size), 0)
    cell = lax.broadcasted_iota(jnp.int32, (ROWS, size), 1) % ROWS
    for out_ref, orient in ((forward_ref, 1), (backward_ref, -1)):
        depth_part = pick_tap(psf_ref, view, 0, orient * (at_in - at_out) + HALF - depth_shift)
        for c in range(3):
            reach = c * ROWS + cell - ROWS - row
            row_part = pick_tap(psf_ref, view, 1, orient * reach + HALF)
            block = depth_part[:, None, :] * row_part[None, :, :]
            out_ref[0, :, c * size : (c + 1) * size] = block.reshape(size, size).astype(BF16)
    source = lax.broadcasted_iota(jnp.int32, (width, width), 0)
    target = lax.broadcasted_iota(jnp.int32, (width, width), 1)
    picked = pick_tap(psf_ref, view, 2, source - target + HALF - column_shift)
    columns_ref[0] = picked.astype(BF16)


def join_kernel(
    views,
    updated,
    *refs,
):
    if updated:
        mine_ref, other_ref, *refs = refs
    (
    place_ref,
    estimate_ref,
    strips_ref,
    swapped_ref,
    observed_ref,
    seen_below_ref,
    seen_above_ref,
    forward_ref,
    backward_ref,
    columns_ref,
    out_ref,
    *refs,
    ) = refs
    if updated:
        now_ref, *refs = refs
    else:
        now_ref = estimate_ref
    cells_ref, mixed_ref, blurred_ref, ratio_ref, product_ref = refs
    depth, rows, width = estimate_ref.shape
    size = depth * ROWS
    blocks = rows // ROWS
    slots = forward_ref.shape[0]
    step = pl.program_id(0)

    @pl.when(step == 0)
    def _():
        if updated:
            logs = mine_ref[...] + other_ref[...]
            now_ref[...] = estimate_ref[...] * jnp.exp(logs.reshape(depth, rows, width))
        first_core = place_ref[0] == 0
        for side, near, far in ((0, 1, 0), (1, blocks + 2, blocks + 3)):
            own = strips_ref[side].astype(F32).reshape(size, width)
            swapped = swapped_ref[side].astype(F32).reshape(size, width)
            cells_ref[near] = jnp.where(first_core, own, swapped).astype(BF16)
            cells_ref[far] = jnp.where(first_core, swapped, own).astype(BF16)
        for b in range(blocks):
            piece = now_ref[:, b * ROWS : (b + 1) * ROWS].reshape(size, width)
            cells_ref[b + 2] = piece.astype(BF16)
        product_ref[...] = jnp.ones_like(product_ref)

        @pl.loop(0, blocks + 2)
        def _(b):
            window = cells_ref[pl.ds(b, 3)].reshape(3 * size, width)
            mixed = dot(forward_ref[...].reshape(slots * size, 3 * size), window)
            mixed_ref[:, b] = mixed.astype(BF16).reshape(slots, size, width)

    columns = columns_ref[0]
    blurred = dot(mixed_ref[step].reshape((blocks + 2) * size, width), columns)
    blurred_ref[...] = blurred.reshape(blocks + 2, size, width)
    for b in range(blocks + 2):
        if b == 0:
            seen = seen_below_ref[0].astype(F32)
        elif b == blocks + 1:
            seen = seen_above_ref[0].astype(F32)
        else:
            seen = observed_ref[0, :, (b - 1) * ROWS : b * ROWS].astype(F32)
        seen = seen.reshape(size, width)
        ratio = jnp.where(seen > 0.0, seen / blurred_ref[b], 0.0)
        ratio_ref[b] = ratio.astype(BF16)
    ratio = dot_t(ratio_ref[...].reshape((blocks + 2) * size, width), columns)
    ratio_ref[...] = ratio.astype(BF16).reshape(blocks + 2, size, width)
    for b in range(blocks):
        window = ratio_ref[b : b + 3].reshape(3 * size, width)
        product_ref[b] = product_ref[b] * dot(backward_ref[0], window)

    @pl.when(step == slots - 1)
    def _():
        for b in range(blocks):
            logs = jnp.log(product_ref[b]) * (1.0 / views)
            out_ref[:, b * ROWS : (b + 1) * ROWS] = logs.reshape(depth, ROWS, width)


def whole(shape):
    return pl.BlockSpec(shape, lambda *_: (0,) * len(shape))


def cost(flops, moved):
    return pl.CostEstimate(flops=int(flops), bytes_accessed=int(moved), transcendentals=0)


def turn(payload):
    return lax.all_to_all(payload, "gz", split_axis=0, concat_axis=0, tiled=True)


def own_strip(near, far):
    return jnp.where(lax.axis_index("view") == 0, near, far)


def send_rims(low, high):
    count = lax.axis_size("gz")
    below = lax.ppermute(high, "gz", [(i, i + 1) for i in range(count - 1)])
    above = lax.ppermute(low, "gz", [(i + 1, i) for i in range(count - 1)])
    return below, above


def swap_cores(field):
    count = lax.axis_size("view")
    return lax.ppermute(field, "view", [(i, (i + 1) % count) for i in range(count)])


def swap_strips(strips):
    mine = jnp.stack(strips)
    return mine, swap_cores(mine)


def on_device(observed, initial, psf_taps, view_shifts, view_map):
    slots, depth, rows, width = observed.shape
    views = view_map.shape[0]
    groups = lax.axis_size("gz")
    length = groups * rows
    local_depth = depth // groups
    size = depth * ROWS
    blocks = rows // ROWS
    place = jnp.stack([lax.axis_index("view"), lax.axis_index("gz")]).astype(jnp.int32)

    columns_forward, columns_inverse = column_tables(width, depth, length)
    row_turn, row_back = row_tables(length, depth, width)

    strips = [initial[:, at : at + ROWS].astype(BF16) for at in (0, ROWS, rows - 2 * ROWS, rows - ROWS)]
    low = jnp.concatenate([observed[:, :, :ROWS], own_strip(strips[0], strips[1])[None]], 0)
    high = jnp.concatenate([observed[:, :, rows - ROWS :], own_strip(strips[3], strips[2])[None]], 0)
    first_rims = send_rims(low, high)

    chunk = slots // 2
    payload_block = (groups, 1, local_depth, rows, width)
    payload_shape = (groups, chunk, local_depth, rows, width)
    payload_bytes = 4 * depth * rows * width * chunk
    volume = depth * rows * width

    def first(start):
        return pl.pallas_call(
            first_kernel,
            grid_spec=pltpu.PrefetchScalarGridSpec(
                num_scalar_prefetch=1,
                grid=(chunk,),
                in_specs=[
                    pl.BlockSpec((1, depth, rows, width), lambda s, m: (lax.rem(s + start + ref_slot_of(m), slots), 0, 0, 0)),
                    whole(columns_forward.shape),
                ],
                out_specs=pl.BlockSpec(payload_block, lambda *a: (0, a[0], 0, 0, 0)),
                scratch_shapes=[pltpu.VMEM((depth, rows, width), F32)] * 2,
            ),
            out_shape=jax.ShapeDtypeStruct(payload_shape, jnp.int16),
            cost_estimate=cost(2 * chunk * volume * 8 * width, payload_bytes),
            name="first",
        )(view_map, observed, columns_forward)

    spectrum_shape = (local_depth, length, width)
    row_flops = 2 * local_depth * length * width * 3 * length

    def reference_spectrum(payload):
        return pl.pallas_call(
            spectrum_kernel,
            grid_spec=pltpu.PrefetchScalarGridSpec(
                num_scalar_prefetch=1,
                grid=(1,),
                in_specs=[
                    pl.BlockSpec(payload_block, lambda *_: (0, 0, 0, 0, 0)),
                    whole(row_turn.shape),
                ],
                out_specs=whole(spectrum_shape),
            ),
            out_shape=jax.ShapeDtypeStruct(spectrum_shape, F32),
            cost_estimate=cost(row_flops, 6 * volume),
            compiler_params=pltpu.CompilerParams(vmem_limit_bytes=16 * 1024 * 1024),
            name="spectrum",
        )(place, payload, row_turn)

    def crossed(payload, mine, other):
        return pl.pallas_call(
            cross_kernel,
            grid_spec=pltpu.PrefetchScalarGridSpec(
                num_scalar_prefetch=2,
                grid=(chunk,),
                in_specs=[
                    pl.BlockSpec(payload_block, lambda *a: (0, a[0], 0, 0, 0)),
                    whole(row_turn.shape),
                    whole(row_back.shape),
                    whole(spectrum_shape),
                    whole(spectrum_shape),
                ],
                out_specs=pl.BlockSpec(payload_block, lambda *a: (0, a[0], 0, 0, 0)),
            ),
            out_shape=jax.ShapeDtypeStruct(payload_shape, jnp.int16),
            cost_estimate=cost(2 * row_flops * chunk, payload_bytes + 10 * volume),
            compiler_params=pltpu.CompilerParams(vmem_limit_bytes=16 * 1024 * 1024),
            name="cross",
        )(view_map, place, payload, row_turn, row_back, mine, other)

    def last(payload, start, partial):
        specs = [
            pl.BlockSpec(payload_block, lambda *a: (0, a[0], 0, 0, 0)),
            whole(columns_inverse.shape),
        ]
        operands = [view_map, payload, columns_inverse]
        aliases = {}
        if partial is not None:
            specs.append(pl.BlockSpec(memory_space=pl.ANY))
            aliases = {len(operands): 0}
            operands.append(partial)
        return pl.pallas_call(
            last_kernel,
            grid_spec=pltpu.PrefetchScalarGridSpec(
                num_scalar_prefetch=1,
                grid=(chunk,),
                in_specs=specs,
                out_specs=pl.BlockSpec((1, depth, rows, width), lambda s, m: (lax.rem(s + start + ref_slot_of(m), slots), 0, 0, 0)),
                scratch_shapes=[pltpu.VMEM((depth, rows, width), F32)] * 2,
            ),
            out_shape=jax.ShapeDtypeStruct((slots, depth, rows, width), F32),
            input_output_aliases=aliases,
            cost_estimate=cost(2 * chunk * volume * 9 * width, payload_bytes * 1.5),
            compiler_params=pltpu.CompilerParams(vmem_limit_bytes=16 * 1024 * 1024),
            name="last",
        )(*operands)

    def filters():
        smem = pl.BlockSpec(memory_space=pltpu.SMEM)
        return pl.pallas_call(
            filter_kernel,
            grid=(slots,),
            in_specs=[smem] * 4,
            out_specs=[
                pl.BlockSpec((1, size, 3 * size), lambda s: (s, 0, 0)),
                pl.BlockSpec((1, size, 3 * size), lambda s: (s, 0, 0)),
                pl.BlockSpec((1, width, width), lambda s: (s, 0, 0)),
            ],
            out_shape=[
                jax.ShapeDtypeStruct((slots, size, 3 * size), BF16),
                jax.ShapeDtypeStruct((slots, size, 3 * size), BF16),
                jax.ShapeDtypeStruct((slots, width, width), BF16),
            ],
            cost_estimate=cost(slots * size * size * 60, slots * size * size * 14),
            name="filters",
        )(place, view_map, view_shifts, psf_taps)

    forward, backward, columns = filters()

    def join(estimate, strips, rims, logs=None):
        def slot_block(shape):
            return pl.BlockSpec((1,) + shape, lambda s: (s,) + (0,) * len(shape))

        updated = logs is not None
        field = jax.ShapeDtypeStruct((depth, rows, width), F32)
        extra_specs = []
        if updated:
            extra_specs = [whole((depth, rows, width))] * 2
        return pl.pallas_call(
            functools.partial(join_kernel, views, updated),
            grid=(slots,),
            in_specs=extra_specs
            + [
                pl.BlockSpec(memory_space=pltpu.SMEM),
                whole((depth, rows, width)),
                whole((2, depth, ROWS, width)),
                whole((2, depth, ROWS, width)),
                slot_block((depth, rows, width)),
                slot_block((depth, ROWS, width)),
                slot_block((depth, ROWS, width)),
                whole((slots, size, 3 * size)),
                slot_block((size, 3 * size)),
                slot_block((width, width)),
            ],
            out_specs=[whole((depth, rows, width))] * (1 + updated),
            out_shape=[field] * (1 + updated),
            scratch_shapes=[
                pltpu.VMEM((blocks + 4, size, width), BF16),
                pltpu.VMEM((slots, blocks + 2, size, width), BF16),
                pltpu.VMEM((blocks + 2, size, width), F32),
                pltpu.VMEM((blocks + 2, size, width), BF16),
                pltpu.VMEM((blocks, size, width), F32),
            ],
            cost_estimate=cost(2 * slots * size * width * ((blocks + 2) * (3 * size + 2 * width) + blocks * 3 * size), 12e6),
            name="join",
        )(*(logs or ()), place, estimate, *strips, observed, *rims, forward, backward, columns)

    payload_a = first(0)
    sent_a = turn(payload_a)
    payload_b = first(chunk)
    sent_b = turn(payload_b)
    mine = reference_spectrum(sent_a)
    other = swap_cores(mine)
    crossed_a = crossed(sent_a, mine, other)
    back_a = turn(crossed_a)
    first_strips = swap_strips([rim[slots] for rim in first_rims])

    (logs,) = join(initial, first_strips, first_rims)
    total = (logs, swap_cores(logs))

    def updated_rows(at):
        window = [lax.slice_in_dim(part, at, at + ROWS, axis=1) for part in (initial, *total)]
        return (window[0] * jnp.exp(window[1] + window[2])).astype(BF16)

    strips = [updated_rows(at) for at in (0, ROWS, rows - 2 * ROWS, rows - ROWS)]
    rims = send_rims(own_strip(strips[0], strips[1]), own_strip(strips[3], strips[2]))
    crossed_b = crossed(sent_b, mine, other)
    strips = swap_strips(rims)
    back_b = turn(crossed_b)
    logs, estimate = join(initial, strips, first_rims, logs=total)
    swapped = swap_cores(logs)
    estimate = estimate * jnp.exp(logs + swapped)

    surfaces = last(back_a, 0, None)
    surfaces = last(back_b, chunk, surfaces)
    return estimate, surfaces


def solution(mesh):
    placed = (P("view", "parts", "gz", None), P("parts", "gz", None), P(), P(), P())

    return jax.shard_map(
        on_device,
        mesh=mesh,
        in_specs=placed,
        out_specs=(P("parts", "gz", None), P("view", "parts", "gz", None)),
        check_vma=False,
    )
```

```python
import functools
import math

import jax
import jax.numpy as jnp
import ml_dtypes
import numpy as np
from jax import lax
from jax.experimental import pallas as pl
from jax.experimental.pallas import tpu as pltpu
from jax.sharding import PartitionSpec as P


TAPS = 15
HALF = TAPS // 2
ROWS = 8
MID = 1.099609375


F32 = jnp.float32
BF16 = jnp.bfloat16


def dot(a, b):
    return jnp.dot(a, b, preferred_element_type=F32)


def dot_t(a, b):
    return lax.dot_general(a, b, (((1,), (1,)), ((), ())), preferred_element_type=F32)


def split(value):
    high = value.astype(BF16)
    return high, (value - high.astype(F32)).astype(BF16)


def np_split(table):
    high = table.astype(ml_dtypes.bfloat16)
    low = (table - high.astype(np.float64)).astype(ml_dtypes.bfloat16)
    return high, low


def side_by_side(table):
    return jnp.asarray(np.concatenate(np_split(table), 1))


def depth_order(depth):
    order = [0, depth // 2]
    for m in range(1, depth // 2):
        order += [m, depth - m]
    return np.array(order)


def angle_table(rows, columns, length):
    return 2.0 * np.pi * ((rows[:, None] * columns[None, :]) % length) / length


def depth_transform(real, imag, orient):
    count = len(real)
    if count == 1:
        return real, imag
    if count == 2:
        return [real[0] + real[1], real[0] - real[1]], [imag[0] + imag[1], imag[0] - imag[1]]
    quarter = count // 4
    parts = [depth_transform(real[j::4], imag[j::4], orient) for j in range(4)]
    out_real, out_imag = [None] * count, [None] * count
    for k in range(quarter):
        turned_parts = []
        for j in range(4):
            part_real, part_imag = parts[j][0][k], parts[j][1][k]
            if j * k:
                angle = -orient * 2.0 * math.pi * j * k / count
                cos, sin = math.cos(angle), math.sin(angle)
                if 8 * j * k == count:
                    part_real, part_imag = (part_real + orient * part_imag) * cos, (part_imag - orient * part_real) * cos
                else:
                    part_real, part_imag = part_real * cos - part_imag * sin, part_real * sin + part_imag * cos
            turned_parts.append((part_real, part_imag))
        (ar, ai), (br, bi), (cr, ci), (dr, di) = turned_parts
        sum_ac, dif_ac = (ar + cr, ai + ci), (ar - cr, ai - ci)
        sum_bd, dif_bd = (br + dr, bi + di), (br - dr, bi - di)
        out_real[k], out_imag[k] = sum_ac[0] + sum_bd[0], sum_ac[1] + sum_bd[1]
        out_real[k + 2 * quarter], out_imag[k + 2 * quarter] = sum_ac[0] - sum_bd[0], sum_ac[1] - sum_bd[1]
        plus = (dif_ac[0] + dif_bd[1], dif_ac[1] - dif_bd[0])
        minus = (dif_ac[0] - dif_bd[1], dif_ac[1] + dif_bd[0])
        first_part, second_part = (plus, minus) if orient > 0 else (minus, plus)
        out_real[k + quarter], out_imag[k + quarter] = first_part
        out_real[k + 3 * quarter], out_imag[k + 3 * quarter] = second_part
    return out_real, out_imag


def forward_bound(depth, width):
    return 0.9005 * math.sqrt(depth * width)


def backward_bound(length):
    return 1.0005 * math.sqrt(length)


def code_scale(bound):
    return bound / 32767.0**2


def encode(value, bound):
    scaled = value * lax.rsqrt(jnp.abs(value) + 1e-30) * (32767.0 / math.sqrt(bound))
    return (scaled + jnp.where(value < 0.0, -0.5, 0.5)).astype(jnp.int32).astype(jnp.int16)


def decode(code):
    value = code.astype(jnp.int32).astype(F32)
    return value * jnp.abs(value)


def row_tables(length, depth, width):
    half = length // 2
    positions = np.arange(length)
    freqs = np.arange(half)
    angles = angle_table(positions, freqs, length)
    cos_part, sin_part = np.cos(angles), np.sin(angles)
    sin_part[:, 0] = 1.0 - 2.0 * (positions % 2)
    both = np.concatenate([cos_part, sin_part], 1) / math.sqrt(length)
    return side_by_side(both.T * code_scale(forward_bound(depth, width))), side_by_side(both)


def column_tables(width, depth, length):
    half = width // 2
    positions = np.arange(width)
    freqs = np.arange(half)
    angles = angle_table(positions, freqs, width)
    scale = 1.0 / math.sqrt(width * depth)
    cos_part = np.cos(angles)
    sin_part = -np.sin(angles)
    sin_part[:, 0] = 1.0 - 2.0 * (positions % 2)
    forward = np.concatenate([cos_part, sin_part], 1) * scale
    weights = np.where(freqs == 0, 1.0, 2.0)
    inverse = np.concatenate([cos_part * weights, sin_part * weights], 1).T * scale
    return side_by_side(forward), side_by_side(inverse * code_scale(backward_bound(length)))


def table_times(table, block):
    size = block.shape[0]
    high, low = split(block)
    return dot(table, jnp.concatenate([high, high], 0)) + dot(table[:, :size], low)


def replace_row(array, row):
    top = array[:ROWS]
    row_id = lax.broadcasted_iota(jnp.int32, top.shape, 0)
    return jnp.concatenate([jnp.where(row_id == 0, row[:1], top), array[ROWS:]], 0)


def rows_forward(table, plane):
    both = table_times(table, plane)
    count = both.shape[0] // 2
    half = both.shape[1] // 2
    cos_real, cos_imag = both[:count, :half], both[:count, half:]
    sin_real, sin_imag = both[count:, :half], both[count:, half:]
    above = (replace_row(cos_real + sin_imag, cos_real), replace_row(cos_imag - sin_real, cos_imag))
    below = (replace_row(cos_real - sin_imag, sin_real), replace_row(cos_imag + sin_real, sin_imag))
    return above, below


def rows_inverse(table, above, below):
    even_real = replace_row(above[0] + below[0], above[0])
    even_imag = replace_row(above[1] + below[1], above[1])
    odd_real = replace_row(below[1] - above[1], below[0])
    odd_imag = replace_row(above[0] - below[0], below[1])
    top = jnp.concatenate([even_real, even_imag], 1)
    bottom = jnp.concatenate([odd_real, odd_imag], 1)
    return table_times(table, jnp.concatenate([top, bottom], 0))


def ref_slot_of(map_ref):
    slot = jnp.int32(0)
    for at in range(1, map_ref.shape[0]):
        slot = jnp.where(map_ref[at] == 0, jnp.int32(at), slot)
    return slot


def first_kernel(map_ref, observed_ref, columns_ref, out_ref, spread_ref, turned_ref):
    depth, rows, width = observed_ref.shape[1:]
    half = width // 2
    groups, _, local_depth = out_ref.shape[:3]
    flat = observed_ref[0].reshape(depth * rows, width)
    table = columns_ref[...]
    spread = dot(flat, table[:, :width]) + dot(flat, table[:, width:])
    spread_ref[...] = spread.reshape(depth, rows, width)
    shift = MID * math.sqrt(width * depth)
    spots = depth_order(depth)
    lane = lax.broadcasted_iota(jnp.int32, (ROWS, half), 1)

    @pl.loop(0, rows // ROWS)
    def _(b):
        at = pl.ds(pl.multiple_of(b * ROWS, ROWS), ROWS)
        real = [spread_ref[z, at, :half] for z in range(depth)]
        imag = [spread_ref[z, at, half:] for z in range(depth)]
        real, imag = depth_transform(real, imag, 1)
        edge = lane == 0
        real[0] = jnp.where(edge, real[0] - shift, real[0])
        for k in range(1, depth // 2):
            n = depth - k
            zero_real, zero_imag = 0.5 * (real[k] + real[n]), 0.5 * (imag[k] - imag[n])
            top_real, top_imag = 0.5 * (imag[k] + imag[n]), 0.5 * (real[n] - real[k])
            real[k], imag[k] = jnp.where(edge, zero_real, real[k]), jnp.where(edge, zero_imag, imag[k])
            real[n], imag[n] = jnp.where(edge, top_real, real[n]), jnp.where(edge, top_imag, imag[n])
        for spot, k in enumerate(spots):
            turned_ref[spot, at, :half] = real[k]
            turned_ref[spot, at, half:] = imag[k]

    code = encode(turned_ref[...], forward_bound(depth, width))
    out_ref[:, 0] = code.reshape(groups, local_depth, rows, width)


def load_plane(in_ref, k):
    groups, _, _, rows, width = in_ref.shape
    return decode(in_ref[:, 0, k].reshape(groups * rows, width))


def edge_mask(shape, group_zero):
    row = lax.broadcasted_iota(jnp.int32, shape, 0)
    lane = lax.broadcasted_iota(jnp.int32, shape, 1)
    return (lane == 0) & (row > 0) & group_zero


def spectrum(table, plane, k, group_zero, depth):
    above, below = rows_forward(table, plane)
    if k == 0:
        shift = MID * math.sqrt(depth * plane.shape[0] * plane.shape[1])
        lane = lax.broadcasted_iota(jnp.int32, above[0].shape, 1)
        here = (lane[:1] == 0) & group_zero
        row = jnp.where(here, above[0][:1] + shift, above[0][:1])
        above = (replace_row(above[0], row), above[1])
    if k < 2:
        mask = edge_mask(above[0].shape, group_zero)
        zero = (0.5 * (above[0] + below[0]), 0.5 * (above[1] - below[1]))
        top = (0.5 * (above[1] + below[1]), 0.5 * (below[0] - above[0]))
        above = tuple(jnp.where(mask, new, old) for new, old in zip(zero, above))
        below = tuple(jnp.where(mask, new, old) for new, old in zip(top, below))
    return above, below


def spectrum_kernel(place_ref, in_ref, rows_ref, out_ref):
    group_zero = place_ref[1] == 0
    groups, _, local_depth, _, width = in_ref.shape
    depth = groups * local_depth
    half = width // 2
    table = rows_ref[...]
    for k in range(local_depth):
        above, below = spectrum(table, load_plane(in_ref, k), k, group_zero, depth)
        count = above[0].shape[0]
        out_ref[k, :count, :half] = above[0]
        out_ref[k, :count, half:] = above[1]
        out_ref[k, count:, :half] = below[0]
        out_ref[k, count:, half:] = below[1]


def root(value):
    return value * lax.rsqrt(jnp.maximum(value, 1e-30))


def cross_of(value, ref):
    real, imag = value
    ref_real, ref_imag = ref
    power = (real * real + imag * imag) * (ref_real * ref_real + ref_imag * ref_imag)
    scale = 1.0 / (root(power) + 1.0)
    return (real * ref_real + imag * ref_imag) * scale, (imag * ref_real - real * ref_imag) * scale


def cross_of_real(value, ref):
    product = value * ref
    return product / (jnp.abs(product) + 1.0)


def cross_plane(value, ref, k, group_zero):
    crossed = cross_of(value, ref)
    if k < 2:
        lane = lax.broadcasted_iota(jnp.int32, (1, value[0].shape[1]), 1)
        here = (lane == 0) & group_zero
        parts = []
        for at in range(2):
            row = jnp.where(here, cross_of_real(value[at][:1], ref[at][:1]), crossed[at][:1])
            parts.append(replace_row(crossed[at], row))
        crossed = tuple(parts)
    return crossed


def cross_kernel(map_ref, place_ref, in_ref, rows_ref, back_ref, mine_ref, other_ref, out_ref):
    groups, _, local_depth, rows, width = in_ref.shape
    slots = map_ref.shape[0] // 2
    holds_ref = ref_slot_of(map_ref) // slots == place_ref[0]
    group_zero = place_ref[1] == 0
    depth = groups * local_depth
    half = width // 2
    length = groups * rows
    count = length // 2
    bound = backward_bound(length)
    table = rows_ref[...]
    for k in range(local_depth):
        above, below = spectrum(table, load_plane(in_ref, k), k, group_zero, depth)
        ref = jnp.where(holds_ref, mine_ref[k], other_ref[k])
        above = cross_plane(above, (ref[:count, :half], ref[:count, half:]), k, group_zero)
        below = cross_plane(below, (ref[count:, :half], ref[count:, half:]), k, group_zero)
        if k < 2:
            mask = edge_mask(above[0].shape, group_zero)
            plus = (above[0] - below[1], above[1] + below[0])
            minus = (above[0] + below[1], below[0] - above[1])
            above = tuple(jnp.where(mask, new, old) for new, old in zip(plus, above))
            below = tuple(jnp.where(mask, new, old) for new, old in zip(minus, below))
        back = rows_inverse(back_ref[...], above, below)
        out_ref[:, 0, k] = encode(back, bound).reshape(groups, rows, width)


def last_kernel(map_ref, in_ref, columns_ref, *rest):
    out_ref, turned_ref, spread_ref = rest[-3:]
    groups, _, local_depth, rows, width = in_ref.shape
    depth = groups * local_depth
    half = width // 2
    table = columns_ref[...]
    spots = depth_order(depth)
    value = decode(in_ref[:, 0])
    turned_ref[...] = value.reshape(depth, rows, width)

    @pl.loop(0, rows // ROWS)
    def _(b):
        at = pl.ds(pl.multiple_of(b * ROWS, ROWS), ROWS)
        real, imag = [None] * depth, [None] * depth
        for spot, k in enumerate(spots):
            real[k] = turned_ref[spot, at, :half]
            imag[k] = turned_ref[spot, at, half:]
        edge = lax.broadcasted_iota(jnp.int32, (ROWS, half), 1) == 0
        for k in range(1, depth // 2):
            n = depth - k
            plus = (real[k] - imag[n], imag[k] + real[n])
            minus = (real[k] + imag[n], real[n] - imag[k])
            real[k], imag[k] = jnp.where(edge, plus[0], real[k]), jnp.where(edge, plus[1], imag[k])
            real[n], imag[n] = jnp.where(edge, minus[0], real[n]), jnp.where(edge, minus[1], imag[n])
        real, imag = depth_transform(real, imag, -1)
        for z in range(depth):
            spread_ref[z, at, :half] = real[z]
            spread_ref[z, at, half:] = imag[z]

    high, low = split(spread_ref[...].reshape(depth * rows, width))
    cells = dot(high, table[:, :width]) + dot(high, table[:, width:]) + dot(low, table[:, :width])
    out_ref[0] = cells.reshape(depth, rows, width)


def pick_tap(psf_ref, view, axis, index):
    value = jnp.zeros(index.shape, F32)
    for j in range(TAPS):
        value = jnp.where(index == j, psf_ref[view, axis, j], value)
    return value


def filter_kernel(place_ref, map_ref, shift_ref, psf_ref, forward_ref, backward_ref, columns_ref):
    size = forward_ref.shape[1]
    width = columns_ref.shape[1]
    depth = size // ROWS
    view = map_ref[place_ref[0] * pl.num_programs(0) + pl.program_id(0)]
    depth_shift = shift_ref[view, 0]
    column_shift = shift_ref[view, 1]
    at_out = lax.broadcasted_iota(jnp.int32, (depth, size), 0)
    at_in = lax.broadcasted_iota(jnp.int32, (depth, size), 1) // ROWS
    row = lax.broadcasted_iota(jnp.int32, (ROWS, size), 0)
    cell = lax.broadcasted_iota(jnp.int32, (ROWS, size), 1) % ROWS
    for out_ref, orient in ((forward_ref, 1), (backward_ref, -1)):
        depth_part = pick_tap(psf_ref, view, 0, orient * (at_in - at_out) + HALF - depth_shift)
        for c in range(3):
            reach = c * ROWS + cell - ROWS - row
            row_part = pick_tap(psf_ref, view, 1, orient * reach + HALF)
            block = depth_part[:, None, :] * row_part[None, :, :]
            out_ref[0, :, c * size : (c + 1) * size] = block.reshape(size, size).astype(BF16)
    source = lax.broadcasted_iota(jnp.int32, (width, width), 0)
    target = lax.broadcasted_iota(jnp.int32, (width, width), 1)
    picked = pick_tap(psf_ref, view, 2, source - target + HALF - column_shift)
    columns_ref[0] = picked.astype(BF16)


def join_kernel(
    views,
    updated,
    partial,
    *refs,
):
    if updated:
        mine_ref, other_ref, *refs = refs
    if partial:
        partial_ref, *refs = refs
    (
    place_ref,
    estimate_ref,
    strips_ref,
    swapped_ref,
    observed_ref,
    seen_below_ref,
    seen_above_ref,
    forward_ref,
    backward_ref,
    columns_ref,
    out_ref,
    *refs,
    ) = refs
    if updated:
        now_ref, *refs = refs
    else:
        now_ref = estimate_ref
    cells_ref, mixed_ref, blurred_ref, ratio_ref, product_ref = refs
    depth, rows, width = estimate_ref.shape
    size = depth * ROWS
    blocks = rows // ROWS
    slots = forward_ref.shape[0]
    step = pl.program_id(0)

    @pl.when(step == 0)
    def _():
        if updated:
            logs = mine_ref[...] + other_ref[...]
            now_ref[...] = estimate_ref[...] * jnp.exp(logs.reshape(depth, rows, width))
        first_core = place_ref[0] == 0
        for side, near, far in ((0, 1, 0), (1, blocks + 2, blocks + 3)):
            own = strips_ref[side].astype(F32).reshape(size, width)
            swapped = swapped_ref[side].astype(F32).reshape(size, width)
            cells_ref[near] = jnp.where(first_core, own, swapped).astype(BF16)
            cells_ref[far] = jnp.where(first_core, swapped, own).astype(BF16)
        for b in range(blocks):
            piece = now_ref[:, b * ROWS : (b + 1) * ROWS].reshape(size, width)
            cells_ref[b + 2] = piece.astype(BF16)
        product_ref[...] = jnp.ones_like(product_ref)

        @pl.loop(0, blocks + 2)
        def _(b):
            window = cells_ref[pl.ds(b, 3)].reshape(3 * size, width)
            mixed = dot(forward_ref[...].reshape(slots * size, 3 * size), window)
            mixed_ref[:, b] = mixed.astype(BF16).reshape(slots, size, width)

    columns = columns_ref[0]
    blurred = dot(mixed_ref[step].reshape((blocks + 2) * size, width), columns)
    blurred_ref[...] = blurred.reshape(blocks + 2, size, width)
    for b in range(blocks + 2):
        if b == 0:
            seen = seen_below_ref[0].astype(F32)
        elif b == blocks + 1:
            seen = seen_above_ref[0].astype(F32)
        else:
            seen = observed_ref[0, :, (b - 1) * ROWS : b * ROWS].astype(F32)
        seen = seen.reshape(size, width)
        ratio = jnp.where(seen > 0.0, seen / blurred_ref[b], 0.0)
        ratio_ref[b] = ratio.astype(BF16)
    ratio = dot_t(ratio_ref[...].reshape((blocks + 2) * size, width), columns)
    ratio_ref[...] = ratio.astype(BF16).reshape(blocks + 2, size, width)
    for b in range(blocks):
        window = ratio_ref[b : b + 3].reshape(3 * size, width)
        product_ref[b] = product_ref[b] * dot(backward_ref[0], window)

    @pl.when(step == slots - 1)
    def _():
        for b in range(blocks):
            logs = jnp.log(product_ref[b]) * (1.0 / views)
            logs = logs.reshape(depth, ROWS, width)
            if partial:
                logs = logs + partial_ref[:, b * ROWS : (b + 1) * ROWS]
            out_ref[:, b * ROWS : (b + 1) * ROWS] = logs


def whole(shape):
    return pl.BlockSpec(shape, lambda *_: (0,) * len(shape))


def cost(flops, moved):
    return pl.CostEstimate(flops=int(flops), bytes_accessed=int(moved), transcendentals=0)


def turn(payload):
    return lax.all_to_all(payload, "gz", split_axis=0, concat_axis=0, tiled=True)


def own_strip(near, far):
    return jnp.where(lax.axis_index("view") == 0, near, far)


def send_rims(low, high):
    count = lax.axis_size("gz")
    below = lax.ppermute(high, "gz", [(i, i + 1) for i in range(count - 1)])
    above = lax.ppermute(low, "gz", [(i + 1, i) for i in range(count - 1)])
    return below, above


def swap_cores(field):
    count = lax.axis_size("view")
    return lax.ppermute(field, "view", [(i, (i + 1) % count) for i in range(count)])


def swap_strips(strips):
    mine = jnp.stack(strips)
    return mine, swap_cores(mine)


def on_device(observed, initial, psf_taps, view_shifts, view_map):
    slots, depth, rows, width = observed.shape
    views = view_map.shape[0]
    groups = lax.axis_size("gz")
    length = groups * rows
    local_depth = depth // groups
    size = depth * ROWS
    blocks = rows // ROWS
    place = jnp.stack([lax.axis_index("view"), lax.axis_index("gz")]).astype(jnp.int32)

    columns_forward, columns_inverse = column_tables(width, depth, length)
    row_turn, row_back = row_tables(length, depth, width)

    strips = [initial[:, at : at + ROWS].astype(BF16) for at in (0, ROWS, rows - 2 * ROWS, rows - ROWS)]
    low = jnp.concatenate([observed[:, :, :ROWS], own_strip(strips[0], strips[1])[None]], 0)
    high = jnp.concatenate([observed[:, :, rows - ROWS :], own_strip(strips[3], strips[2])[None]], 0)
    first_rims = send_rims(low, high)

    chunk = slots // 2
    payload_block = (groups, 1, local_depth, rows, width)
    payload_shape = (groups, chunk, local_depth, rows, width)
    payload_bytes = 4 * depth * rows * width * chunk
    volume = depth * rows * width

    def first(start):
        return pl.pallas_call(
            first_kernel,
            grid_spec=pltpu.PrefetchScalarGridSpec(
                num_scalar_prefetch=1,
                grid=(chunk,),
                in_specs=[
                    pl.BlockSpec((1, depth, rows, width), lambda s, m: (lax.rem(s + start + ref_slot_of(m), slots), 0, 0, 0)),
                    whole(columns_forward.shape),
                ],
                out_specs=pl.BlockSpec(payload_block, lambda *a: (0, a[0], 0, 0, 0)),
                scratch_shapes=[pltpu.VMEM((depth, rows, width), F32)] * 2,
            ),
            out_shape=jax.ShapeDtypeStruct(payload_shape, jnp.int16),
            cost_estimate=cost(2 * chunk * volume * 8 * width, payload_bytes),
            name="first",
        )(view_map, observed, columns_forward)

    spectrum_shape = (local_depth, length, width)
    row_flops = 2 * local_depth * length * width * 3 * length

    def reference_spectrum(payload):
        return pl.pallas_call(
            spectrum_kernel,
            grid_spec=pltpu.PrefetchScalarGridSpec(
                num_scalar_prefetch=1,
                grid=(1,),
                in_specs=[
                    pl.BlockSpec(payload_block, lambda *_: (0, 0, 0, 0, 0)),
                    whole(row_turn.shape),
                ],
                out_specs=whole(spectrum_shape),
            ),
            out_shape=jax.ShapeDtypeStruct(spectrum_shape, F32),
            cost_estimate=cost(row_flops, 6 * volume),
            compiler_params=pltpu.CompilerParams(vmem_limit_bytes=16 * 1024 * 1024),
            name="spectrum",
        )(place, payload, row_turn)

    def crossed(payload, mine, other):
        return pl.pallas_call(
            cross_kernel,
            grid_spec=pltpu.PrefetchScalarGridSpec(
                num_scalar_prefetch=2,
                grid=(chunk,),
                in_specs=[
                    pl.BlockSpec(payload_block, lambda *a: (0, a[0], 0, 0, 0)),
                    whole(row_turn.shape),
                    whole(row_back.shape),
                    whole(spectrum_shape),
                    whole(spectrum_shape),
                ],
                out_specs=pl.BlockSpec(payload_block, lambda *a: (0, a[0], 0, 0, 0)),
            ),
            out_shape=jax.ShapeDtypeStruct(payload_shape, jnp.int16),
            cost_estimate=cost(2 * row_flops * chunk, payload_bytes + 10 * volume),
            compiler_params=pltpu.CompilerParams(vmem_limit_bytes=16 * 1024 * 1024),
            name="cross",
        )(view_map, place, payload, row_turn, row_back, mine, other)

    def last(payload, start, partial):
        specs = [
            pl.BlockSpec(payload_block, lambda *a: (0, a[0], 0, 0, 0)),
            whole(columns_inverse.shape),
        ]
        operands = [view_map, payload, columns_inverse]
        aliases = {}
        if partial is not None:
            specs.append(pl.BlockSpec(memory_space=pl.ANY))
            aliases = {len(operands): 0}
            operands.append(partial)
        return pl.pallas_call(
            last_kernel,
            grid_spec=pltpu.PrefetchScalarGridSpec(
                num_scalar_prefetch=1,
                grid=(chunk,),
                in_specs=specs,
                out_specs=pl.BlockSpec((1, depth, rows, width), lambda s, m: (lax.rem(s + start + ref_slot_of(m), slots), 0, 0, 0)),
                scratch_shapes=[pltpu.VMEM((depth, rows, width), F32)] * 2,
            ),
            out_shape=jax.ShapeDtypeStruct((slots, depth, rows, width), F32),
            input_output_aliases=aliases,
            cost_estimate=cost(2 * chunk * volume * 9 * width, payload_bytes * 1.5),
            compiler_params=pltpu.CompilerParams(vmem_limit_bytes=16 * 1024 * 1024),
            name="last",
        )(*operands)

    def filters():
        smem = pl.BlockSpec(memory_space=pltpu.SMEM)
        return pl.pallas_call(
            filter_kernel,
            grid=(slots,),
            in_specs=[smem] * 4,
            out_specs=[
                pl.BlockSpec((1, size, 3 * size), lambda s: (s, 0, 0)),
                pl.BlockSpec((1, size, 3 * size), lambda s: (s, 0, 0)),
                pl.BlockSpec((1, width, width), lambda s: (s, 0, 0)),
            ],
            out_shape=[
                jax.ShapeDtypeStruct((slots, size, 3 * size), BF16),
                jax.ShapeDtypeStruct((slots, size, 3 * size), BF16),
                jax.ShapeDtypeStruct((slots, width, width), BF16),
            ],
            cost_estimate=cost(slots * size * size * 60, slots * size * size * 14),
            name="filters",
        )(place, view_map, view_shifts, psf_taps)

    forward, backward, columns = filters()

    def join(estimate, strips, rims, logs=None, partial=None, start=0, count=slots):
        def slot_block(shape):
            return pl.BlockSpec((1,) + shape, lambda s: (s + start,) + (0,) * len(shape))

        updated = logs is not None
        field = jax.ShapeDtypeStruct((depth, rows, width), F32)
        extra = list(logs or ()) + ([] if partial is None else [partial])
        at = start // count
        return pl.pallas_call(
            functools.partial(join_kernel, views, updated, partial is not None),
            grid=(count,),
            in_specs=[whole((depth, rows, width))] * len(extra)
            + [
                pl.BlockSpec(memory_space=pltpu.SMEM),
                whole((depth, rows, width)),
                whole((2, depth, ROWS, width)),
                whole((2, depth, ROWS, width)),
                slot_block((depth, rows, width)),
                slot_block((depth, ROWS, width)),
                slot_block((depth, ROWS, width)),
                pl.BlockSpec((count, size, 3 * size), lambda s: (at, 0, 0)),
                slot_block((size, 3 * size)),
                slot_block((width, width)),
            ],
            out_specs=[whole((depth, rows, width))] * (1 + updated),
            out_shape=[field] * (1 + updated),
            scratch_shapes=[
                pltpu.VMEM((blocks + 4, size, width), BF16),
                pltpu.VMEM((count, blocks + 2, size, width), BF16),
                pltpu.VMEM((blocks + 2, size, width), F32),
                pltpu.VMEM((blocks + 2, size, width), BF16),
                pltpu.VMEM((blocks, size, width), F32),
            ],
            cost_estimate=cost(2 * count * size * width * ((blocks + 2) * (3 * size + 2 * width) + blocks * 3 * size), 12e6),
            name="join",
        )(*extra, place, estimate, *strips, observed, *rims, forward, backward, columns)

    sent_a = turn(first(0))
    payload_b = first(chunk)
    sent_b = turn(payload_b)
    mine = reference_spectrum(sent_a)
    other = swap_cores(mine)
    first_rims, crossed_a = lax.optimization_barrier((first_rims, crossed(sent_a, mine, other)))
    back_a = turn(crossed_a)
    first_strips = swap_strips([rim[slots] for rim in first_rims])

    (logs,) = join(initial, first_strips, first_rims, start=0, count=chunk)
    (logs,) = join(initial, first_strips, first_rims, partial=logs, start=chunk, count=chunk)
    total = (logs, swap_cores(logs))

    def updated_rows(at):
        window = [lax.slice_in_dim(part, at, at + ROWS, axis=1) for part in (initial, *total)]
        return (window[0] * jnp.exp(window[1] + window[2])).astype(BF16)

    strips = [updated_rows(at) for at in (0, ROWS, rows - 2 * ROWS, rows - ROWS)]
    rims = send_rims(own_strip(strips[0], strips[1]), own_strip(strips[3], strips[2]))
    crossed_b = crossed(sent_b, mine, other)
    strips = swap_strips(rims)
    back_b = turn(crossed_b)
    logs, estimate = join(initial, strips, first_rims, logs=total)
    swapped = swap_cores(logs)
    estimate = estimate * jnp.exp(logs + swapped)

    surfaces = last(back_a, 0, None)
    surfaces = last(back_b, chunk, surfaces)
    return estimate, surfaces


def solution(mesh):
    placed = (P("view", "parts", "gz", None), P("parts", "gz", None), P(), P(), P())

    return jax.shard_map(
        on_device,
        mesh=mesh,
        in_specs=placed,
        out_specs=(P("parts", "gz", None), P("view", "parts", "gz", None)),
        check_vma=False,
    )
```

```python
import functools
import math

import jax
import jax.numpy as jnp
import ml_dtypes
import numpy as np
from jax import lax
from jax.experimental import pallas as pl
from jax.experimental.pallas import tpu as pltpu
from jax.sharding import PartitionSpec as P


TAPS = 15
HALF = TAPS // 2
ROWS = 8
MID = 1.099609375


F32 = jnp.float32
BF16 = jnp.bfloat16


def dot(a, b):
    return jnp.dot(a, b, preferred_element_type=F32)


def dot_t(a, b):
    return lax.dot_general(a, b, (((1,), (1,)), ((), ())), preferred_element_type=F32)


def split(value):
    high = value.astype(BF16)
    return high, (value - high.astype(F32)).astype(BF16)


def np_split(table):
    high = table.astype(ml_dtypes.bfloat16)
    low = (table - high.astype(np.float64)).astype(ml_dtypes.bfloat16)
    return high, low


def side_by_side(table):
    return jnp.asarray(np.concatenate(np_split(table), 1))


def depth_order(depth):
    order = [0, depth // 2]
    for m in range(1, depth // 2):
        order += [m, depth - m]
    return np.array(order)


def angle_table(rows, columns, length):
    return 2.0 * np.pi * ((rows[:, None] * columns[None, :]) % length) / length


def depth_transform(real, imag, orient):
    count = len(real)
    if count == 1:
        return real, imag
    if count == 2:
        return [real[0] + real[1], real[0] - real[1]], [imag[0] + imag[1], imag[0] - imag[1]]
    quarter = count // 4
    parts = [depth_transform(real[j::4], imag[j::4], orient) for j in range(4)]
    out_real, out_imag = [None] * count, [None] * count
    for k in range(quarter):
        turned_parts = []
        for j in range(4):
            part_real, part_imag = parts[j][0][k], parts[j][1][k]
            if j * k:
                angle = -orient * 2.0 * math.pi * j * k / count
                cos, sin = math.cos(angle), math.sin(angle)
                if 8 * j * k == count:
                    part_real, part_imag = (part_real + orient * part_imag) * cos, (part_imag - orient * part_real) * cos
                else:
                    part_real, part_imag = part_real * cos - part_imag * sin, part_real * sin + part_imag * cos
            turned_parts.append((part_real, part_imag))
        (ar, ai), (br, bi), (cr, ci), (dr, di) = turned_parts
        sum_ac, dif_ac = (ar + cr, ai + ci), (ar - cr, ai - ci)
        sum_bd, dif_bd = (br + dr, bi + di), (br - dr, bi - di)
        out_real[k], out_imag[k] = sum_ac[0] + sum_bd[0], sum_ac[1] + sum_bd[1]
        out_real[k + 2 * quarter], out_imag[k + 2 * quarter] = sum_ac[0] - sum_bd[0], sum_ac[1] - sum_bd[1]
        plus = (dif_ac[0] + dif_bd[1], dif_ac[1] - dif_bd[0])
        minus = (dif_ac[0] - dif_bd[1], dif_ac[1] + dif_bd[0])
        first_part, second_part = (plus, minus) if orient > 0 else (minus, plus)
        out_real[k + quarter], out_imag[k + quarter] = first_part
        out_real[k + 3 * quarter], out_imag[k + 3 * quarter] = second_part
    return out_real, out_imag


def forward_bound(depth, width):
    return 0.9005 * math.sqrt(depth * width)


def backward_bound(length):
    return 1.0005 * math.sqrt(length)


def code_scale(bound):
    return bound / 32767.0**2


def encode(value, bound):
    scaled = value * lax.rsqrt(jnp.abs(value) + 1e-30) * (32767.0 / math.sqrt(bound))
    return (scaled + jnp.where(value < 0.0, -0.5, 0.5)).astype(jnp.int32).astype(jnp.int16)


def decode(code):
    value = code.astype(jnp.int32).astype(F32)
    return value * jnp.abs(value)


def row_tables(length, depth, width):
    half = length // 2
    positions = np.arange(length)
    freqs = np.arange(half)
    angles = angle_table(positions, freqs, length)
    cos_part, sin_part = np.cos(angles), np.sin(angles)
    sin_part[:, 0] = 1.0 - 2.0 * (positions % 2)
    both = np.concatenate([cos_part, sin_part], 1) / math.sqrt(length)
    return side_by_side(both.T * code_scale(forward_bound(depth, width))), side_by_side(both)


def column_tables(width, depth, length):
    half = width // 2
    positions = np.arange(width)
    freqs = np.arange(half)
    angles = angle_table(positions, freqs, width)
    scale = 1.0 / math.sqrt(width * depth)
    cos_part = np.cos(angles)
    sin_part = -np.sin(angles)
    sin_part[:, 0] = 1.0 - 2.0 * (positions % 2)
    forward = np.concatenate([cos_part, sin_part], 1) * scale
    weights = np.where(freqs == 0, 1.0, 2.0)
    inverse = np.concatenate([cos_part * weights, sin_part * weights], 1).T * scale
    return side_by_side(forward), side_by_side(inverse * code_scale(backward_bound(length)))


def table_times(table, block):
    size = block.shape[0]
    high, low = split(block)
    return dot(table, jnp.concatenate([high, high], 0)) + dot(table[:, :size], low)


def replace_row(array, row):
    top = array[:ROWS]
    row_id = lax.broadcasted_iota(jnp.int32, top.shape, 0)
    return jnp.concatenate([jnp.where(row_id == 0, row[:1], top), array[ROWS:]], 0)


def rows_forward(table, plane):
    both = table_times(table, plane)
    count = both.shape[0] // 2
    half = both.shape[1] // 2
    cos_real, cos_imag = both[:count, :half], both[:count, half:]
    sin_real, sin_imag = both[count:, :half], both[count:, half:]
    above = (replace_row(cos_real + sin_imag, cos_real), replace_row(cos_imag - sin_real, cos_imag))
    below = (replace_row(cos_real - sin_imag, sin_real), replace_row(cos_imag + sin_real, sin_imag))
    return above, below


def rows_inverse(table, above, below):
    even_real = replace_row(above[0] + below[0], above[0])
    even_imag = replace_row(above[1] + below[1], above[1])
    odd_real = replace_row(below[1] - above[1], below[0])
    odd_imag = replace_row(above[0] - below[0], below[1])
    top = jnp.concatenate([even_real, even_imag], 1)
    bottom = jnp.concatenate([odd_real, odd_imag], 1)
    return table_times(table, jnp.concatenate([top, bottom], 0))


def ref_slot_of(map_ref):
    slot = jnp.int32(0)
    for at in range(1, map_ref.shape[0]):
        slot = jnp.where(map_ref[at] == 0, jnp.int32(at), slot)
    return slot


def first_kernel(map_ref, observed_ref, columns_ref, out_ref, spread_ref, turned_ref):
    depth, rows, width = observed_ref.shape[1:]
    half = width // 2
    groups, _, local_depth = out_ref.shape[:3]
    flat = observed_ref[0].reshape(depth * rows, width)
    table = columns_ref[...]
    spread = dot(flat, table[:, :width]) + dot(flat, table[:, width:])
    spread_ref[...] = spread.reshape(depth, rows, width)
    shift = MID * math.sqrt(width * depth)
    spots = depth_order(depth)
    lane = lax.broadcasted_iota(jnp.int32, (ROWS, half), 1)

    @pl.loop(0, rows // ROWS)
    def _(b):
        at = pl.ds(pl.multiple_of(b * ROWS, ROWS), ROWS)
        real = [spread_ref[z, at, :half] for z in range(depth)]
        imag = [spread_ref[z, at, half:] for z in range(depth)]
        real, imag = depth_transform(real, imag, 1)
        edge = lane == 0
        real[0] = jnp.where(edge, real[0] - shift, real[0])
        for k in range(1, depth // 2):
            n = depth - k
            zero_real, zero_imag = 0.5 * (real[k] + real[n]), 0.5 * (imag[k] - imag[n])
            top_real, top_imag = 0.5 * (imag[k] + imag[n]), 0.5 * (real[n] - real[k])
            real[k], imag[k] = jnp.where(edge, zero_real, real[k]), jnp.where(edge, zero_imag, imag[k])
            real[n], imag[n] = jnp.where(edge, top_real, real[n]), jnp.where(edge, top_imag, imag[n])
        for spot, k in enumerate(spots):
            turned_ref[spot, at, :half] = real[k]
            turned_ref[spot, at, half:] = imag[k]

    code = encode(turned_ref[...], forward_bound(depth, width))
    out_ref[:, 0] = code.reshape(groups, local_depth, rows, width)


def load_plane(in_ref, k):
    groups, _, _, rows, width = in_ref.shape
    return decode(in_ref[:, 0, k].reshape(groups * rows, width))


def edge_mask(shape, group_zero):
    row = lax.broadcasted_iota(jnp.int32, shape, 0)
    lane = lax.broadcasted_iota(jnp.int32, shape, 1)
    return (lane == 0) & (row > 0) & group_zero


def spectrum(table, plane, k, group_zero, depth):
    above, below = rows_forward(table, plane)
    if k == 0:
        shift = MID * math.sqrt(depth * plane.shape[0] * plane.shape[1])
        lane = lax.broadcasted_iota(jnp.int32, above[0].shape, 1)
        here = (lane[:1] == 0) & group_zero
        row = jnp.where(here, above[0][:1] + shift, above[0][:1])
        above = (replace_row(above[0], row), above[1])
    if k < 2:
        mask = edge_mask(above[0].shape, group_zero)
        zero = (0.5 * (above[0] + below[0]), 0.5 * (above[1] - below[1]))
        top = (0.5 * (above[1] + below[1]), 0.5 * (below[0] - above[0]))
        above = tuple(jnp.where(mask, new, old) for new, old in zip(zero, above))
        below = tuple(jnp.where(mask, new, old) for new, old in zip(top, below))
    return above, below


def spectrum_kernel(place_ref, in_ref, rows_ref, out_ref):
    group_zero = place_ref[1] == 0
    groups, _, local_depth, _, width = in_ref.shape
    depth = groups * local_depth
    half = width // 2
    table = rows_ref[...]
    for k in range(local_depth):
        above, below = spectrum(table, load_plane(in_ref, k), k, group_zero, depth)
        count = above[0].shape[0]
        out_ref[k, :count, :half] = above[0]
        out_ref[k, :count, half:] = above[1]
        out_ref[k, count:, :half] = below[0]
        out_ref[k, count:, half:] = below[1]


def root(value):
    return value * lax.rsqrt(jnp.maximum(value, 1e-30))


def cross_of(value, ref):
    real, imag = value
    ref_real, ref_imag = ref
    power = (real * real + imag * imag) * (ref_real * ref_real + ref_imag * ref_imag)
    scale = 1.0 / (root(power) + 1.0)
    return (real * ref_real + imag * ref_imag) * scale, (imag * ref_real - real * ref_imag) * scale


def cross_of_real(value, ref):
    product = value * ref
    return product / (jnp.abs(product) + 1.0)


def cross_plane(value, ref, k, group_zero):
    crossed = cross_of(value, ref)
    if k < 2:
        lane = lax.broadcasted_iota(jnp.int32, (1, value[0].shape[1]), 1)
        here = (lane == 0) & group_zero
        parts = []
        for at in range(2):
            row = jnp.where(here, cross_of_real(value[at][:1], ref[at][:1]), crossed[at][:1])
            parts.append(replace_row(crossed[at], row))
        crossed = tuple(parts)
    return crossed


def cross_kernel(map_ref, place_ref, in_ref, rows_ref, back_ref, mine_ref, other_ref, out_ref):
    groups, _, local_depth, rows, width = in_ref.shape
    slots = map_ref.shape[0] // 2
    holds_ref = ref_slot_of(map_ref) // slots == place_ref[0]
    group_zero = place_ref[1] == 0
    depth = groups * local_depth
    half = width // 2
    length = groups * rows
    count = length // 2
    bound = backward_bound(length)
    table = rows_ref[...]
    for k in range(local_depth):
        above, below = spectrum(table, load_plane(in_ref, k), k, group_zero, depth)
        ref = jnp.where(holds_ref, mine_ref[k], other_ref[k])
        above = cross_plane(above, (ref[:count, :half], ref[:count, half:]), k, group_zero)
        below = cross_plane(below, (ref[count:, :half], ref[count:, half:]), k, group_zero)
        if k < 2:
            mask = edge_mask(above[0].shape, group_zero)
            plus = (above[0] - below[1], above[1] + below[0])
            minus = (above[0] + below[1], below[0] - above[1])
            above = tuple(jnp.where(mask, new, old) for new, old in zip(plus, above))
            below = tuple(jnp.where(mask, new, old) for new, old in zip(minus, below))
        back = rows_inverse(back_ref[...], above, below)
        out_ref[:, 0, k] = encode(back, bound).reshape(groups, rows, width)


def last_kernel(map_ref, in_ref, columns_ref, *rest):
    out_ref, turned_ref, spread_ref = rest[-3:]
    groups, _, local_depth, rows, width = in_ref.shape
    depth = groups * local_depth
    half = width // 2
    table = columns_ref[...]
    spots = depth_order(depth)
    value = decode(in_ref[:, 0])
    turned_ref[...] = value.reshape(depth, rows, width)

    @pl.loop(0, rows // ROWS)
    def _(b):
        at = pl.ds(pl.multiple_of(b * ROWS, ROWS), ROWS)
        real, imag = [None] * depth, [None] * depth
        for spot, k in enumerate(spots):
            real[k] = turned_ref[spot, at, :half]
            imag[k] = turned_ref[spot, at, half:]
        edge = lax.broadcasted_iota(jnp.int32, (ROWS, half), 1) == 0
        for k in range(1, depth // 2):
            n = depth - k
            plus = (real[k] - imag[n], imag[k] + real[n])
            minus = (real[k] + imag[n], real[n] - imag[k])
            real[k], imag[k] = jnp.where(edge, plus[0], real[k]), jnp.where(edge, plus[1], imag[k])
            real[n], imag[n] = jnp.where(edge, minus[0], real[n]), jnp.where(edge, minus[1], imag[n])
        real, imag = depth_transform(real, imag, -1)
        for z in range(depth):
            spread_ref[z, at, :half] = real[z]
            spread_ref[z, at, half:] = imag[z]

    high, low = split(spread_ref[...].reshape(depth * rows, width))
    cells = dot(high, table[:, :width]) + dot(high, table[:, width:]) + dot(low, table[:, :width])
    out_ref[0] = cells.reshape(depth, rows, width)


def pick_tap(psf_ref, view, axis, index):
    value = jnp.zeros(index.shape, F32)
    for j in range(TAPS):
        value = jnp.where(index == j, psf_ref[view, axis, j], value)
    return value


def filter_kernel(place_ref, map_ref, shift_ref, psf_ref, forward_ref, backward_ref, columns_ref):
    size = forward_ref.shape[1]
    width = columns_ref.shape[1]
    depth = size // ROWS
    view = map_ref[place_ref[0] * pl.num_programs(0) + pl.program_id(0)]
    depth_shift = shift_ref[view, 0]
    column_shift = shift_ref[view, 1]
    at_out = lax.broadcasted_iota(jnp.int32, (depth, size), 0)
    at_in = lax.broadcasted_iota(jnp.int32, (depth, size), 1) // ROWS
    row = lax.broadcasted_iota(jnp.int32, (ROWS, size), 0)
    cell = lax.broadcasted_iota(jnp.int32, (ROWS, size), 1) % ROWS
    for out_ref, orient in ((forward_ref, 1), (backward_ref, -1)):
        depth_part = pick_tap(psf_ref, view, 0, orient * (at_in - at_out) + HALF - depth_shift)
        for c in range(3):
            reach = c * ROWS + cell - ROWS - row
            row_part = pick_tap(psf_ref, view, 1, orient * reach + HALF)
            block = depth_part[:, None, :] * row_part[None, :, :]
            out_ref[0, :, c * size : (c + 1) * size] = block.reshape(size, size).astype(BF16)
    source = lax.broadcasted_iota(jnp.int32, (width, width), 0)
    target = lax.broadcasted_iota(jnp.int32, (width, width), 1)
    picked = pick_tap(psf_ref, view, 2, source - target + HALF - column_shift)
    columns_ref[0] = picked.astype(BF16)


def join_kernel(
    views,
    updated,
    partial,
    *refs,
):
    if updated:
        mine_ref, other_ref, *refs = refs
    if partial:
        partial_ref, *refs = refs
    (
    place_ref,
    estimate_ref,
    strips_ref,
    swapped_ref,
    observed_ref,
    seen_first_ref,
    seen_second_ref,
    forward_ref,
    backward_ref,
    columns_ref,
    out_ref,
    *refs,
    ) = refs
    if updated:
        now_ref, *refs = refs
    else:
        now_ref = estimate_ref
    cells_ref, mixed_ref, blurred_ref, ratio_ref, product_ref = refs
    depth, rows, width = estimate_ref.shape
    size = depth * ROWS
    blocks = rows // ROWS
    slots = forward_ref.shape[0]
    step = pl.program_id(0)
    odd = place_ref[1] % 2 == 1

    @pl.when(step == 0)
    def _():
        if updated:
            logs = mine_ref[...] + other_ref[...]
            now_ref[...] = estimate_ref[...] * jnp.exp(logs.reshape(depth, rows, width))
        first_core = place_ref[0] == 0
        for below, near, far in ((True, 1, 0), (False, blocks + 2, blocks + 3)):
            side = jnp.where(odd == below, 0, 1)
            own = strips_ref[side].astype(F32).reshape(size, width)
            swapped = swapped_ref[side].astype(F32).reshape(size, width)
            cells_ref[near] = jnp.where(first_core, own, swapped).astype(BF16)
            cells_ref[far] = jnp.where(first_core, swapped, own).astype(BF16)
        for b in range(blocks):
            piece = now_ref[:, b * ROWS : (b + 1) * ROWS].reshape(size, width)
            cells_ref[b + 2] = piece.astype(BF16)
        product_ref[...] = jnp.ones_like(product_ref)

        @pl.loop(0, blocks + 2)
        def _(b):
            window = cells_ref[pl.ds(b, 3)].reshape(3 * size, width)
            mixed = dot(forward_ref[...].reshape(slots * size, 3 * size), window)
            mixed_ref[:, b] = mixed.astype(BF16).reshape(slots, size, width)

    columns = columns_ref[0]
    blurred = dot(mixed_ref[step].reshape((blocks + 2) * size, width), columns)
    blurred_ref[...] = blurred.reshape(blocks + 2, size, width)
    for b in range(blocks + 2):
        if b == 0:
            seen = jnp.where(odd, seen_first_ref[0].astype(F32), seen_second_ref[0].astype(F32))
        elif b == blocks + 1:
            seen = jnp.where(odd, seen_second_ref[0].astype(F32), seen_first_ref[0].astype(F32))
        else:
            seen = observed_ref[0, :, (b - 1) * ROWS : b * ROWS].astype(F32)
        seen = seen.reshape(size, width)
        ratio = jnp.where(seen > 0.0, seen / blurred_ref[b], 0.0)
        ratio_ref[b] = ratio.astype(BF16)
    ratio = dot_t(ratio_ref[...].reshape((blocks + 2) * size, width), columns)
    ratio_ref[...] = ratio.astype(BF16).reshape(blocks + 2, size, width)
    for b in range(blocks):
        window = ratio_ref[b : b + 3].reshape(3 * size, width)
        product_ref[b] = product_ref[b] * dot(backward_ref[0], window)

    @pl.when(step == slots - 1)
    def _():
        for b in range(blocks):
            logs = jnp.log(product_ref[b]) * (1.0 / views)
            logs = logs.reshape(depth, ROWS, width)
            if partial:
                logs = logs + partial_ref[:, b * ROWS : (b + 1) * ROWS]
            out_ref[:, b * ROWS : (b + 1) * ROWS] = logs


def whole(shape):
    return pl.BlockSpec(shape, lambda *_: (0,) * len(shape))


def cost(flops, moved):
    return pl.CostEstimate(flops=int(flops), bytes_accessed=int(moved), transcendentals=0)


def turn(payload):
    return lax.all_to_all(payload, "gz", split_axis=0, concat_axis=0, tiled=True)


def own_strip(near, far):
    return jnp.where(lax.axis_index("view") == 0, near, far)


def by_parity(for_odd, for_even):
    return jnp.where(lax.axis_index("gz") % 2 == 1, for_odd, for_even)


def send_rims(near_pair, far_pair):
    count = lax.axis_size("gz")
    first = lax.ppermute(near_pair, "gz", [(i, i ^ 1) for i in range(count)])
    links = [(i, i + 1) for i in range(1, count - 1, 2)]
    second = lax.ppermute(far_pair, "gz", links + [(j, i) for i, j in links])
    return first, second


def swap_cores(field):
    count = lax.axis_size("view")
    return lax.ppermute(field, "view", [(i, (i + 1) % count) for i in range(count)])


def swap_strips(strips):
    mine = jnp.stack(strips)
    return mine, swap_cores(mine)


def on_device(observed, initial, psf_taps, view_shifts, view_map):
    slots, depth, rows, width = observed.shape
    views = view_map.shape[0]
    groups = lax.axis_size("gz")
    length = groups * rows
    local_depth = depth // groups
    size = depth * ROWS
    blocks = rows // ROWS
    place = jnp.stack([lax.axis_index("view"), lax.axis_index("gz")]).astype(jnp.int32)

    columns_forward, columns_inverse = column_tables(width, depth, length)
    row_turn, row_back = row_tables(length, depth, width)

    strips = [initial[:, at : at + ROWS].astype(BF16) for at in (0, ROWS, rows - 2 * ROWS, rows - ROWS)]
    low, high = own_strip(strips[0], strips[1]), own_strip(strips[3], strips[2])
    seen_low, seen_high = observed[:, :, :ROWS], observed[:, :, rows - ROWS :]
    near_pair = jnp.concatenate([by_parity(seen_low, seen_high), by_parity(low, high)[None]], 0)
    far_pair = jnp.concatenate([by_parity(seen_high, seen_low), by_parity(high, low)[None]], 0)
    first_rims = send_rims(near_pair, far_pair)

    chunk = slots // 2
    payload_block = (groups, 1, local_depth, rows, width)
    payload_shape = (groups, chunk, local_depth, rows, width)
    payload_bytes = 4 * depth * rows * width * chunk
    volume = depth * rows * width

    def first(start):
        return pl.pallas_call(
            first_kernel,
            grid_spec=pltpu.PrefetchScalarGridSpec(
                num_scalar_prefetch=1,
                grid=(chunk,),
                in_specs=[
                    pl.BlockSpec((1, depth, rows, width), lambda s, m: (lax.rem(s + start + ref_slot_of(m), slots), 0, 0, 0)),
                    whole(columns_forward.shape),
                ],
                out_specs=pl.BlockSpec(payload_block, lambda *a: (0, a[0], 0, 0, 0)),
                scratch_shapes=[pltpu.VMEM((depth, rows, width), F32)] * 2,
            ),
            out_shape=jax.ShapeDtypeStruct(payload_shape, jnp.int16),
            cost_estimate=cost(2 * chunk * volume * 8 * width, payload_bytes),
            name="first",
        )(view_map, observed, columns_forward)

    spectrum_shape = (local_depth, length, width)
    row_flops = 2 * local_depth * length * width * 3 * length

    def reference_spectrum(payload):
        return pl.pallas_call(
            spectrum_kernel,
            grid_spec=pltpu.PrefetchScalarGridSpec(
                num_scalar_prefetch=1,
                grid=(1,),
                in_specs=[
                    pl.BlockSpec(payload_block, lambda *_: (0, 0, 0, 0, 0)),
                    whole(row_turn.shape),
                ],
                out_specs=whole(spectrum_shape),
            ),
            out_shape=jax.ShapeDtypeStruct(spectrum_shape, F32),
            cost_estimate=cost(row_flops, 6 * volume),
            compiler_params=pltpu.CompilerParams(vmem_limit_bytes=16 * 1024 * 1024),
            name="spectrum",
        )(place, payload, row_turn)

    def crossed(payload, mine, other):
        return pl.pallas_call(
            cross_kernel,
            grid_spec=pltpu.PrefetchScalarGridSpec(
                num_scalar_prefetch=2,
                grid=(chunk,),
                in_specs=[
                    pl.BlockSpec(payload_block, lambda *a: (0, a[0], 0, 0, 0)),
                    whole(row_turn.shape),
                    whole(row_back.shape),
                    whole(spectrum_shape),
                    whole(spectrum_shape),
                ],
                out_specs=pl.BlockSpec(payload_block, lambda *a: (0, a[0], 0, 0, 0)),
            ),
            out_shape=jax.ShapeDtypeStruct(payload_shape, jnp.int16),
            cost_estimate=cost(2 * row_flops * chunk, payload_bytes + 10 * volume),
            compiler_params=pltpu.CompilerParams(vmem_limit_bytes=16 * 1024 * 1024),
            name="cross",
        )(view_map, place, payload, row_turn, row_back, mine, other)

    def last(payload, start, partial):
        specs = [
            pl.BlockSpec(payload_block, lambda *a: (0, a[0], 0, 0, 0)),
            whole(columns_inverse.shape),
        ]
        operands = [view_map, payload, columns_inverse]
        aliases = {}
        if partial is not None:
            specs.append(pl.BlockSpec(memory_space=pl.ANY))
            aliases = {len(operands): 0}
            operands.append(partial)
        return pl.pallas_call(
            last_kernel,
            grid_spec=pltpu.PrefetchScalarGridSpec(
                num_scalar_prefetch=1,
                grid=(chunk,),
                in_specs=specs,
                out_specs=pl.BlockSpec((1, depth, rows, width), lambda s, m: (lax.rem(s + start + ref_slot_of(m), slots), 0, 0, 0)),
                scratch_shapes=[pltpu.VMEM((depth, rows, width), F32)] * 2,
            ),
            out_shape=jax.ShapeDtypeStruct((slots, depth, rows, width), F32),
            input_output_aliases=aliases,
            cost_estimate=cost(2 * chunk * volume * 9 * width, payload_bytes * 1.5),
            compiler_params=pltpu.CompilerParams(vmem_limit_bytes=16 * 1024 * 1024),
            name="last",
        )(*operands)

    def filters():
        smem = pl.BlockSpec(memory_space=pltpu.SMEM)
        return pl.pallas_call(
            filter_kernel,
            grid=(slots,),
            in_specs=[smem] * 4,
            out_specs=[
                pl.BlockSpec((1, size, 3 * size), lambda s: (s, 0, 0)),
                pl.BlockSpec((1, size, 3 * size), lambda s: (s, 0, 0)),
                pl.BlockSpec((1, width, width), lambda s: (s, 0, 0)),
            ],
            out_shape=[
                jax.ShapeDtypeStruct((slots, size, 3 * size), BF16),
                jax.ShapeDtypeStruct((slots, size, 3 * size), BF16),
                jax.ShapeDtypeStruct((slots, width, width), BF16),
            ],
            cost_estimate=cost(slots * size * size * 60, slots * size * size * 14),
            name="filters",
        )(place, view_map, view_shifts, psf_taps)

    forward, backward, columns = filters()

    def join(estimate, strips, rims, logs=None, partial=None, start=0, count=slots):
        def slot_block(shape):
            return pl.BlockSpec((1,) + shape, lambda s: (s + start,) + (0,) * len(shape))

        updated = logs is not None
        field = jax.ShapeDtypeStruct((depth, rows, width), F32)
        extra = list(logs or ()) + ([] if partial is None else [partial])
        at = start // count
        return pl.pallas_call(
            functools.partial(join_kernel, views, updated, partial is not None),
            grid=(count,),
            in_specs=[whole((depth, rows, width))] * len(extra)
            + [
                pl.BlockSpec(memory_space=pltpu.SMEM),
                whole((depth, rows, width)),
                whole((2, depth, ROWS, width)),
                whole((2, depth, ROWS, width)),
                slot_block((depth, rows, width)),
                slot_block((depth, ROWS, width)),
                slot_block((depth, ROWS, width)),
                pl.BlockSpec((count, size, 3 * size), lambda s: (at, 0, 0)),
                slot_block((size, 3 * size)),
                slot_block((width, width)),
            ],
            out_specs=[whole((depth, rows, width))] * (1 + updated),
            out_shape=[field] * (1 + updated),
            scratch_shapes=[
                pltpu.VMEM((blocks + 4, size, width), BF16),
                pltpu.VMEM((count, blocks + 2, size, width), BF16),
                pltpu.VMEM((blocks + 2, size, width), F32),
                pltpu.VMEM((blocks + 2, size, width), BF16),
                pltpu.VMEM((blocks, size, width), F32),
            ],
            cost_estimate=cost(2 * count * size * width * ((blocks + 2) * (3 * size + 2 * width) + blocks * 3 * size), 12e6),
            name="join",
        )(*extra, place, estimate, *strips, observed, *rims, forward, backward, columns)

    sent_a = turn(first(0))
    payload_b = first(chunk)
    sent_b = turn(payload_b)
    mine = reference_spectrum(sent_a)
    other = swap_cores(mine)
    first_rims, crossed_a = lax.optimization_barrier((first_rims, crossed(sent_a, mine, other)))
    back_a = turn(crossed_a)
    first_strips = swap_strips([rim[slots] for rim in first_rims])

    (logs,) = join(initial, first_strips, first_rims, start=0, count=chunk)
    (logs,) = join(initial, first_strips, first_rims, partial=logs, start=chunk, count=chunk)
    total = (logs, swap_cores(logs))

    def updated_rows(at):
        window = [lax.slice_in_dim(part, at, at + ROWS, axis=1) for part in (initial, *total)]
        return (window[0] * jnp.exp(window[1] + window[2])).astype(BF16)

    strips = [updated_rows(at) for at in (0, ROWS, rows - 2 * ROWS, rows - ROWS)]
    low, high = own_strip(strips[0], strips[1]), own_strip(strips[3], strips[2])
    rims = send_rims(by_parity(low, high), by_parity(high, low))
    crossed_b = crossed(sent_b, mine, other)
    strips = swap_strips(rims)
    back_b = turn(crossed_b)
    logs, estimate = join(initial, strips, first_rims, logs=total)
    swapped = swap_cores(logs)
    estimate = estimate * jnp.exp(logs + swapped)

    surfaces = last(back_a, 0, None)
    surfaces = last(back_b, chunk, surfaces)
    return estimate, surfaces


def solution(mesh):
    placed = (P("view", "parts", "gz", None), P("parts", "gz", None), P(), P(), P())

    return jax.shard_map(
        on_device,
        mesh=mesh,
        in_specs=placed,
        out_specs=(P("parts", "gz", None), P("view", "parts", "gz", None)),
        check_vma=False,
    )
```
